32 devices in a mesh: wide: 16 (over z, x, core), narrow: 2 (over y).
Axes of the slice: x: 2, y: 2, z: 4, core: 2. Of those that a mesh axis runs over, the one named last changes fastest.
Arguments:
- tokens: bfloat16 [32, 256, 1152], P('wide', 'narrow'), may hold values from -6 to 6
- cond: bfloat16 [32, 1152], P('wide'), may hold values from -6 to 6
- timesteps: int32 [32], P('wide'), may hold values from 0 to 999
- counts: int32 [16], P('wide'), may hold values from 1 to 2, as said below
- w_ada: bfloat16 [1152, 6912], P('wide'), may hold values from -0.1875 to 0.1875
- b_ada: bfloat16 [6912], P('wide'), may hold values from -2 to 2
- w_qkv: bfloat16 [1152, 3456], P('wide'), may hold values from -0.1875 to 0.1875
- b_qv: bfloat16 [2304], P('wide'), may hold values from -2 to 2
- w_proj: bfloat16 [1152, 1152], P('wide'), may hold values from -1.5 to 1.5
- b_proj: bfloat16 [1152], P('wide'), may hold values from -2 to 2
- w_fc1: bfloat16 [1152, 4608], P('wide'), may hold values from -0.1875 to 0.1875
- b_fc1: bfloat16 [4608], P('wide'), may hold values from -2 to 2
- w_fc2: bfloat16 [4608, 1152], P('wide'), may hold values from -0.09375 to 0.09375
- b_fc2: bfloat16 [1152], P('wide'), may hold values from -2 to 2
- cotangent: bfloat16 [32, 256, 1152], P('wide', 'narrow'), may hold values from -6 to 6
Outputs:
- out: bfloat16 [32, 256, 1152], P('wide', 'narrow')
- grad_tokens: float32 [32, 256, 1152], P('wide', 'narrow')
- grad_cond: float32 [32, 1152], P('wide')
- grad_w_ada: float32 [1152, 6912], P('wide')
- grad_b_ada: float32 [6912], P('wide')
- grad_w_qkv: float32 [1152, 3456], P('wide')
- grad_b_qv: float32 [2304], P('wide')
- grad_w_proj: float32 [1152, 1152], P('wide')
- grad_b_proj: float32 [1152], P('wide')
- grad_w_fc1: float32 [1152, 4608], P('wide')
- grad_b_fc1: float32 [4608], P('wide')
- grad_w_fc2: float32 [4608, 1152], P('wide')
- grad_b_fc2: float32 [1152], P('wide')
The draws below stay inside these ranges and needn't reach their ends.
Inputs may be any that keep to these rules, and one draw needn't show every extreme that they name: Image slot s of index w of wide is occupied when s < counts[w]; empty slots have zero output and add nothing to any gradient. In every draw some index of wide has all 2 slots occupied and some index has only one.
All inputs are finite; a program needn't handle non-finite values.
Results may differ from the reference program's by a relative error of at most 0.018.
The reference program's roundings to bfloat16 on the way count: a program that leaves them out, or rounds other values in their place, can miss the bound.
Values may be sent and summed in bfloat16 or wider, within the bound.
A program may use at most 256 MiB of HBM per device.

```python
import math
import jax
import jax.numpy as jnp
import numpy as np
from jax import lax

D = 1152
HEADS = 16
HEAD_DIM = 72
MLP = 4608
SEQ = 256
CAP = 2
ITEMS = 32
N_WIDE = 16


def draw_counts(key, part):
    key_fill = jax.random.fold_in(key, 11)
    key_full = jax.random.fold_in(key, 23)
    key_single = jax.random.fold_in(key, 37)
    filled = jax.random.randint(key_fill, (N_WIDE,), 1, CAP + 1).astype(jnp.int32)
    where_full = jax.random.randint(key_full, (), 0, N_WIDE).astype(jnp.int32)
    offset = jax.random.randint(key_single, (), 1, N_WIDE).astype(jnp.int32)
    where_single = (where_full + offset) % N_WIDE
    filled = filled.at[where_full].set(CAP)
    return filled.at[where_single].set(1)


def place_ends(drawn, stream_key, smallest, high):
    longest = drawn.shape.index(max(drawn.shape))
    spots = []
    for shift in (0, 1):
        where = [jax.random.randint(jax.random.fold_in(stream_key, axis), (), 0, length) for axis, length in enumerate(drawn.shape)]
        where[longest] = (where[longest] + shift) % drawn.shape[longest]
        spots.append(tuple(where))
    return drawn.at[spots[0]].set(smallest).at[spots[1]].set(high)


def with_spikes(drawn, key, source, target, shards_of, factor):
    def block_of(axis_at):
        return (jnp.arange(drawn.shape[axis_at]) // (drawn.shape[axis_at] // shards_of)).reshape((-1,) + (1,) * (drawn.ndim - 1 - axis_at))

    first = jax.random.permutation(key, shards_of)[block_of(target)]
    second = (block_of(target) + shards_of // 2) % shards_of
    return jnp.where((block_of(source) == first) | (block_of(source) == second), factor * drawn, drawn)


def levels(own_key, dims, cuts, low, largest):
    gain = 1.0
    for position, shards_of in cuts:
        steps = jax.random.uniform(jax.random.fold_in(jax.random.fold_in(own_key, 6), position), (shards_of,), jnp.float32, low / len(cuts), largest / len(cuts))
        gain = gain * jnp.repeat(jnp.exp(steps), dims[position] // shards_of).reshape((-1,) + (1,) * (len(dims) - 1 - position))
    return gain


def rank_bounds(number_of, lean):
    loads = [(1 << 20) // math.isqrt(rank ** lean) + 1 for rank in range(1, number_of + 1)]
    spread = 1 + sum(loads) // (1 << 30)
    return np.cumsum(np.array([max(1, weight // spread) for weight in loads]))


def skewed_ids(rng, shape, number_of, skew):
    grid = rank_bounds(number_of, skew)
    lot = jax.random.randint(jax.random.fold_in(rng, 1), shape, 0, int(grid[number_of - 1]))
    grade = jnp.searchsorted(jnp.asarray(grid, jnp.int32), lot, side="right")
    return jax.random.permutation(jax.random.fold_in(rng, 2), number_of)[grade].astype(jnp.int32)


def gaussian(own_key, extent, scale, reach, shards=(), held_as=jnp.bfloat16):
    values = jax.random.normal(own_key, extent, jnp.float32) * scale
    if len(shards) > 0:
        values = levels(own_key, extent, shards, -0.22, 0.18) * values
    return jnp.clip(values, min=-reach, max=reach).astype(held_as)


def heavy_noise(key, dims, spread, limit, split, heavy, held_as=jnp.bfloat16):
    values = spread * jax.random.normal(key, dims, jnp.float32)
    if split:
        values = values * levels(key, dims, split, -0.22, 0.18)
    return jnp.clip(with_spikes(values, jax.random.fold_in(key, 3), *heavy), -limit, limit).astype(held_as)


def setup_inputs(seed: int = 0) -> dict:
    streams_of = jax.random.split(jax.random.key(seed), 16)
    return {
        "tokens": heavy_noise(streams_of[0], (ITEMS, SEQ, D), 1.0, 6.0, ((0, 16), (1, 2)), (0, 2, 16, 2.0)),
        "cond": gaussian(streams_of[1], (ITEMS, D), 1.0, 6.0, ((0, 16),)),
        "timesteps": place_ends(skewed_ids(streams_of[2], (ITEMS,), 1000, 2), jax.random.fold_in(streams_of[2], 3), 0, 999).astype(jnp.int32),
        "counts": draw_counts(jax.random.fold_in(streams_of[15], 71), 0),
        "w_ada": gaussian(streams_of[4], (D, 6 * D), D ** -0.5, 0.1875, ((0, 16),)),
        "b_ada": gaussian(streams_of[5], (6 * D,), 0.3, 2.0, ((0, 16),)),
        "w_qkv": gaussian(streams_of[6], (D, 3 * D), D ** -0.5, 0.1875, ((0, 16),)),
        "b_qv": gaussian(streams_of[7], (2 * D,), 0.3, 2.0, ((0, 16),)),
        "w_proj": gaussian(streams_of[8], (D, D), (D // 64) ** -0.5, 1.5, ((0, 16),)),
        "b_proj": gaussian(streams_of[9], (D,), 0.3, 2.0, ((0, 16),)),
        "w_fc1": gaussian(streams_of[10], (D, MLP), D ** -0.5, 0.1875, ((0, 16),)),
        "b_fc1": gaussian(streams_of[11], (MLP,), 0.3, 2.0, ((0, 16),)),
        "w_fc2": gaussian(streams_of[12], (MLP, D), MLP ** -0.5, 0.09375, ((0, 16),)),
        "b_fc2": gaussian(streams_of[13], (D,), 0.3, 2.0, ((0, 16),)),
        "cotangent": heavy_noise(streams_of[14], (ITEMS, SEQ, D), 1.0, 6.0, ((0, 16), (1, 2)), (0, 2, 16, 2.0)),
    }


@jax.custom_vjp
def low(v):
    return lax.optimization_barrier(v.astype(jnp.bfloat16)).astype(jnp.float32)

@jax.custom_vjp
def low_back(v):
    return v

def low_keep(v):
    return (low(v), None)

def low_pass(kept, grad):
    return (grad,)

def back_keep(v):
    return (v, None)

def back_low(kept, grad):
    return (low(grad),)
low.defvjp(low_keep, low_pass)
low_back.defvjp(back_keep, back_low)
highest = lax.Precision.HIGHEST
eps_norm = 1e-06

def layer_norm(value):
    center = value - lax.optimization_barrier(jnp.mean(value, axis=-1, keepdims=True))
    return center * lax.rsqrt(lax.optimization_barrier(jnp.mean(center * center, axis=-1, keepdims=True)) + eps_norm)

def gelu_tanh(value):
    return 0.5 * value * (1.0 + jnp.tanh(0.7978845608028654 * (value + 0.044715 * value * value * value)))

def time_features(steps):
    half_width = D // 2
    freqs = jnp.exp(-math.log(10000.0) * jnp.arange(half_width).astype(jnp.float32) / half_width)
    angles = steps.astype(jnp.float32)[:, None] * freqs[None, :]
    return jnp.concatenate([jnp.cos(angles), jnp.sin(angles)], axis=-1)

def forward(tok_in, cond_in, feats, live, params):
    w_ada, b_ada, w_qkv, b_qv, w_proj, b_proj, w_fc1, b_fc1, w_fc2, b_fc2 = params
    batch = tok_in.shape[0]
    cond_vec = cond_in + feats
    silu_c = low(cond_vec * jax.nn.sigmoid(cond_vec))
    modulate = low_back(jnp.dot(silu_c, w_ada, precision=highest) + b_ada)
    pieces = [modulate[:, None, i * D:(i + 1) * D] for i in range(6)]
    shift_one, scale_one, gate_one, shift_two, scale_two, gate_two = pieces
    a_in = low(layer_norm(tok_in) * (1.0 + scale_one) + shift_one)
    qkv = jnp.einsum('bsd,de->bse', a_in, w_qkv, precision=highest)
    query = qkv[..., :D] + b_qv[:D]
    keys = qkv[..., D:2 * D]
    values = qkv[..., 2 * D:] + b_qv[D:]
    query = low(low_back(query)).reshape(batch, SEQ, HEADS, HEAD_DIM)
    keys = low(low_back(keys)).reshape(batch, SEQ, HEADS, HEAD_DIM)
    values = low(low_back(values)).reshape(batch, SEQ, HEADS, HEAD_DIM)
    scores = low_back(jnp.einsum('bqhe,bkhe->bhqk', query, keys, precision=highest) / math.sqrt(HEAD_DIM))
    probs = low(jax.nn.softmax(scores, axis=-1))
    attended = jnp.einsum('bhqk,bkhe->bqhe', probs, values, precision=highest).reshape(batch, SEQ, D)
    attended = low(low_back(attended))
    attn_out = low_back(jnp.einsum('bsd,de->bse', attended, w_proj, precision=highest) + b_proj)
    mid = tok_in + gate_one * attn_out
    m_in = low(layer_norm(mid) * (1.0 + scale_two) + shift_two)
    hidden = low_back(jnp.einsum('bsd,de->bse', m_in, w_fc1, precision=highest) + b_fc1)
    act = low(gelu_tanh(hidden))
    mlp_out = low_back(jnp.einsum('bse,ed->bsd', act, w_fc2, precision=highest) + b_fc2)
    return live[:, None, None] * (mid + gate_two * mlp_out)

def reference(tokens, cond, timesteps, counts, w_ada, b_ada, w_qkv, b_qv, w_proj, b_proj, w_fc1, b_fc1, w_fc2, b_fc2, cotangent):
    params = tuple((p.astype(jnp.float32) for p in (w_ada, b_ada, w_qkv, b_qv, w_proj, b_proj, w_fc1, b_fc1, w_fc2, b_fc2)))
    slot_ids = jnp.arange(ITEMS).astype(jnp.int32)
    live = (slot_ids % CAP < counts[slot_ids // CAP]).astype(jnp.float32)
    feats = time_features(timesteps)
    group = 4 * CAP
    groups = ITEMS // group

    def shaped(array):
        return array.reshape((groups, group) + array.shape[1:])
    inputs = (shaped(tokens.astype(jnp.float32)), shaped(cond.astype(jnp.float32)), shaped(feats), shaped(live), shaped(cotangent.astype(jnp.float32)))
    zeros = tuple((jnp.zeros(p.shape, jnp.float32) for p in params))

    def step(totals, block):
        tok_g, cond_g, feat_g, live_g, cot_g = block

        def apply(tok_in, cond_in, prm):
            return forward(tok_in, cond_in, feat_g, live_g, prm)
        result, pull = jax.vjp(apply, tok_g, cond_g, params)
        grad_tok, grad_c, grad_p = pull(cot_g)
        totals = tuple((a + b for a, b in zip(totals, grad_p)))
        return (totals, (result, grad_tok, grad_c))
    totals, (result, grad_tok, grad_c) = lax.scan(step, zeros, inputs)
    out = result.reshape(ITEMS, SEQ, D).astype(jnp.bfloat16)
    grad_tokens = grad_tok.reshape(ITEMS, SEQ, D)
    grad_cond = grad_c.reshape(ITEMS, D)
    return (out, grad_tokens, grad_cond, totals[0], totals[1], totals[2], totals[3], totals[4], totals[5], totals[6], totals[7], totals[8], totals[9])
```

```python
import math

import jax
import jax.numpy as jnp
from jax import lax
from jax.sharding import PartitionSpec as P

HEADS = 16
HEAD_DIM = 72

F32 = jnp.float32
BF16 = jnp.bfloat16
eps_norm = 1e-06


def norm_rows(value):
    center = value - jnp.mean(value, axis=-1, keepdims=True)
    inv_std = lax.rsqrt(jnp.mean(center * center, axis=-1, keepdims=True) + eps_norm)
    return (center * inv_std, inv_std)


def norm_back(grad, normed, inv_std):
    return inv_std * (
        grad
        - jnp.mean(grad, axis=-1, keepdims=True)
        - normed * jnp.mean(grad * normed, axis=-1, keepdims=True)
    )


def gelu_tanh(value):
    return (
        0.5
        * value
        * (1.0 + jnp.tanh(0.7978845608028654 * (value + 0.044715 * value * value * value)))
    )


def gelu_tanh_grad(value):
    inner = 0.7978845608028654 * (value + 0.044715 * value * value * value)
    tan = jnp.tanh(inner)
    slope = 0.7978845608028654 * (1.0 + 3.0 * 0.044715 * value * value)
    return 0.5 * (1.0 + tan) + 0.5 * value * (1.0 - tan * tan) * slope


def time_features(steps, width):
    half_width = width // 2
    freqs = jnp.exp(-math.log(10000.0) * jnp.arange(half_width).astype(F32) / half_width)
    angles = steps.astype(F32)[:, None] * freqs[None, :]
    return jnp.concatenate([jnp.cos(angles), jnp.sin(angles)], axis=-1)


def mm(left, right):
    return jnp.einsum("sk,kn->sn", left, right, preferred_element_type=F32)


def mm_back(grad, weight):
    return jnp.einsum("sn,kn->sk", grad, weight, preferred_element_type=F32)


def outer_sum(left, right):
    return jnp.einsum("sk,sn->kn", left, right, preferred_element_type=F32)


def gather_wide(value, axis=0):
    return lax.all_gather(value, "wide", axis=axis, tiled=True)


def on_device(
    tokens,
    cond,
    timesteps,
    counts,
    w_ada,
    b_ada,
    w_qkv,
    b_qv,
    w_proj,
    b_proj,
    w_fc1,
    b_fc1,
    w_fc2,
    b_fc2,
    cotangent,
):
    slots, half_len, width = tokens.shape
    pair = lax.axis_size("narrow")
    n_wide = lax.axis_size("wide")
    me = lax.axis_index("narrow")
    here = lax.axis_index("wide")
    seq = half_len * pair
    rows = slots * half_len
    all_rows = slots * seq
    wh = width // pair
    heads = HEADS // pair
    mlp = w_fc1.shape[1]
    mh = mlp // pair
    shard = w_ada.shape[0]
    head_scale = 1.0 / math.sqrt(HEAD_DIM)

    qkv_half = lax.dynamic_index_in_dim(
        w_qkv.reshape(-1, 3, pair, wh), me, 2, keepdims=False
    ).reshape(-1, 3 * wh)
    fc1_half = lax.dynamic_index_in_dim(
        w_fc1.reshape(-1, n_wide, pair, mh // n_wide), me, 2, keepdims=False
    ).reshape(-1, mh)
    fc2_half = lax.dynamic_index_in_dim(
        w_fc2.reshape(pair, -1, width), me, 0, keepdims=False
    )

    cond_vec = cond.astype(F32) + time_features(timesteps, width)
    cond_sig = jax.nn.sigmoid(cond_vec)
    silu_low = (cond_vec * cond_sig).astype(BF16)
    silu_all = gather_wide(silu_low)
    silu_cols = lax.dynamic_slice_in_dim(silu_all, here * shard, shard, 1)
    mod_part = jnp.dot(silu_cols, w_ada, preferred_element_type=F32)
    biases = gather_wide(jnp.concatenate([b_ada, b_qv, b_proj, b_fc1, b_fc2])[None])
    cuts = []
    at = 0
    for piece in (b_ada, b_qv, b_proj, b_fc1, b_fc2):
        cuts.append(biases[:, at : at + piece.shape[0]].astype(F32))
        at += piece.shape[0]
    ada_bias, qv_bias, proj_bias, fc1_bias, fc2_bias = [c.reshape(-1) for c in cuts]
    fc1_bias_half = lax.dynamic_index_in_dim(
        fc1_bias.reshape(n_wide, pair, -1), me, 1, keepdims=False
    ).reshape(-1)
    qv_bias_half = lax.dynamic_index_in_dim(qv_bias.reshape(2, pair, wh), me, 1, keepdims=False)

    modulate = lax.psum_scatter(mod_part, "wide", scatter_dimension=0, tiled=True) + ada_bias
    shift_one, scale_one, gate_one, shift_two, scale_two, gate_two = [
        modulate[:, None, i * width : (i + 1) * width] for i in range(6)
    ]

    qkv_w = gather_wide(qkv_half)
    proj_w = gather_wide(w_proj)
    fc1_w = gather_wide(fc1_half)
    fc2_w = gather_wide(fc2_half)

    def both_halves(value):
        value = value.reshape(slots, half_len, -1)
        return lax.all_gather(value, "narrow", axis=1, tiled=True).reshape(all_rows, -1)

    def sum_halves(value):
        value = value.astype(BF16).reshape(slots, seq, -1)
        return (
            lax.psum_scatter(value, "narrow", scatter_dimension=1, tiled=True)
            .astype(F32)
            .reshape(slots, half_len, -1)
        )

    live_slot = (jnp.arange(slots, dtype=jnp.int32) < counts[0]).astype(F32)[:, None, None]
    tok_float = tokens.astype(F32)
    normed_one, inv_one = norm_rows(tok_float)
    a_in = (normed_one * (1.0 + scale_one) + shift_one).astype(BF16).reshape(rows, width)
    a_full = both_halves(a_in)
    qkv = mm(a_full, qkv_w)
    query = (qkv[:, :wh] + qv_bias_half[0]).astype(BF16)
    keys = qkv[:, wh : 2 * wh].astype(BF16)
    values = (qkv[:, 2 * wh :] + qv_bias_half[1]).astype(BF16)

    def to_heads(value):
        return value.reshape(slots, seq, heads, HEAD_DIM)

    query_heads, key_heads, value_heads = to_heads(query), to_heads(keys), to_heads(values)
    scores = (
        jnp.einsum("cqhe,ckhe->chqk", query_heads, key_heads, preferred_element_type=F32)
        * head_scale
    )
    log_total = jax.nn.logsumexp(scores, axis=-1, keepdims=True)
    probs = jnp.exp(scores - log_total)
    probs_low = probs.astype(BF16)
    attended = (
        jnp.einsum("chqk,ckhe->cqhe", probs_low, value_heads, preferred_element_type=F32)
        .astype(BF16)
        .reshape(slots, seq, wh)
    )
    att_own = lax.all_to_all(attended, "narrow", split_axis=1, concat_axis=2, tiled=True)
    att_own = att_own.reshape(rows, width)
    attn_out = (mm(att_own, proj_w) + proj_bias).reshape(slots, half_len, width)
    mid = tok_float + gate_one * attn_out
    normed_two, inv_two = norm_rows(mid)
    m_in = (normed_two * (1.0 + scale_two) + shift_two).astype(BF16).reshape(rows, width)
    m_full = both_halves(m_in)
    hidden = mm(m_full, fc1_w) + fc1_bias_half
    act_low = gelu_tanh(hidden).astype(BF16)
    mlp_out = sum_halves(mm(act_low, fc2_w)) + fc2_bias
    out = (live_slot * (mid + gate_two * mlp_out)).astype(BF16)

    grad_out = live_slot * cotangent.astype(F32)
    d_mlp = (gate_two * grad_out).astype(BF16).reshape(rows, width)
    d_mlp_full = both_halves(d_mlp)
    d_gate_two = jnp.sum(grad_out * mlp_out, axis=1)
    fc2_bias_sum = jnp.sum(d_mlp.astype(F32), axis=0)
    grad_fc2_part = outer_sum(act_low, d_mlp_full)
    d_hidden = (mm_back(d_mlp_full, fc2_w) * gelu_tanh_grad(hidden)).astype(BF16)
    fc1_bias_sum = jnp.sum(d_hidden.astype(F32), axis=0)
    grad_fc1_part = outer_sum(m_full, d_hidden)
    d_m_in = sum_halves(mm_back(d_hidden, fc1_w))
    d_scale_two = jnp.sum(d_m_in * normed_two, axis=1)
    d_shift_two = jnp.sum(d_m_in, axis=1)
    d_mid = grad_out + norm_back(d_m_in * (1.0 + scale_two), normed_two, inv_two)
    d_attn = (gate_one * d_mid).astype(BF16).reshape(rows, width)
    d_gate_one = jnp.sum(d_mid * attn_out, axis=1)
    proj_bias_sum = jnp.sum(d_attn.astype(F32), axis=0)
    grad_proj_part = outer_sum(att_own, d_attn)
    d_att_own = mm_back(d_attn, proj_w).astype(BF16).reshape(slots, half_len, width)
    d_att = lax.all_to_all(d_att_own, "narrow", split_axis=2, concat_axis=1, tiled=True)
    d_att = to_heads(d_att)
    d_probs = jnp.einsum("cqhe,ckhe->chqk", d_att, value_heads, preferred_element_type=F32)
    d_scores = (probs * (d_probs - jnp.sum(probs * d_probs, axis=-1, keepdims=True))).astype(BF16)
    d_query = (
        jnp.einsum("chqk,ckhe->cqhe", d_scores, key_heads, preferred_element_type=F32)
        * head_scale
    ).astype(BF16).reshape(all_rows, wh)
    d_keys = (
        jnp.einsum("chqk,cqhe->ckhe", d_scores, query_heads, preferred_element_type=F32)
        * head_scale
    ).astype(BF16).reshape(all_rows, wh)
    d_values = (
        jnp.einsum("chqk,cqhe->ckhe", probs_low, d_att, preferred_element_type=F32)
        .astype(BF16)
        .reshape(all_rows, wh)
    )
    d_qkv = jnp.concatenate([d_query, d_keys, d_values], axis=-1)
    qv_bias_sum = jnp.stack(
        [jnp.sum(d_query.astype(F32), axis=0), jnp.sum(d_values.astype(F32), axis=0)]
    )
    grad_qkv_part = outer_sum(a_full, d_qkv)
    d_a_in = sum_halves(mm_back(d_qkv, qkv_w))
    d_scale_one = jnp.sum(d_a_in * normed_one, axis=1)
    d_shift_one = jnp.sum(d_a_in, axis=1)
    grad_tokens = d_mid + norm_back(d_a_in * (1.0 + scale_one), normed_one, inv_one)

    d_modulate = jnp.concatenate(
        [d_shift_one, d_scale_one, d_gate_one, d_shift_two, d_scale_two, d_gate_two], axis=-1
    )
    def place(half, shape, axis):
        spread = jnp.zeros(shape, F32)
        return lax.dynamic_update_index_in_dim(spread, half, me, axis)

    qv_sum = place(qv_bias_sum, (2, pair, wh), 1).reshape(n_wide, -1)
    fc1_sum = place(fc1_bias_sum.reshape(n_wide, -1), (n_wide, pair, mh // n_wide), 1).reshape(
        n_wide, -1
    )
    bias_sums = jnp.concatenate(
        [
            qv_sum,
            proj_bias_sum.reshape(n_wide, -1),
            fc1_sum,
            fc2_bias_sum.reshape(n_wide, -1),
        ],
        axis=1,
    )
    bias_own = lax.psum(
        lax.psum_scatter(bias_sums, "wide", scatter_dimension=0, tiled=True), "narrow"
    ).reshape(-1)
    bias_grads = []
    at = 0
    for piece in (b_qv, b_proj, b_fc1, b_fc2):
        bias_grads.append(bias_own[at : at + piece.shape[0]])
        at += piece.shape[0]

    d_mod_low = lax.psum(d_modulate, "narrow").astype(BF16)
    d_mod_all = gather_wide(d_mod_low)
    grad_ada = outer_sum(silu_cols, d_mod_all)
    ada_cut = b_ada.shape[0]
    grad_ada_bias = jnp.sum(
        lax.dynamic_slice_in_dim(d_mod_all, here * ada_cut, ada_cut, 1).astype(F32), axis=0
    )
    d_silu_cols = mm_back(d_mod_all, w_ada)
    d_silu = lax.all_to_all(d_silu_cols, "wide", split_axis=0, concat_axis=1, tiled=True)
    grad_cond = d_silu * (cond_sig + cond_vec * cond_sig * (1.0 - cond_sig))

    def scatter_wide(part):
        return lax.psum_scatter(part.astype(BF16), "wide", scatter_dimension=0, tiled=True)

    def join_pair(piece):
        return lax.all_gather(piece, "narrow", axis=0, tiled=False).astype(F32)

    fc2_own = join_pair(scatter_wide(grad_fc2_part)).reshape(-1, width)
    fc1_own = join_pair(scatter_wide(grad_fc1_part)).reshape(pair, shard, n_wide, -1)
    fc1_own = fc1_own.transpose(1, 2, 0, 3).reshape(shard, mlp)
    proj_own = jnp.sum(join_pair(scatter_wide(grad_proj_part)), axis=0)
    qkv_own = join_pair(scatter_wide(grad_qkv_part)).reshape(pair, shard, 3, wh)
    qkv_own = qkv_own.transpose(1, 2, 0, 3).reshape(shard, 3 * width)

    return (
        out,
        grad_tokens,
        grad_cond,
        grad_ada,
        grad_ada_bias,
        qkv_own,
        bias_grads[0],
        proj_own,
        bias_grads[1],
        fc1_own,
        bias_grads[2],
        fc2_own,
        bias_grads[3],
    )


def solution(mesh):
    in_specs = (
        P("wide", "narrow", None),
        P("wide", None),
        P("wide"),
        P("wide"),
        P("wide", None),
        P("wide"),
        P("wide", None),
        P("wide"),
        P("wide", None),
        P("wide"),
        P("wide", None),
        P("wide"),
        P("wide", None),
        P("wide"),
        P("wide", "narrow", None),
    )
    out_specs = (
        P("wide", "narrow", None),
        P("wide", "narrow", None),
        P("wide", None),
        P("wide", None),
        P("wide"),
        P("wide", None),
        P("wide"),
        P("wide", None),
        P("wide"),
        P("wide", None),
        P("wide"),
        P("wide", None),
        P("wide"),
    )
    return jax.shard_map(
        on_device, mesh=mesh, in_specs=in_specs, out_specs=out_specs, check_vma=False
    )
```

```python
import math

import jax
import jax.numpy as jnp
from jax import lax
from jax.experimental import pallas as pl
from jax.experimental.pallas import tpu as pltpu
from jax.sharding import PartitionSpec as P

HEADS = 16
HEAD_DIM = 72

F32 = jnp.float32
BF16 = jnp.bfloat16
eps_norm = 1e-06


def norm_rows(value):
    center = value - jnp.mean(value, axis=-1, keepdims=True)
    inv_std = lax.rsqrt(jnp.mean(center * center, axis=-1, keepdims=True) + eps_norm)
    return (center * inv_std, inv_std)


def norm_back(grad, normed, inv_std):
    return inv_std * (
        grad
        - jnp.mean(grad, axis=-1, keepdims=True)
        - normed * jnp.mean(grad * normed, axis=-1, keepdims=True)
    )


def gelu_tanh(value):
    return (
        0.5
        * value
        * (1.0 + jnp.tanh(0.7978845608028654 * (value + 0.044715 * value * value * value)))
    )


def gelu_tanh_grad(value):
    inner = 0.7978845608028654 * (value + 0.044715 * value * value * value)
    tan = jnp.tanh(inner)
    slope = 0.7978845608028654 * (1.0 + 3.0 * 0.044715 * value * value)
    return 0.5 * (1.0 + tan) + 0.5 * value * (1.0 - tan * tan) * slope


def time_features(steps, width):
    half_width = width // 2
    freqs = jnp.exp(-math.log(10000.0) * jnp.arange(half_width).astype(F32) / half_width)
    angles = steps.astype(F32)[:, None] * freqs[None, :]
    return jnp.concatenate([jnp.cos(angles), jnp.sin(angles)], axis=-1)


def mm(left, right):
    return jnp.einsum("sk,kn->sn", left, right, preferred_element_type=F32)


def mm_back(grad, weight):
    return jnp.einsum("sn,kn->sk", grad, weight, preferred_element_type=F32)


def outer_sum(left, right):
    return jnp.einsum("sk,sn->kn", left, right, preferred_element_type=F32)


def gather_wide(value, axis=0):
    return lax.all_gather(value, "wide", axis=axis, tiled=True)


def on_device(
    tokens,
    cond,
    timesteps,
    counts,
    w_ada,
    b_ada,
    w_qkv,
    b_qv,
    w_proj,
    b_proj,
    w_fc1,
    b_fc1,
    w_fc2,
    b_fc2,
    cotangent,
):
    slots, half_len, width = tokens.shape
    pair = lax.axis_size("narrow")
    n_wide = lax.axis_size("wide")
    me = lax.axis_index("narrow")
    here = lax.axis_index("wide")
    seq = half_len * pair
    rows = slots * half_len
    all_rows = slots * seq
    wh = width // pair
    heads = HEADS // pair
    mlp = w_fc1.shape[1]
    mh = mlp // pair
    shard = w_ada.shape[0]
    head_scale = 1.0 / math.sqrt(HEAD_DIM)

    qkv_half = lax.dynamic_index_in_dim(
        w_qkv.reshape(-1, 3, pair, wh), me, 2, keepdims=False
    ).reshape(-1, 3 * wh)
    fc1_half = lax.dynamic_index_in_dim(
        w_fc1.reshape(-1, n_wide, pair, mh // n_wide), me, 2, keepdims=False
    ).reshape(-1, mh)
    fc2_half = lax.dynamic_index_in_dim(
        w_fc2.reshape(pair, -1, width), me, 0, keepdims=False
    )

    cond_vec = cond.astype(F32) + time_features(timesteps, width)
    cond_sig = jax.nn.sigmoid(cond_vec)
    silu_low = (cond_vec * cond_sig).astype(BF16)
    silu_all = gather_wide(silu_low)
    silu_cols = lax.dynamic_slice_in_dim(silu_all, here * shard, shard, 1)
    mod_part = jnp.dot(silu_cols, w_ada, preferred_element_type=F32)
    biases = gather_wide(jnp.concatenate([b_ada, b_qv, b_proj, b_fc1, b_fc2])[None])
    cuts = []
    at = 0
    for piece in (b_ada, b_qv, b_proj, b_fc1, b_fc2):
        cuts.append(biases[:, at : at + piece.shape[0]].astype(F32))
        at += piece.shape[0]
    ada_bias, qv_bias, proj_bias, fc1_bias, fc2_bias = [c.reshape(-1) for c in cuts]
    fc1_bias_half = lax.dynamic_index_in_dim(
        fc1_bias.reshape(n_wide, pair, -1), me, 1, keepdims=False
    ).reshape(-1)
    qv_bias_half = lax.dynamic_index_in_dim(qv_bias.reshape(2, pair, wh), me, 1, keepdims=False)

    modulate = lax.psum_scatter(mod_part, "wide", scatter_dimension=0, tiled=True) + ada_bias
    shift_one, scale_one, gate_one, shift_two, scale_two, gate_two = [
        modulate[:, None, i * width : (i + 1) * width] for i in range(6)
    ]

    qkv_w = gather_wide(qkv_half)
    proj_w = gather_wide(w_proj)
    fc1_w = gather_wide(fc1_half)
    fc2_w = gather_wide(fc2_half)

    def both_halves(value):
        value = value.reshape(slots, half_len, -1)
        return lax.all_gather(value, "narrow", axis=1, tiled=True).reshape(all_rows, -1)

    def sum_halves(value):
        value = value.astype(BF16).reshape(slots, seq, -1)
        return (
            lax.psum_scatter(value, "narrow", scatter_dimension=1, tiled=True)
            .astype(F32)
            .reshape(slots, half_len, -1)
        )

    live_slot = (jnp.arange(slots, dtype=jnp.int32) < counts[0]).astype(F32)[:, None, None]
    tok_float = tokens.astype(F32)
    normed_one, inv_one = norm_rows(tok_float)
    a_in = (normed_one * (1.0 + scale_one) + shift_one).astype(BF16).reshape(rows, width)
    a_full = both_halves(a_in)
    qkv = mm(a_full, qkv_w)
    query = (qkv[:, :wh] + qv_bias_half[0]).astype(BF16)
    keys = qkv[:, wh : 2 * wh].astype(BF16)
    values = (qkv[:, 2 * wh :] + qv_bias_half[1]).astype(BF16)

    def to_heads(value):
        return value.reshape(slots, seq, heads, HEAD_DIM)

    query_heads, key_heads, value_heads = to_heads(query), to_heads(keys), to_heads(values)
    scores = (
        jnp.einsum("cqhe,ckhe->chqk", query_heads, key_heads, preferred_element_type=F32)
        * head_scale
    )
    log_total = jax.nn.logsumexp(scores, axis=-1, keepdims=True)
    probs = jnp.exp(scores - log_total)
    probs_low = probs.astype(BF16)
    attended = (
        jnp.einsum("chqk,ckhe->cqhe", probs_low, value_heads, preferred_element_type=F32)
        .astype(BF16)
        .reshape(slots, seq, wh)
    )
    att_own = lax.all_to_all(attended, "narrow", split_axis=1, concat_axis=2, tiled=True)
    att_own = att_own.reshape(rows, width)
    attn_out = (mm(att_own, proj_w) + proj_bias).reshape(slots, half_len, width)
    mid = tok_float + gate_one * attn_out
    normed_two, inv_two = norm_rows(mid)
    m_in = (normed_two * (1.0 + scale_two) + shift_two).astype(BF16).reshape(rows, width)
    m_full = both_halves(m_in)
    hidden = mm(m_full, fc1_w) + fc1_bias_half
    act_low = gelu_tanh(hidden).astype(BF16)
    mlp_out = sum_halves(mm(act_low, fc2_w)) + fc2_bias
    out = (live_slot * (mid + gate_two * mlp_out)).astype(BF16)

    grad_out = live_slot * cotangent.astype(F32)
    d_mlp = (gate_two * grad_out).astype(BF16).reshape(rows, width)
    d_mlp_full = both_halves(d_mlp)
    d_gate_two = jnp.sum(grad_out * mlp_out, axis=1)
    fc2_bias_sum = jnp.sum(d_mlp.astype(F32), axis=0)
    grad_fc2_part = outer_sum(act_low, d_mlp_full)
    d_hidden = (mm_back(d_mlp_full, fc2_w) * gelu_tanh_grad(hidden)).astype(BF16)
    fc1_bias_sum = jnp.sum(d_hidden.astype(F32), axis=0)
    grad_fc1_part = outer_sum(m_full, d_hidden)
    d_m_in = sum_halves(mm_back(d_hidden, fc1_w))
    d_scale_two = jnp.sum(d_m_in * normed_two, axis=1)
    d_shift_two = jnp.sum(d_m_in, axis=1)
    d_mid = grad_out + norm_back(d_m_in * (1.0 + scale_two), normed_two, inv_two)
    d_attn = (gate_one * d_mid).astype(BF16).reshape(rows, width)
    d_gate_one = jnp.sum(d_mid * attn_out, axis=1)
    proj_bias_sum = jnp.sum(d_attn.astype(F32), axis=0)
    grad_proj_part = outer_sum(att_own, d_attn)
    d_att_own = mm_back(d_attn, proj_w).astype(BF16).reshape(slots, half_len, width)
    d_att = lax.all_to_all(d_att_own, "narrow", split_axis=2, concat_axis=1, tiled=True)
    d_att = to_heads(d_att)
    d_probs = jnp.einsum("cqhe,ckhe->chqk", d_att, value_heads, preferred_element_type=F32)
    d_scores = (probs * (d_probs - jnp.sum(probs * d_probs, axis=-1, keepdims=True))).astype(BF16)
    d_query = (
        jnp.einsum("chqk,ckhe->cqhe", d_scores, key_heads, preferred_element_type=F32)
        * head_scale
    ).astype(BF16).reshape(all_rows, wh)
    d_keys = (
        jnp.einsum("chqk,cqhe->ckhe", d_scores, query_heads, preferred_element_type=F32)
        * head_scale
    ).astype(BF16).reshape(all_rows, wh)
    d_values = (
        jnp.einsum("chqk,cqhe->ckhe", probs_low, d_att, preferred_element_type=F32)
        .astype(BF16)
        .reshape(all_rows, wh)
    )
    d_qkv = jnp.concatenate([d_query, d_keys, d_values], axis=-1)
    qv_bias_sum = jnp.stack(
        [jnp.sum(d_query.astype(F32), axis=0), jnp.sum(d_values.astype(F32), axis=0)]
    )
    grad_qkv_part = outer_sum(a_full, d_qkv)
    d_a_in = sum_halves(mm_back(d_qkv, qkv_w))
    d_scale_one = jnp.sum(d_a_in * normed_one, axis=1)
    d_shift_one = jnp.sum(d_a_in, axis=1)
    grad_tokens = d_mid + norm_back(d_a_in * (1.0 + scale_one), normed_one, inv_one)

    d_modulate = jnp.concatenate(
        [d_shift_one, d_scale_one, d_gate_one, d_shift_two, d_scale_two, d_gate_two], axis=-1
    )
    def place(half, shape, axis):
        spread = jnp.zeros(shape, F32)
        return lax.dynamic_update_index_in_dim(spread, half, me, axis)

    qv_sum = place(qv_bias_sum, (2, pair, wh), 1).reshape(n_wide, -1)
    fc1_sum = place(fc1_bias_sum.reshape(n_wide, -1), (n_wide, pair, mh // n_wide), 1).reshape(
        n_wide, -1
    )
    bias_sums = jnp.concatenate(
        [
            qv_sum,
            proj_bias_sum.reshape(n_wide, -1),
            fc1_sum,
            fc2_bias_sum.reshape(n_wide, -1),
        ],
        axis=1,
    )
    bias_own = lax.psum(
        lax.psum_scatter(bias_sums, "wide", scatter_dimension=0, tiled=True), "narrow"
    ).reshape(-1)
    bias_grads = []
    at = 0
    for piece in (b_qv, b_proj, b_fc1, b_fc2):
        bias_grads.append(bias_own[at : at + piece.shape[0]])
        at += piece.shape[0]

    d_mod_low = lax.psum(d_modulate, "narrow").astype(BF16)
    d_mod_all = gather_wide(d_mod_low)
    grad_ada = outer_sum(silu_cols, d_mod_all)
    ada_cut = b_ada.shape[0]
    grad_ada_bias = jnp.sum(
        lax.dynamic_slice_in_dim(d_mod_all, here * ada_cut, ada_cut, 1).astype(F32), axis=0
    )
    d_silu_cols = mm_back(d_mod_all, w_ada)
    d_silu = lax.all_to_all(d_silu_cols, "wide", split_axis=0, concat_axis=1, tiled=True)
    grad_cond = d_silu * (cond_sig + cond_vec * cond_sig * (1.0 - cond_sig))

    def scatter_wide(part):
        return lax.psum_scatter(part.astype(BF16), "wide", scatter_dimension=0, tiled=True)

    def join_pair(piece):
        return lax.all_gather(piece, "narrow", axis=0, tiled=False).astype(F32)

    fc2_own = join_pair(scatter_wide(grad_fc2_part)).reshape(-1, width)
    fc1_own = join_pair(scatter_wide(grad_fc1_part)).reshape(pair, shard, n_wide, -1)
    fc1_own = fc1_own.transpose(1, 2, 0, 3).reshape(shard, mlp)
    proj_own = jnp.sum(join_pair(scatter_wide(grad_proj_part)), axis=0)
    qkv_own = join_pair(scatter_wide(grad_qkv_part)).reshape(pair, shard, 3, wh)
    qkv_own = qkv_own.transpose(1, 2, 0, 3).reshape(shard, 3 * width)

    return (
        out,
        grad_tokens,
        grad_cond,
        grad_ada,
        grad_ada_bias,
        qkv_own,
        bias_grads[0],
        proj_own,
        bias_grads[1],
        fc1_own,
        bias_grads[2],
        fc2_own,
        bias_grads[3],
    )


MESH = pl.DeviceIdType.MESH
NZ = 4
GELU_C = 0.7978845608028654
HBM_SPEC = pl.BlockSpec(memory_space=pl.ANY)
VMEM_SPEC = pl.BlockSpec(memory_space=pltpu.VMEM)
VMEM_LIMIT = 63 << 20


def dot_nn(a, b):
    return lax.dot_general(a, b, (((1,), (0,)), ((), ())), preferred_element_type=F32)


def dot_nt(a, b):
    return lax.dot_general(a, b, (((1,), (1,)), ((), ())), preferred_element_type=F32)


def dot_tn(a, b):
    return lax.dot_general(a, b, (((0,), (0,)), ((), ())), preferred_element_type=F32)


def do_when(cond, fn):
    if cond is True:
        fn()
    else:
        pl.when(cond)(fn)


def both(a, b):
    if a is True:
        return b
    if b is True:
        return a
    return jnp.logical_and(a, b)


def greet(peers):
    barrier = pltpu.get_barrier_semaphore()
    total = 0
    for cond, dev in peers:
        do_when(
            cond,
            lambda dev=dev: pl.semaphore_signal(
                barrier, inc=1, device_id=dev, device_id_type=MESH
            ),
        )
        total = total + (1 if cond is True else cond.astype(jnp.int32))
    pl.semaphore_wait(barrier, total)


def plane_exchange(source, target, send, recv, base, n_wide, w, y):
    copies = []
    for k in range(1, n_wide):
        peer = lax.rem(w + k, n_wide)
        copy = pltpu.make_async_remote_copy(
            src_ref=source(peer),
            dst_ref=target.at[w],
            send_sem=send.at[base + k],
            recv_sem=recv.at[base + k],
            device_id=(peer, y),
            device_id_type=MESH,
        )
        copy.start()
        copies.append(copy)

    def finish():
        for copy in copies:
            copy.wait_recv()
        for copy in copies:
            copy.wait_send()

    return finish


def swap(source, target, send, recv, index, dev):
    copy = pltpu.make_async_remote_copy(
        src_ref=source,
        dst_ref=target,
        send_sem=send.at[index],
        recv_sem=recv.at[index],
        device_id=dev,
        device_id_type=MESH,
    )
    copy.start()
    return copy


def plane_peers(n_wide, w, y):
    peers = [(True, (lax.rem(w + k, n_wide), y)) for k in range(1, n_wide)]
    return peers + [(True, (w, 1 - y))]


def head_kernel(parcel_ref, wada_ref, got_ref, mod_ref, left, part, parts, tot, send, recv):
    n_wide = parcel_ref.shape[0]
    shard = wada_ref.shape[0]
    half = mod_ref.shape[2]
    w, y = lax.axis_index("wide"), lax.axis_index("narrow")
    greet(plane_peers(n_wide, w, y))
    wait = plane_exchange(lambda p: parcel_ref.at[p], got_ref, send, recv, 0, n_wide, w, y)
    got_ref[w] = parcel_ref[w]
    wait()
    for s in range(n_wide):
        left[2 * s : 2 * s + 2, :] = got_ref[s, 0:2, 0:128]
    lhs = left[...][:, :shard].astype(BF16)
    cols = pl.ds(pl.multiple_of(y * half, 128), half)
    res = dot_nn(lhs, wada_ref[:, cols])
    for s in range(n_wide):
        part[s] = res[2 * s : 2 * s + 2, :]
    wait = plane_exchange(lambda p: part.at[p], parts, send, recv, n_wide, n_wide, w, y)
    parts[w] = part[w]
    wait()
    total = parts[0]
    for s in range(1, n_wide):
        total = total + parts[s]
    tot[...] = total
    mod_ref[y] = total
    copy = swap(tot, mod_ref.at[y], send, recv, 0, (w, 1 - y))
    copy.wait()


def tail_kernel(
    dmod_ref, v_ref, silu_ref, wada_ref,
    ada_ref, bsum_ref, vout_ref, dsil_ref,
    dm_pair, dm_low, dm_all, v_all, v_half, v_pair, dm_rows, ds_send, send, recv,
):
    n_wide = v_ref.shape[0]
    shard = wada_ref.shape[0]
    w, y = lax.axis_index("wide"), lax.axis_index("narrow")
    greet(plane_peers(n_wide, w, y))
    copy = swap(dmod_ref, dm_pair, send, recv, 0, (w, 1 - y))
    wait_v = plane_exchange(lambda p: v_ref.at[p], v_all, send, recv, n_wide, n_wide, w, y)
    v_all[w] = v_ref[w]
    copy.wait()
    dm_low[...] = (dmod_ref[...] + dm_pair[...]).astype(BF16)
    wait_dm = plane_exchange(lambda p: dm_low, dm_all, send, recv, 2 * n_wide, n_wide, w, y)
    dm_all[w] = dm_low[...]
    wait_v()
    total = v_all[0]
    for s in range(1, n_wide):
        total = total + v_all[s]
    v_half[...] = total
    copy = swap(v_half, v_pair, send, recv, n_wide, (w, 1 - y))
    wait_dm()
    for s in range(n_wide):
        dm_rows[2 * s : 2 * s + 2, :] = dm_all[s].astype(F32)
    dm32 = dm_rows[...]
    dmb = dm32.astype(BF16)
    res = dot_nt(dmb, wada_ref[...])
    for s in range(n_wide):
        ds_send[s, :, 0:shard] = res[2 * s : 2 * s + 2, :]
    wait_ds = plane_exchange(lambda p: ds_send.at[p], dsil_ref, send, recv, 3 * n_wide, n_wide, w, y)
    dsil_ref[w] = ds_send[w]
    bsum_ref[...] = jnp.sum(dm32, axis=0, keepdims=True)
    ada_ref[...] = dot_tn(silu_ref[...], dmb)
    copy.wait()
    vout_ref[...] = v_half[...] + v_pair[...]
    wait_ds()


class Sems:
    def __init__(self, send, recv):
        self.send, self.recv, self.n = send, recv, 0

    def take(self, count):
        at = self.n
        self.n += count
        return at


class Links:
    def __init__(self, sems):
        self.sems = sems
        self.sent = []

    def copy(self, src, dst, index, dev):
        return pltpu.make_async_remote_copy(
            src_ref=src,
            dst_ref=dst,
            send_sem=self.sems.send.at[index],
            recv_sem=self.sems.recv.at[index],
            device_id=dev,
            device_id_type=MESH,
        )

    def start(self, cond, src, dst, send_index, recv_index, dev):
        copy = pltpu.make_async_remote_copy(
            src_ref=src,
            dst_ref=dst,
            send_sem=self.sems.send.at[send_index],
            recv_sem=self.sems.recv.at[recv_index],
            device_id=dev,
            device_id_type=MESH,
        )
        do_when(cond, copy.start)
        self.sent.append((cond, copy))
        return copy

    def arrived(self, cond, ref, index, dev):
        copy = self.copy(ref, ref, index, dev)
        do_when(cond, copy.wait_recv)

    def left(self, copy):
        copy.wait_send()
        self.sent = [entry for entry in self.sent if entry[1] is not copy]

    def drain(self):
        for cond, copy in self.sent:
            do_when(cond, copy.wait_send)
        self.sent = []


class Gather:
    def __init__(self, links, pos, block, source, sink):
        self.links, self.pos, self.block = links, pos, block
        self.source, self.sink = source, sink
        take = links.sems.take
        self.z_at, self.x_at, self.up_at, self.down_at = take(4), take(4), take(4), take(4)

    def forward(self, cond, s, up, down):
        z, x, c, y = self.pos["z"], self.pos["x"], self.pos["c"], self.pos["y"]
        ref = self.block(s, x)
        if up:
            self.links.start(
                both(cond, z < NZ - 1), ref, ref, self.up_at + s, self.z_at + s,
                self.pos["dev"](z + 1, x, c, y),
            )
        if down:
            self.links.start(
                both(cond, z > 0), ref, ref, self.down_at + s, self.z_at + s,
                self.pos["dev"](z - 1, x, c, y),
            )
        self.links.start(
            cond, ref, ref, self.x_at + s, self.x_at + s, self.pos["dev"](z, 1 - x, c, y)
        )

    def own(self):
        self.forward(self.source, self.pos["z"], True, True)

    def step(self, d):
        z, x = self.pos["z"], self.pos["x"]
        cond = both(self.source, z >= d)
        s = jnp.maximum(z - d, 0)
        self.links.arrived(cond, self.block(s, x), self.z_at + s, self.pos["me"])
        self.forward(cond, s, True, False)
        cond = both(self.source, z <= NZ - 1 - d)
        s = jnp.minimum(z + d, NZ - 1)
        self.links.arrived(cond, self.block(s, x), self.z_at + s, self.pos["me"])
        self.forward(cond, s, False, True)

    def finish(self):
        x = self.pos["x"]
        for s in range(NZ):
            self.links.arrived(self.sink, self.block(s, 1 - x), self.x_at + s, self.pos["me"])


class Scatter:
    def __init__(self, links, pos, block, sums_x, sums_z, source, sink):
        self.links, self.pos, self.block = links, pos, block
        self.sums_x, self.sums_z = sums_x, sums_z
        self.source, self.sink = source, sink
        take = links.sems.take
        self.x_at, self.z_at, self.up_at, self.down_at = take(4), take(5), take(4), take(4)

    def begin(self):
        z, x, c, y = self.pos["z"], self.pos["x"], self.pos["c"], self.pos["y"]
        for s in (3, 0, 2, 1):
            self.links.start(
                self.source, self.block(s, 1 - x), self.sums_x.at[s], self.x_at + s,
                self.x_at + s, self.pos["dev"](z, 1 - x, c, y),
            )

    def add_x(self, s):
        self.links.arrived(True, self.sums_x.at[s], self.x_at + s, self.pos["me"])
        return self.block(s, self.pos["x"])[...].astype(F32) + self.sums_x[s].astype(F32)

    def hop(self, s, up):
        z, x, c, y = self.pos["z"], self.pos["x"], self.pos["c"], self.pos["y"]
        cond = both(self.sink, (z < s) if up else (z > s))

        def run():
            ref = self.block(s, x)
            ref[...] = self.add_x(s).astype(BF16)
            inner = (z > 0) if up else (z < NZ - 1)

            @pl.when(inner)
            def _():
                self.links.arrived(True, self.sums_z.at[s], self.z_at + s, self.pos["me"])
                ref[...] = (ref[...].astype(F32) + self.sums_z[s].astype(F32)).astype(BF16)

        do_when(cond, run)
        near = (z == s - 1) if up else (z == s + 1)
        slot = s if up else jnp.where(near, 4, s)
        to = self.pos["dev"](z + 1 if up else z - 1, x, c, y)
        at = (self.up_at if up else self.down_at) + s
        self.links.start(
            cond, self.block(s, x), self.sums_z.at[slot], at, self.z_at + slot, to
        )

    def finish(self, store):
        z, x = self.pos["z"], self.pos["x"]
        keep = self.block(z, x)

        def run():
            total = keep[...].astype(F32)
            self.links.arrived(True, self.sums_x.at[z], self.x_at + z, self.pos["me"])
            total = total + self.sums_x[z].astype(F32)
            keep[...] = total.astype(BF16)

            @pl.when(z > 0)
            def _():
                self.links.arrived(True, self.sums_z.at[z], self.z_at + z, self.pos["me"])
                keep[...] = (keep[...].astype(F32) + self.sums_z[z].astype(F32)).astype(BF16)

            @pl.when(z < NZ - 1)
            def _():
                self.links.arrived(True, self.sums_z.at[4], self.z_at + 4, self.pos["me"])
                keep[...] = (keep[...].astype(F32) + self.sums_z[4].astype(F32)).astype(BF16)

            store(keep)

        do_when(self.sink, run)

    def hops(self):
        out = []
        for k in range(3):
            out.append(lambda k=k: self.hop(3 - k, True))
            out.append(lambda k=k: self.hop(k, False))
        return out


class GroupGather:
    def __init__(self, links, pos, full):
        self.links, self.pos, self.full = links, pos, full
        self.at = links.sems.take(3)

    def begin(self):
        z, x, c, y = self.pos["z"], self.pos["x"], self.pos["c"], self.pos["y"]
        ref = self.full.at[pl.ds(2 * c, 2), y]
        self.links.start(True, ref, ref, self.at, self.at, self.pos["dev"](z, x, c, 1 - y))
        self.links.start(True, ref, ref, self.at + 1, self.at + 1, self.pos["dev"](z, x, 1 - c, y))

    def relay(self):
        z, x, c, y = self.pos["z"], self.pos["x"], self.pos["c"], self.pos["y"]
        ref = self.full.at[pl.ds(2 * c, 2), 1 - y]
        self.links.arrived(True, ref, self.at, self.pos["me"])
        self.links.start(True, ref, ref, self.at + 2, self.at + 2, self.pos["dev"](z, x, 1 - c, y))

    def finish(self):
        c, y = self.pos["c"], self.pos["y"]
        other = pl.ds(2 * (1 - c), 2)
        self.links.arrived(True, self.full.at[other, y], self.at + 1, self.pos["me"])
        self.links.arrived(True, self.full.at[other, 1 - y], self.at + 2, self.pos["me"])


class GroupSum:
    def __init__(self, links, pos, full, from_core, to_pair, from_pair):
        self.links, self.pos, self.full = links, pos, full
        self.from_core, self.to_pair, self.from_pair = from_core, to_pair, from_pair
        self.at = links.sems.take(2)

    def begin(self):
        z, x, c, y = self.pos["z"], self.pos["x"], self.pos["c"], self.pos["y"]
        self.core_copy = self.links.start(
            True, self.full.at[pl.ds(2 * (1 - c), 2)], self.from_core, self.at, self.at,
            self.pos["dev"](z, x, 1 - c, y),
        )

    def relay(self):
        z, x, c, y = self.pos["z"], self.pos["x"], self.pos["c"], self.pos["y"]
        self.links.arrived(True, self.from_core, self.at, self.pos["me"])
        for s in range(2):
            self.to_pair[s] = (
                self.full[2 * c + s, 1 - y].astype(F32) + self.from_core[s, 1 - y].astype(F32)
            ).astype(BF16)
        self.pair_copy = self.links.start(
            True, self.to_pair, self.from_pair, self.at + 1, self.at + 1,
            self.pos["dev"](z, x, c, 1 - y),
        )

    def arrived(self):
        self.links.arrived(True, self.from_pair, self.at + 1, self.pos["me"])

    def total(self, s):
        c, y = self.pos["c"], self.pos["y"]
        return (
            self.full[2 * c + s, y].astype(F32)
            + self.from_core[s, y].astype(F32)
            + self.from_pair[s].astype(F32)
        )


def gelu_both(u):
    inner = GELU_C * (u + 0.044715 * u * u * u)
    tan = jnp.tanh(inner)
    slope = GELU_C * (1.0 + 3.0 * 0.044715 * u * u)
    act = 0.5 * u * (1.0 + tan)
    grad = 0.5 * (1.0 + tan) + 0.5 * u * (1.0 - tan * tan) * slope
    return act, grad


def block_kernel(
    tok_ref, cot_ref, mod_ref, bqkv_ref, bproj_ref, bfc1_ref, bfc2_ref,
    src_qkv, src_proj, src_fc1, src_fc2,
    out_ref, gtok_ref, dmod_ref, bias_ref, j_qkv, j_fc1, j_fc2, j_proj,
    g_qkv, g_proj, g_fc1, g_fc2,
    i_qkv, i_fc1, i_fc2, own_qkv, own_fc1, own_fc2,
    x_qkv, x_proj, x_fc1, x_fc2, z_qkv, z_proj, z_fc1, z_fc2,
    t_qkv, t_fc1, t_fc2, t_proj,
    a_all, m_all, d_all, da_all, qkv_all, att_all, act_all, gp_all, dqkv_all,
    sum_a, sum_b, core_a, core_b, to_a, to_b, from_a, from_b,
    attn_own, mid_own, dmid_own, mlp_own,
    send, recv, local,
):
    w, y = lax.axis_index("wide"), lax.axis_index("narrow")
    z, x, c = w // 4, (w // 2) % 2, w % 2
    chip = 2 * z + x

    def dev(z, x, c, y):
        return ((z * 2 + x) * 2 + c, y)

    pos = {"z": z, "x": x, "c": c, "y": y, "dev": dev, "me": dev(z, x, 1 - c, y)}
    sems = Sems(send, recv)
    links = Links(sems)
    half_len = tok_ref.shape[1]
    width = tok_ref.shape[2]
    hw = HEAD_DIM * 4
    shard = own_qkv.shape[0]
    rows2 = 2 * shard
    head_scale = 1.0 / math.sqrt(HEAD_DIM)

    sib = dev(z, x, 1 - c, y)
    greet(
        [
            (True, sib),
            (True, dev(z, x, c, 1 - y)),
            (True, dev(z, x, 1 - c, 1 - y)),
            (True, dev(z, 1 - x, c, y)),
            (z < NZ - 1, dev(z + 1, x, c, y)),
            (z > 0, dev(z - 1, x, c, y)),
        ]
    )

    init = sems.take(3)
    pieces = (
        (src_qkv, i_qkv, own_qkv, g_qkv),
        (src_fc1, i_fc1, own_fc1, g_fc1),
        (src_fc2, i_fc2, own_fc2, g_fc2),
    )
    locals_ = []
    for k, (src, inbox, own, full) in enumerate(pieces):
        links.start(True, src.at[2 * y + 1 - c], inbox, init + k, init + k, sib)
        copy = pltpu.make_async_copy(src.at[2 * y + c], own, local.at[k])
        copy.start()
        locals_.append(copy)
    proj_copy = pltpu.make_async_copy(src_proj, g_proj.at[z], local.at[3])
    on_column = x == y
    do_when(on_column, proj_copy.start)

    def place_own(k):
        src, inbox, own, full = pieces[k]
        locals_[k].wait()
        links.arrived(True, inbox, init + k, sib)
        mine, other = own[...].astype(F32), inbox[...].astype(F32)
        first = jnp.where(c == 0, mine, other)
        second = jnp.where(c == 0, other, mine)
        at = pl.ds(pl.multiple_of(chip * rows2, 16), rows2)
        full[at, :] = jnp.concatenate([first, second], axis=0).astype(BF16)

    def rows_of(full):
        return lambda s, xx: full.at[pl.ds(pl.multiple_of((2 * s + xx) * rows2, 16), rows2), :]

    def head_of(s, xx):
        return g_proj.at[s]

    not_column = jnp.logical_not(on_column)
    ga_qkv = Gather(links, pos, rows_of(g_qkv), True, True)
    ga_proj = Gather(links, pos, head_of, on_column, not_column)
    ga_fc1 = Gather(links, pos, rows_of(g_fc1), True, True)
    ga_fc2 = Gather(links, pos, rows_of(g_fc2), True, True)

    def mod(k, s):
        return mod_ref[s, k : k + 1, :]

    def norm(value):
        center = value - jnp.mean(value, axis=-1, keepdims=True)
        inv = lax.rsqrt(jnp.mean(center * center, axis=-1, keepdims=True) + eps_norm)
        return center * inv, inv

    def norm_grad(grad, normed, inv):
        return inv * (
            grad
            - jnp.mean(grad, axis=-1, keepdims=True)
            - normed * jnp.mean(grad * normed, axis=-1, keepdims=True)
        )

    place_own(0)
    ga_qkv.own()
    for s in range(2):
        normed, inv = norm(tok_ref[s].astype(F32))
        a_all[2 * c + s, y] = (normed * (1.0 + mod(1, s)) + mod(0, s)).astype(BF16)
    gg_a = GroupGather(links, pos, a_all)
    gg_a.begin()
    do_when(on_column, proj_copy.wait)
    ga_proj.own()
    for s in range(2):
        d_all[2 * c + s, y] = (mod(5, s) * cot_ref[s].astype(F32)).astype(BF16)
    ga_qkv.step(1)
    place_own(1)
    ga_fc1.own()
    gg_a.relay()
    ga_qkv.step(2)
    gg_d = GroupGather(links, pos, d_all)
    gg_d.begin()
    ga_qkv.step(3)
    place_own(2)
    ga_proj.step(1)
    ga_fc1.step(1)
    ga_fc2.own()
    ga_proj.step(2)
    ga_proj.step(3)
    gg_d.relay()
    gg_a.finish()
    ga_qkv.finish()

    rows = 2 * half_len

    @pl.loop(0, 4)
    def _(i):
        res = dot_nn(a_all[i].reshape(rows, width), g_qkv[...]) + bqkv_ref[...]
        qkv_all[i] = res.astype(BF16)

    ga_fc1.step(2)
    ga_fc1.step(3)
    ga_fc2.step(1)
    ga_proj.finish()

    def head_parts(packed, h):
        return [packed[:, t * hw + h * HEAD_DIM : t * hw + (h + 1) * HEAD_DIM] for t in range(3)]

    def softmax(q, k):
        scores = dot_nt(q, k) * head_scale
        top = jnp.max(scores, axis=-1, keepdims=True)
        e = jnp.exp(scores - top)
        return e * (1.0 / jnp.sum(e, axis=-1, keepdims=True))

    @pl.loop(0, 4)
    def _(i):
        packed = qkv_all[i]
        acc = None
        for h in range(4):
            q, k, v = head_parts(packed, h)
            p = softmax(q, k).astype(BF16)
            o = dot_nn(p, v).astype(BF16)
            att_all[h, i] = o
            term = dot_nn(o, g_proj[h])
            acc = term if acc is None else acc + term
        sum_a[i] = acc.astype(BF16).reshape(2, half_len, width)

    gs_attn = GroupSum(links, pos, sum_a, core_a, to_a, from_a)
    gs_attn.begin()
    ga_fc2.step(2)
    gs_attn.relay()
    ga_fc2.step(3)
    gs_attn.arrived()
    for s in range(2):
        attn = gs_attn.total(s) + bproj_ref[...]
        attn_own[s] = attn
        mid = tok_ref[s].astype(F32) + mod(2, s) * attn
        mid_own[s] = mid
        normed, inv = norm(mid)
        m_all[2 * c + s, y] = (normed * (1.0 + mod(4, s)) + mod(3, s)).astype(BF16)
    gg_m = GroupGather(links, pos, m_all)
    gg_m.begin()
    gg_d.finish()
    ga_fc1.finish()
    gg_m.relay()
    gg_m.finish()

    @pl.loop(0, 4)
    def _(i):
        u = dot_nn(m_all[i].reshape(rows, width), g_fc1[...]) + bfc1_ref[...]
        act, grad = gelu_both(u)
        act_all[i] = act.astype(BF16)
        gp_all[i] = grad.astype(BF16)

    ga_fc2.finish()

    @pl.loop(0, 4)
    def _(i):
        res = dot_nn(act_all[i], g_fc2[...])
        sum_b[i] = res.astype(BF16).reshape(2, half_len, width)

    gs_mlp = GroupSum(links, pos, sum_b, core_b, to_b, from_b)
    gs_mlp.begin()

    bias_ref[...] = jnp.zeros_like(bias_ref)

    def d_hidden_of(i):
        d_act = dot_nt(d_all[i].reshape(rows, width), g_fc2[...])
        d_hidden = (d_act * gp_all[i].astype(F32)).astype(BF16)
        gp_all[i] = d_hidden
        bias_ref[0:1, :] += jnp.sum(d_hidden.astype(F32), axis=0, keepdims=True)

    pl.loop(0, 4)(d_hidden_of)
    links.drain()
    gs_mlp.relay()

    @pl.loop(0, 4)
    def _(i):
        res = dot_nt(gp_all[i], g_fc1[...])
        sum_a[i] = res.astype(BF16).reshape(2, half_len, width)

    gs_dm = GroupSum(links, pos, sum_a, core_a, to_a, from_a)
    gs_dm.begin()

    def outer(left, right, full, lanes):
        @pl.loop(0, width // lanes)
        def _(j):
            at = pl.ds(pl.multiple_of(j * lanes, 128), lanes)
            res = dot_tn(left(at), right())
            full[at, :] = res.astype(BF16)

    all_rows = 4 * rows
    lanes = width // 3
    outer(
        lambda at: act_all[:, :, at].reshape(all_rows, lanes),
        lambda: d_all[...].reshape(all_rows, width),
        g_fc2,
        lanes,
    )
    sc_fc2 = Scatter(links, pos, rows_of(g_fc2), x_fc2, z_fc2, True, True)
    sc_fc2.begin()
    gs_dm.relay()
    outer(
        lambda at: m_all[:, :, :, at].reshape(all_rows, lanes),
        lambda: gp_all[...].reshape(all_rows, width),
        g_fc1,
        lanes,
    )
    sc_fc1 = Scatter(links, pos, rows_of(g_fc1), x_fc1, z_fc1, True, True)
    sc_fc1.begin()
    gs_mlp.arrived()
    for s in range(2):
        mlp = gs_mlp.total(s) + bfc2_ref[...]
        mid = mid_own[s]
        out_ref[s] = (mid + mod(5, s) * mlp).astype(BF16)
        grad_out = cot_ref[s].astype(F32)
        dmod_ref[5, s : s + 1, :] = jnp.sum(grad_out * mlp, axis=0, keepdims=True)
        bias_ref[2:3, :] += jnp.sum(
            d_all[2 * c + s, y].astype(F32), axis=0, keepdims=True
        )
    gs_dm.arrived()
    for s in range(2):
        d_m = gs_dm.total(s)
        normed, inv = norm(mid_own[s])
        dmod_ref[4, s : s + 1, :] = jnp.sum(d_m * normed, axis=0, keepdims=True)
        dmod_ref[3, s : s + 1, :] = jnp.sum(d_m, axis=0, keepdims=True)
        d_mid = cot_ref[s].astype(F32) + norm_grad(d_m * (1.0 + mod(4, s)), normed, inv)
        dmid_own[s] = d_mid
        d_attn = (mod(2, s) * d_mid).astype(BF16)
        da_all[2 * c + s, y] = d_attn
        dmod_ref[2, s : s + 1, :] = jnp.sum(d_mid * attn_own[s], axis=0, keepdims=True)
        bias_ref[1:2, :] += jnp.sum(d_attn.astype(F32), axis=0, keepdims=True)
    gg_da = GroupGather(links, pos, da_all)
    gg_da.begin()
    h_fc2, h_fc1 = sc_fc2.hops(), sc_fc1.hops()
    h_fc2[0]()
    h_fc2[1]()
    gg_da.relay()
    h_fc2[2]()
    h_fc2[3]()
    gg_da.finish()

    @pl.loop(0, 4)
    def _(i):
        packed = qkv_all[i]
        d_attn = da_all[i].reshape(rows, width)
        grads = [[], [], []]
        for h in range(4):
            q, k, v = head_parts(packed, h)
            p = softmax(q, k)
            p_low = p.astype(BF16)
            d_att = dot_nt(d_attn, g_proj[h]).astype(BF16)
            d_p = dot_nt(d_att, v)
            d_s = (p * (d_p - jnp.sum(p * d_p, axis=-1, keepdims=True))).astype(BF16)
            grads[0].append(dot_nn(d_s, k) * head_scale)
            grads[1].append(dot_tn(d_s, q) * head_scale)
            grads[2].append(dot_tn(p_low, d_att))
        d_qkv = jnp.concatenate(grads[0] + grads[1] + grads[2], axis=1).astype(BF16)
        dqkv_all[i] = d_qkv
        bias_ref[3:4, 0 : 3 * hw] += jnp.sum(d_qkv.astype(F32), axis=0, keepdims=True)

    h_fc2[4]()
    h_fc2[5]()

    @pl.loop(0, 4)
    def _(i):
        res = dot_nt(dqkv_all[i], g_qkv[...])
        sum_b[i] = res.astype(BF16).reshape(2, half_len, width)

    gs_da = GroupSum(links, pos, sum_b, core_b, to_b, from_b)
    gs_da.begin()
    h_fc1[0]()
    h_fc1[1]()
    outer(
        lambda at: a_all[:, :, :, at].reshape(all_rows, lanes),
        lambda: dqkv_all[...].reshape(all_rows, 3 * hw),
        g_qkv,
        lanes,
    )
    sc_qkv = Scatter(links, pos, rows_of(g_qkv), x_qkv, z_qkv, True, True)
    sc_qkv.begin()
    links.left(gs_mlp.pair_copy)
    gs_da.relay()

    @pl.loop(0, 4)
    def _(h):
        left = att_all[h].reshape(all_rows, HEAD_DIM)
        g_proj[h] = dot_tn(left, da_all[...].reshape(all_rows, width)).astype(BF16)

    sc_proj = Scatter(links, pos, head_of, x_proj, z_proj, not_column, on_column)
    sc_proj.begin()
    h_fc1[2]()
    h_fc1[3]()
    h_fc1[4]()
    h_fc1[5]()

    joins = []

    def join(scatter, pack, target):
        at = sems.take(4)

        def store(keep):
            total = keep[...].astype(F32)
            pack[0] = total[:shard].astype(BF16)
            pack[1] = total[shard:].astype(BF16)

        scatter.finish(store)
        q = 2 * y + c
        links.start(True, pack.at[1 - c], target.at[q], at, at, dev(z, x, 1 - c, y))
        links.start(True, pack.at[c], target.at[q], at + 1, at + 1, dev(z, x, c, 1 - y))
        links.start(True, pack.at[1 - c], target.at[q], at + 2, at + 2, dev(z, x, 1 - c, 1 - y))
        keep_copy = pltpu.make_async_copy(pack.at[c], target.at[q], local.at[len(joins)])
        keep_copy.start()

        def done():
            keep_copy.wait()
            links.arrived(True, target.at[2 * y + 1 - c], at, sib)
            links.arrived(True, target.at[2 * (1 - y) + c], at + 1, sib)
            links.arrived(True, target.at[2 * (1 - y) + 1 - c], at + 2, sib)

        joins.append(done)

    join(sc_fc2, t_fc2, j_fc2)
    h_qkv, h_proj = sc_qkv.hops(), sc_proj.hops()
    gs_da.arrived()
    for s in range(2):
        d_a = gs_da.total(s)
        normed, inv = norm(tok_ref[s].astype(F32))
        dmod_ref[1, s : s + 1, :] = jnp.sum(d_a * normed, axis=0, keepdims=True)
        dmod_ref[0, s : s + 1, :] = jnp.sum(d_a, axis=0, keepdims=True)
        gtok_ref[s] = dmid_own[s] + norm_grad(d_a * (1.0 + mod(1, s)), normed, inv)
    h_qkv[0]()
    h_qkv[1]()
    join(sc_fc1, t_fc1, j_fc1)
    for k in range(2, 6):
        h_qkv[k]()
    for k in range(6):
        h_proj[k]()

    join(sc_qkv, t_qkv, j_qkv)

    at = sems.take(1)

    def keep_proj(keep):
        t_proj[...] = keep[...]

    sc_proj.finish(keep_proj)
    links.start(on_column, t_proj, t_proj, at, at, dev(z, x, c, 1 - y))
    links.arrived(not_column, t_proj, at, sib)
    j_proj[...] = t_proj[...]
    for done in joins:
        done()
    links.drain()


def fast_device(
    tokens,
    cond,
    timesteps,
    counts,
    w_ada,
    b_ada,
    w_qkv,
    b_qv,
    w_proj,
    b_proj,
    w_fc1,
    b_fc1,
    w_fc2,
    b_fc2,
    cotangent,
):
    slots, half_len, width = tokens.shape
    n_wide = lax.axis_size("wide")
    w, y = lax.axis_index("wide"), lax.axis_index("narrow")
    c = w % 2
    quarter = 2 * y + c
    shard = w_ada.shape[0]
    mlp = w_fc1.shape[1]
    hq = HEADS // 4
    hw = hq * HEAD_DIM
    nq = 3 * hw
    rows = slots * half_len
    mq = mlp // 4

    cond_vec = cond.astype(F32) + time_features(timesteps, width)
    cond_sig = jax.nn.sigmoid(cond_vec)
    silu = (cond_vec * cond_sig).astype(BF16).astype(F32)
    chunks = jnp.pad(
        silu.reshape(slots, n_wide, shard).transpose(1, 0, 2),
        ((0, 0), (0, 0), (0, width - shard)),
    )
    sizes = [b.shape[0] for b in (b_qv, b_proj, b_fc1, b_fc2, b_ada)]
    vector = jnp.concatenate([b_qv, b_proj, b_fc1, b_fc2, b_ada]).astype(F32)
    vector = jnp.pad(vector, (0, width - vector.shape[0]))
    parcel = jnp.concatenate(
        [chunks, jnp.broadcast_to(vector, (n_wide, 2, width))], axis=1
    )
    half = w_ada.shape[1] // 2
    got, mod_halves = pl.pallas_call(
        head_kernel,
        out_shape=(
            jax.ShapeDtypeStruct((n_wide, 4, width), F32),
            jax.ShapeDtypeStruct((2, slots, half), F32),
        ),
        in_specs=[VMEM_SPEC, VMEM_SPEC],
        out_specs=(VMEM_SPEC, VMEM_SPEC),
        scratch_shapes=[
            pltpu.VMEM((n_wide * slots, 128), F32),
            pltpu.VMEM((n_wide, slots, half), F32),
            pltpu.VMEM((n_wide, slots, half), F32),
            pltpu.VMEM((slots, half), F32),
            pltpu.SemaphoreType.DMA((2 * n_wide,)),
            pltpu.SemaphoreType.DMA((2 * n_wide,)),
        ],
        compiler_params=pltpu.CompilerParams(
            collective_id=0, has_side_effects=True, vmem_limit_bytes=48 << 20
        ),
    )(parcel, w_ada)
    cuts = []
    at = 0
    for size in sizes:
        cuts.append(got[:, 2, at : at + size])
        at += size
    qv_bias, proj_bias, fc1_bias, fc2_bias, ada_bias = cuts
    modulate = mod_halves.transpose(1, 0, 2).reshape(slots, -1) + ada_bias.reshape(-1)
    modulate = modulate.reshape(slots, 6, width)
    qv_quarter = lax.dynamic_index_in_dim(
        qv_bias.reshape(2, hq, 4, HEAD_DIM), quarter, 2, keepdims=False
    ).reshape(2, hw)
    bqkv = jnp.concatenate([qv_quarter[0], jnp.zeros((hw,), F32), qv_quarter[1]])[None]
    bfc1 = lax.dynamic_index_in_dim(
        fc1_bias.reshape(n_wide, 4, -1), quarter, 1, keepdims=False
    ).reshape(1, mq)

    live = (jnp.arange(slots, dtype=jnp.int32) < counts[0])[:, None, None]
    cot_live = jnp.where(live, cotangent, jnp.zeros_like(cotangent))
    src_qkv = (
        w_qkv.reshape(shard, 3, hq, 4, HEAD_DIM).transpose(3, 0, 1, 2, 4).reshape(4, shard, nq)
    )
    src_fc1 = (
        w_fc1.reshape(shard, n_wide, 4, mq // n_wide).transpose(2, 0, 1, 3).reshape(4, shard, mq)
    )
    src_fc2 = w_fc2.reshape(4, shard, width)

    v16 = lambda *shape: pltpu.VMEM(shape, BF16)
    v32 = lambda *shape: pltpu.VMEM(shape, F32)
    pair_rows = 2 * shard
    full = (4, 2, half_len, width)
    scratch = [
        v16(width, nq), v16(hq, shard, width), v16(width, mq), v16(mq, width),
        v16(shard, nq), v16(shard, mq), v16(shard, width),
        v16(shard, nq), v16(shard, mq), v16(shard, width),
        v16(4, pair_rows, nq), v16(4, shard, width), v16(4, pair_rows, mq), v16(4, pair_rows, width),
        v16(5, pair_rows, nq), v16(5, shard, width), v16(5, pair_rows, mq), v16(5, pair_rows, width),
        v16(2, shard, nq), v16(2, shard, mq), v16(2, shard, width), v16(shard, width),
        v16(*full), v16(*full), v16(*full), v16(*full),
        v16(4, rows, nq), v16(hq, 4, rows, HEAD_DIM), v16(4, rows, mq), v16(4, rows, mq),
        v16(4, rows, nq),
        v16(*full), v16(*full),
        v16(2, 2, half_len, width), v16(2, 2, half_len, width),
        v16(2, half_len, width), v16(2, half_len, width),
        v16(2, half_len, width), v16(2, half_len, width),
        v32(slots, half_len, width), v32(slots, half_len, width),
        v32(slots, half_len, width), v32(slots, half_len, width),
        pltpu.SemaphoreType.DMA((200,)),
        pltpu.SemaphoreType.DMA((200,)),
        pltpu.SemaphoreType.DMA((4,)),
    ]
    out, gtok, dmod, bias_sums, j_qkv, j_fc1, j_fc2, j_proj = pl.pallas_call(
        block_kernel,
        out_shape=(
            jax.ShapeDtypeStruct(tokens.shape, BF16),
            jax.ShapeDtypeStruct(tokens.shape, F32),
            jax.ShapeDtypeStruct((6, slots, width), F32),
            jax.ShapeDtypeStruct((4, width), F32),
            jax.ShapeDtypeStruct((4, shard, nq), BF16),
            jax.ShapeDtypeStruct((4, shard, mq), BF16),
            jax.ShapeDtypeStruct((4, shard, width), BF16),
            jax.ShapeDtypeStruct((shard, width), BF16),
        ),
        in_specs=[VMEM_SPEC] * 7 + [HBM_SPEC] * 4,
        out_specs=(VMEM_SPEC,) * 4 + (HBM_SPEC,) * 3 + (VMEM_SPEC,),
        scratch_shapes=scratch,
        compiler_params=pltpu.CompilerParams(
            collective_id=1, has_side_effects=True, vmem_limit_bytes=VMEM_LIMIT
        ),
    )(
        tokens, cot_live, modulate, bqkv, proj_bias.reshape(1, width), bfc1,
        fc2_bias.reshape(1, width), src_qkv, w_proj, src_fc1, src_fc2,
    )
    out = jnp.where(live, out, jnp.zeros_like(out))

    def spread(part, count):
        part = part.reshape(count, 1, -1)
        mine = (jnp.arange(4) == quarter).astype(F32)[None, :, None]
        return (part * mine).reshape(n_wide, -1)

    qv_sum = jnp.concatenate([bias_sums[3, :hw], bias_sums[3, 2 * hw : nq]])
    v_rows = jnp.concatenate(
        [
            spread(qv_sum, 2 * hq),
            bias_sums[1].reshape(n_wide, -1),
            spread(bias_sums[0], n_wide),
            bias_sums[2].reshape(n_wide, -1),
        ],
        axis=1,
    )
    v_size = v_rows.shape[1]
    v_pad = -(-v_size // 128) * 128
    v_rows = jnp.pad(v_rows, ((0, 0), (0, v_pad - v_size)))[:, None, :]
    silu_cols = got[:, 0:2, :shard].reshape(n_wide * slots, shard).astype(BF16)
    dmod = dmod.transpose(1, 0, 2).reshape(slots, 6 * width)
    grad_ada, ada_sum, v_out, d_silu = pl.pallas_call(
        tail_kernel,
        out_shape=(
            jax.ShapeDtypeStruct(w_ada.shape, F32),
            jax.ShapeDtypeStruct((1, w_ada.shape[1]), F32),
            jax.ShapeDtypeStruct((1, v_pad), F32),
            jax.ShapeDtypeStruct((n_wide, slots, 128), F32),
        ),
        in_specs=[VMEM_SPEC] * 4,
        out_specs=(VMEM_SPEC,) * 4,
        scratch_shapes=[
            v32(slots, 6 * width), v16(slots, 6 * width), v16(n_wide, slots, 6 * width),
            v32(n_wide, 1, v_pad), v32(1, v_pad), v32(1, v_pad),
            v32(n_wide * slots, 6 * width), v32(n_wide, slots, 128),
            pltpu.SemaphoreType.DMA((4 * n_wide,)),
            pltpu.SemaphoreType.DMA((4 * n_wide,)),
        ],
        compiler_params=pltpu.CompilerParams(
            collective_id=2, has_side_effects=True, vmem_limit_bytes=48 << 20
        ),
    )(dmod, v_rows, silu_cols, w_ada)
    ada_cut = b_ada.shape[0]
    grad_b_ada = lax.dynamic_slice_in_dim(ada_sum[0], w * ada_cut, ada_cut, 0)
    d_silu = d_silu[:, :, :shard].transpose(1, 0, 2).reshape(slots, width)
    grad_cond = d_silu * (cond_sig + cond_vec * cond_sig * (1.0 - cond_sig))
    bias_grads = []
    at = 0
    for size in sizes[:4]:
        bias_grads.append(v_out[0, at : at + size])
        at += size

    grad_qkv = (
        j_qkv.astype(F32)
        .reshape(4, shard, 3, hq, HEAD_DIM)
        .transpose(1, 2, 3, 0, 4)
        .reshape(w_qkv.shape)
    )
    grad_fc1 = (
        j_fc1.astype(F32)
        .reshape(4, shard, n_wide, mq // n_wide)
        .transpose(1, 2, 0, 3)
        .reshape(w_fc1.shape)
    )
    grad_fc2 = j_fc2.astype(F32).reshape(w_fc2.shape)
    return (
        out,
        gtok,
        grad_cond,
        grad_ada,
        grad_b_ada,
        grad_qkv,
        bias_grads[0],
        j_proj.astype(F32),
        bias_grads[1],
        grad_fc1,
        bias_grads[2],
        grad_fc2,
        bias_grads[3],
    )


def solution(mesh):
    in_specs = (
        P("wide", "narrow", None),
        P("wide", None),
        P("wide"),
        P("wide"),
        P("wide", None),
        P("wide"),
        P("wide", None),
        P("wide"),
        P("wide", None),
        P("wide"),
        P("wide", None),
        P("wide"),
        P("wide", None),
        P("wide"),
        P("wide", "narrow", None),
    )
    out_specs = (
        P("wide", "narrow", None),
        P("wide", "narrow", None),
        P("wide", None),
        P("wide", None),
        P("wide"),
        P("wide", None),
        P("wide"),
        P("wide", None),
        P("wide"),
        P("wide", None),
        P("wide"),
        P("wide", None),
        P("wide"),
    )
    small = mesh.shape["wide"] == 16 and mesh.shape["narrow"] == 2
    per_device = fast_device if small else on_device
    return jax.shard_map(
        per_device, mesh=mesh, in_specs=in_specs, out_specs=out_specs, check_vma=False
    )
```

```python
import functools
import math

import jax
import jax.numpy as jnp
from jax import lax
from jax.experimental import pallas as pl
from jax.experimental.pallas import tpu as pltpu
from jax.sharding import PartitionSpec as P

HEADS = 16
HEAD_DIM = 72

F32 = jnp.float32
BF16 = jnp.bfloat16
eps_norm = 1e-06


def norm_rows(value):
    center = value - jnp.mean(value, axis=-1, keepdims=True)
    inv_std = lax.rsqrt(jnp.mean(center * center, axis=-1, keepdims=True) + eps_norm)
    return (center * inv_std, inv_std)


def norm_back(grad, normed, inv_std):
    return inv_std * (
        grad
        - jnp.mean(grad, axis=-1, keepdims=True)
        - normed * jnp.mean(grad * normed, axis=-1, keepdims=True)
    )


def gelu_tanh(value):
    return (
        0.5
        * value
        * (1.0 + jnp.tanh(0.7978845608028654 * (value + 0.044715 * value * value * value)))
    )


def gelu_tanh_grad(value):
    inner = 0.7978845608028654 * (value + 0.044715 * value * value * value)
    tan = jnp.tanh(inner)
    slope = 0.7978845608028654 * (1.0 + 3.0 * 0.044715 * value * value)
    return 0.5 * (1.0 + tan) + 0.5 * value * (1.0 - tan * tan) * slope


def time_features(steps, width):
    half_width = width // 2
    freqs = jnp.exp(-math.log(10000.0) * jnp.arange(half_width).astype(F32) / half_width)
    angles = steps.astype(F32)[:, None] * freqs[None, :]
    return jnp.concatenate([jnp.cos(angles), jnp.sin(angles)], axis=-1)


def mm(left, right):
    return jnp.einsum("sk,kn->sn", left, right, preferred_element_type=F32)


def mm_back(grad, weight):
    return jnp.einsum("sn,kn->sk", grad, weight, preferred_element_type=F32)


def outer_sum(left, right):
    return jnp.einsum("sk,sn->kn", left, right, preferred_element_type=F32)


def gather_wide(value, axis=0):
    return lax.all_gather(value, "wide", axis=axis, tiled=True)


def on_device(
    tokens,
    cond,
    timesteps,
    counts,
    w_ada,
    b_ada,
    w_qkv,
    b_qv,
    w_proj,
    b_proj,
    w_fc1,
    b_fc1,
    w_fc2,
    b_fc2,
    cotangent,
):
    slots, half_len, width = tokens.shape
    pair = lax.axis_size("narrow")
    n_wide = lax.axis_size("wide")
    me = lax.axis_index("narrow")
    here = lax.axis_index("wide")
    seq = half_len * pair
    rows = slots * half_len
    all_rows = slots * seq
    wh = width // pair
    heads = HEADS // pair
    mlp = w_fc1.shape[1]
    mh = mlp // pair
    shard = w_ada.shape[0]
    head_scale = 1.0 / math.sqrt(HEAD_DIM)

    qkv_half = lax.dynamic_index_in_dim(
        w_qkv.reshape(-1, 3, pair, wh), me, 2, keepdims=False
    ).reshape(-1, 3 * wh)
    fc1_half = lax.dynamic_index_in_dim(
        w_fc1.reshape(-1, n_wide, pair, mh // n_wide), me, 2, keepdims=False
    ).reshape(-1, mh)
    fc2_half = lax.dynamic_index_in_dim(
        w_fc2.reshape(pair, -1, width), me, 0, keepdims=False
    )

    cond_vec = cond.astype(F32) + time_features(timesteps, width)
    cond_sig = jax.nn.sigmoid(cond_vec)
    silu_low = (cond_vec * cond_sig).astype(BF16)
    silu_all = gather_wide(silu_low)
    silu_cols = lax.dynamic_slice_in_dim(silu_all, here * shard, shard, 1)
    mod_part = jnp.dot(silu_cols, w_ada, preferred_element_type=F32)
    biases = gather_wide(jnp.concatenate([b_ada, b_qv, b_proj, b_fc1, b_fc2])[None])
    cuts = []
    at = 0
    for piece in (b_ada, b_qv, b_proj, b_fc1, b_fc2):
        cuts.append(biases[:, at : at + piece.shape[0]].astype(F32))
        at += piece.shape[0]
    ada_bias, qv_bias, proj_bias, fc1_bias, fc2_bias = [c.reshape(-1) for c in cuts]
    fc1_bias_half = lax.dynamic_index_in_dim(
        fc1_bias.reshape(n_wide, pair, -1), me, 1, keepdims=False
    ).reshape(-1)
    qv_bias_half = lax.dynamic_index_in_dim(qv_bias.reshape(2, pair, wh), me, 1, keepdims=False)

    modulate = lax.psum_scatter(mod_part, "wide", scatter_dimension=0, tiled=True) + ada_bias
    shift_one, scale_one, gate_one, shift_two, scale_two, gate_two = [
        modulate[:, None, i * width : (i + 1) * width] for i in range(6)
    ]

    qkv_w = gather_wide(qkv_half)
    proj_w = gather_wide(w_proj)
    fc1_w = gather_wide(fc1_half)
    fc2_w = gather_wide(fc2_half)

    def both_halves(value):
        value = value.reshape(slots, half_len, -1)
        return lax.all_gather(value, "narrow", axis=1, tiled=True).reshape(all_rows, -1)

    def sum_halves(value):
        value = value.astype(BF16).reshape(slots, seq, -1)
        return (
            lax.psum_scatter(value, "narrow", scatter_dimension=1, tiled=True)
            .astype(F32)
            .reshape(slots, half_len, -1)
        )

    live_slot = (jnp.arange(slots, dtype=jnp.int32) < counts[0]).astype(F32)[:, None, None]
    tok_float = tokens.astype(F32)
    normed_one, inv_one = norm_rows(tok_float)
    a_in = (normed_one * (1.0 + scale_one) + shift_one).astype(BF16).reshape(rows, width)
    a_full = both_halves(a_in)
    qkv = mm(a_full, qkv_w)
    query = (qkv[:, :wh] + qv_bias_half[0]).astype(BF16)
    keys = qkv[:, wh : 2 * wh].astype(BF16)
    values = (qkv[:, 2 * wh :] + qv_bias_half[1]).astype(BF16)

    def to_heads(value):
        return value.reshape(slots, seq, heads, HEAD_DIM)

    query_heads, key_heads, value_heads = to_heads(query), to_heads(keys), to_heads(values)
    scores = (
        jnp.einsum("cqhe,ckhe->chqk", query_heads, key_heads, preferred_element_type=F32)
        * head_scale
    )
    log_total = jax.nn.logsumexp(scores, axis=-1, keepdims=True)
    probs = jnp.exp(scores - log_total)
    probs_low = probs.astype(BF16)
    attended = (
        jnp.einsum("chqk,ckhe->cqhe", probs_low, value_heads, preferred_element_type=F32)
        .astype(BF16)
        .reshape(slots, seq, wh)
    )
    att_own = lax.all_to_all(attended, "narrow", split_axis=1, concat_axis=2, tiled=True)
    att_own = att_own.reshape(rows, width)
    attn_out = (mm(att_own, proj_w) + proj_bias).reshape(slots, half_len, width)
    mid = tok_float + gate_one * attn_out
    normed_two, inv_two = norm_rows(mid)
    m_in = (normed_two * (1.0 + scale_two) + shift_two).astype(BF16).reshape(rows, width)
    m_full = both_halves(m_in)
    hidden = mm(m_full, fc1_w) + fc1_bias_half
    act_low = gelu_tanh(hidden).astype(BF16)
    mlp_out = sum_halves(mm(act_low, fc2_w)) + fc2_bias
    out = (live_slot * (mid + gate_two * mlp_out)).astype(BF16)

    grad_out = live_slot * cotangent.astype(F32)
    d_mlp = (gate_two * grad_out).astype(BF16).reshape(rows, width)
    d_mlp_full = both_halves(d_mlp)
    d_gate_two = jnp.sum(grad_out * mlp_out, axis=1)
    fc2_bias_sum = jnp.sum(d_mlp.astype(F32), axis=0)
    grad_fc2_part = outer_sum(act_low, d_mlp_full)
    d_hidden = (mm_back(d_mlp_full, fc2_w) * gelu_tanh_grad(hidden)).astype(BF16)
    fc1_bias_sum = jnp.sum(d_hidden.astype(F32), axis=0)
    grad_fc1_part = outer_sum(m_full, d_hidden)
    d_m_in = sum_halves(mm_back(d_hidden, fc1_w))
    d_scale_two = jnp.sum(d_m_in * normed_two, axis=1)
    d_shift_two = jnp.sum(d_m_in, axis=1)
    d_mid = grad_out + norm_back(d_m_in * (1.0 + scale_two), normed_two, inv_two)
    d_attn = (gate_one * d_mid).astype(BF16).reshape(rows, width)
    d_gate_one = jnp.sum(d_mid * attn_out, axis=1)
    proj_bias_sum = jnp.sum(d_attn.astype(F32), axis=0)
    grad_proj_part = outer_sum(att_own, d_attn)
    d_att_own = mm_back(d_attn, proj_w).astype(BF16).reshape(slots, half_len, width)
    d_att = lax.all_to_all(d_att_own, "narrow", split_axis=2, concat_axis=1, tiled=True)
    d_att = to_heads(d_att)
    d_probs = jnp.einsum("cqhe,ckhe->chqk", d_att, value_heads, preferred_element_type=F32)
    d_scores = (probs * (d_probs - jnp.sum(probs * d_probs, axis=-1, keepdims=True))).astype(BF16)
    d_query = (
        jnp.einsum("chqk,ckhe->cqhe", d_scores, key_heads, preferred_element_type=F32)
        * head_scale
    ).astype(BF16).reshape(all_rows, wh)
    d_keys = (
        jnp.einsum("chqk,cqhe->ckhe", d_scores, query_heads, preferred_element_type=F32)
        * head_scale
    ).astype(BF16).reshape(all_rows, wh)
    d_values = (
        jnp.einsum("chqk,cqhe->ckhe", probs_low, d_att, preferred_element_type=F32)
        .astype(BF16)
        .reshape(all_rows, wh)
    )
    d_qkv = jnp.concatenate([d_query, d_keys, d_values], axis=-1)
    qv_bias_sum = jnp.stack(
        [jnp.sum(d_query.astype(F32), axis=0), jnp.sum(d_values.astype(F32), axis=0)]
    )
    grad_qkv_part = outer_sum(a_full, d_qkv)
    d_a_in = sum_halves(mm_back(d_qkv, qkv_w))
    d_scale_one = jnp.sum(d_a_in * normed_one, axis=1)
    d_shift_one = jnp.sum(d_a_in, axis=1)
    grad_tokens = d_mid + norm_back(d_a_in * (1.0 + scale_one), normed_one, inv_one)

    d_modulate = jnp.concatenate(
        [d_shift_one, d_scale_one, d_gate_one, d_shift_two, d_scale_two, d_gate_two], axis=-1
    )
    def place(half, shape, axis):
        spread = jnp.zeros(shape, F32)
        return lax.dynamic_update_index_in_dim(spread, half, me, axis)

    qv_sum = place(qv_bias_sum, (2, pair, wh), 1).reshape(n_wide, -1)
    fc1_sum = place(fc1_bias_sum.reshape(n_wide, -1), (n_wide, pair, mh // n_wide), 1).reshape(
        n_wide, -1
    )
    bias_sums = jnp.concatenate(
        [
            qv_sum,
            proj_bias_sum.reshape(n_wide, -1),
            fc1_sum,
            fc2_bias_sum.reshape(n_wide, -1),
        ],
        axis=1,
    )
    bias_own = lax.psum(
        lax.psum_scatter(bias_sums, "wide", scatter_dimension=0, tiled=True), "narrow"
    ).reshape(-1)
    bias_grads = []
    at = 0
    for piece in (b_qv, b_proj, b_fc1, b_fc2):
        bias_grads.append(bias_own[at : at + piece.shape[0]])
        at += piece.shape[0]

    d_mod_low = lax.psum(d_modulate, "narrow").astype(BF16)
    d_mod_all = gather_wide(d_mod_low)
    grad_ada = outer_sum(silu_cols, d_mod_all)
    ada_cut = b_ada.shape[0]
    grad_ada_bias = jnp.sum(
        lax.dynamic_slice_in_dim(d_mod_all, here * ada_cut, ada_cut, 1).astype(F32), axis=0
    )
    d_silu_cols = mm_back(d_mod_all, w_ada)
    d_silu = lax.all_to_all(d_silu_cols, "wide", split_axis=0, concat_axis=1, tiled=True)
    grad_cond = d_silu * (cond_sig + cond_vec * cond_sig * (1.0 - cond_sig))

    def scatter_wide(part):
        return lax.psum_scatter(part.astype(BF16), "wide", scatter_dimension=0, tiled=True)

    def join_pair(piece):
        return lax.all_gather(piece, "narrow", axis=0, tiled=False).astype(F32)

    fc2_own = join_pair(scatter_wide(grad_fc2_part)).reshape(-1, width)
    fc1_own = join_pair(scatter_wide(grad_fc1_part)).reshape(pair, shard, n_wide, -1)
    fc1_own = fc1_own.transpose(1, 2, 0, 3).reshape(shard, mlp)
    proj_own = jnp.sum(join_pair(scatter_wide(grad_proj_part)), axis=0)
    qkv_own = join_pair(scatter_wide(grad_qkv_part)).reshape(pair, shard, 3, wh)
    qkv_own = qkv_own.transpose(1, 2, 0, 3).reshape(shard, 3 * width)

    return (
        out,
        grad_tokens,
        grad_cond,
        grad_ada,
        grad_ada_bias,
        qkv_own,
        bias_grads[0],
        proj_own,
        bias_grads[1],
        fc1_own,
        bias_grads[2],
        fc2_own,
        bias_grads[3],
    )


MESH = pl.DeviceIdType.MESH
NZ = 4
GELU_C = 0.7978845608028654
HBM_SPEC = pl.BlockSpec(memory_space=pl.ANY)
VMEM_SPEC = pl.BlockSpec(memory_space=pltpu.VMEM)
VMEM_LIMIT = 63 << 20


def dot_nn(a, b):
    return lax.dot_general(a, b, (((1,), (0,)), ((), ())), preferred_element_type=F32)


def dot_nt(a, b):
    return lax.dot_general(a, b, (((1,), (1,)), ((), ())), preferred_element_type=F32)


def dot_tn(a, b):
    return lax.dot_general(a, b, (((0,), (0,)), ((), ())), preferred_element_type=F32)


def do_when(cond, fn):
    if cond is True:
        fn()
    else:
        pl.when(cond)(fn)


def both(a, b):
    if a is True:
        return b
    if b is True:
        return a
    return jnp.logical_and(a, b)


def greet(peers):
    barrier = pltpu.get_barrier_semaphore()
    total = 0
    for cond, dev in peers:
        do_when(
            cond,
            lambda dev=dev: pl.semaphore_signal(
                barrier, inc=1, device_id=dev, device_id_type=MESH
            ),
        )
        total = total + (1 if cond is True else cond.astype(jnp.int32))
    pl.semaphore_wait(barrier, total)


class Sems:
    def __init__(self, send, recv):
        self.send, self.recv, self.n = send, recv, 0

    def take(self, count):
        at = self.n
        self.n += count
        return at


class Links:
    def __init__(self, sems):
        self.sems = sems
        self.sent = []

    def copy(self, src, dst, index, dev):
        return pltpu.make_async_remote_copy(
            src_ref=src,
            dst_ref=dst,
            send_sem=self.sems.send.at[index],
            recv_sem=self.sems.recv.at[index],
            device_id=dev,
            device_id_type=MESH,
        )

    def start(self, cond, src, dst, send_index, recv_index, dev):
        copy = pltpu.make_async_remote_copy(
            src_ref=src,
            dst_ref=dst,
            send_sem=self.sems.send.at[send_index],
            recv_sem=self.sems.recv.at[recv_index],
            device_id=dev,
            device_id_type=MESH,
        )
        do_when(cond, copy.start)
        self.sent.append((cond, copy))
        return copy

    def arrived(self, cond, ref, index, dev):
        copy = self.copy(ref, ref, index, dev)
        do_when(cond, copy.wait_recv)

    def left(self, copy):
        for cond, one in self.sent:
            if one is copy:
                do_when(cond, one.wait_send)
        self.sent = [entry for entry in self.sent if entry[1] is not copy]

    def drain(self):
        for cond, copy in self.sent:
            do_when(cond, copy.wait_send)
        self.sent = []


class Gather:
    def __init__(self, links, pos, block, source, sink):
        self.links, self.pos, self.block = links, pos, block
        self.source, self.sink = source, sink
        take = links.sems.take
        self.z_at, self.x_at, self.up_at, self.down_at = take(4), take(4), take(4), take(4)
        self.mine = []

    def along_z(self, cond, s, up, down):
        z, x, c, y = self.pos["z"], self.pos["x"], self.pos["c"], self.pos["y"]
        ref = self.block(s, x)
        for wanted, inside, at, to in (
            (up, z < NZ - 1, self.up_at, z + 1),
            (down, z > 0, self.down_at, z - 1),
        ):
            if wanted:
                self.mine.append(
                    self.links.start(
                        both(cond, inside), ref, ref, at + s, self.z_at + s,
                        self.pos["dev"](to, x, c, y),
                    )
                )

    def forward(self, cond, s, up, down):
        z, x, c, y = self.pos["z"], self.pos["x"], self.pos["c"], self.pos["y"]
        self.along_z(cond, s, up, down)
        ref = self.block(s, x)
        self.mine.append(
            self.links.start(
                cond, ref, ref, self.x_at + s, self.x_at + s, self.pos["dev"](z, 1 - x, c, y)
            )
        )

    def own(self):
        self.forward(self.source, self.pos["z"], True, True)

    def step(self, d):
        z, x = self.pos["z"], self.pos["x"]
        cond = both(self.source, z >= d)
        s = jnp.maximum(z - d, 0)
        self.links.arrived(cond, self.block(s, x), self.z_at + s, self.pos["me"])
        self.forward(cond, s, True, False)
        cond = both(self.source, z <= NZ - 1 - d)
        s = jnp.minimum(z + d, NZ - 1)
        self.links.arrived(cond, self.block(s, x), self.z_at + s, self.pos["me"])
        self.forward(cond, s, False, True)

    def finish(self):
        x = self.pos["x"]
        for s in range(NZ):
            self.links.arrived(self.sink, self.block(s, 1 - x), self.x_at + s, self.pos["me"])


class GatherAcross(Gather):
    def __init__(self, links, pos, block, on_column, not_column):
        super().__init__(links, pos, block, True, True)
        self.on_column, self.not_column = on_column, not_column

    def forward(self, cond, s, up, down):
        self.along_z(cond, s, up, down)

    def across(self):
        z, x, c, y = self.pos["z"], self.pos["x"], self.pos["c"], self.pos["y"]
        ref = self.block(z, x)
        self.mine.append(
            self.links.start(
                self.on_column, ref, ref, self.x_at, self.x_at, self.pos["dev"](z, 1 - x, c, y)
            )
        )

    def own(self):
        z, x = self.pos["z"], self.pos["x"]
        self.links.arrived(self.not_column, self.block(z, x), self.x_at, self.pos["me"])
        self.forward(True, z, True, True)

    def finish(self):
        pass


class Scatter:
    def __init__(self, links, pos, block, sums_x, sums_z, source, sink):
        self.links, self.pos, self.block = links, pos, block
        self.sums_x, self.sums_z = sums_x, sums_z
        self.source, self.sink = source, sink
        take = links.sems.take
        self.x_at, self.z_at, self.up_at, self.down_at = take(4), take(5), take(4), take(4)

    def begin(self):
        z, x, c, y = self.pos["z"], self.pos["x"], self.pos["c"], self.pos["y"]
        for s in (3, 0, 2, 1):
            self.links.start(
                self.source, self.block(s, 1 - x), self.sums_x.at[s], self.x_at + s,
                self.x_at + s, self.pos["dev"](z, 1 - x, c, y),
            )

    def add_x(self, s):
        self.links.arrived(True, self.sums_x.at[s], self.x_at + s, self.pos["me"])
        return self.block(s, self.pos["x"])[...].astype(F32) + self.sums_x[s].astype(F32)

    def hop(self, s, up):
        z, x, c, y = self.pos["z"], self.pos["x"], self.pos["c"], self.pos["y"]
        cond = both(self.sink, (z < s) if up else (z > s))

        def run():
            ref = self.block(s, x)
            ref[...] = self.add_x(s).astype(BF16)
            inner = (z > 0) if up else (z < NZ - 1)

            @pl.when(inner)
            def _():
                self.links.arrived(True, self.sums_z.at[s], self.z_at + s, self.pos["me"])
                ref[...] = (ref[...].astype(F32) + self.sums_z[s].astype(F32)).astype(BF16)

        do_when(cond, run)
        near = (z == s - 1) if up else (z == s + 1)
        slot = s if up else jnp.where(near, 4, s)
        to = self.pos["dev"](z + 1 if up else z - 1, x, c, y)
        at = (self.up_at if up else self.down_at) + s
        self.links.start(
            cond, self.block(s, x), self.sums_z.at[slot], at, self.z_at + slot, to
        )

    def finish(self, store):
        z, x = self.pos["z"], self.pos["x"]
        keep = self.block(z, x)

        def run():
            total = keep[...].astype(F32)
            self.links.arrived(True, self.sums_x.at[z], self.x_at + z, self.pos["me"])
            total = total + self.sums_x[z].astype(F32)
            keep[...] = total.astype(BF16)

            @pl.when(z > 0)
            def _():
                self.links.arrived(True, self.sums_z.at[z], self.z_at + z, self.pos["me"])
                keep[...] = (keep[...].astype(F32) + self.sums_z[z].astype(F32)).astype(BF16)

            @pl.when(z < NZ - 1)
            def _():
                self.links.arrived(True, self.sums_z.at[4], self.z_at + 4, self.pos["me"])
                keep[...] = (keep[...].astype(F32) + self.sums_z[4].astype(F32)).astype(BF16)

            store(keep)

        do_when(self.sink, run)

    def hops(self):
        out = []
        for k in range(3):
            out.append(lambda k=k: self.hop(3 - k, True))
            out.append(lambda k=k: self.hop(k, False))
        return out


class ScatterAcross(Scatter):
    def begin(self):
        pass

    def add_x(self, s):
        return self.block(s, self.pos["x"])[...].astype(F32)

    def finish(self, not_column, on_column):
        z, x, c, y = self.pos["z"], self.pos["x"], self.pos["c"], self.pos["y"]
        keep = self.block(z, x)

        @pl.when(z > 0)
        def _():
            self.links.arrived(True, self.sums_z.at[z], self.z_at + z, self.pos["me"])
            keep[...] = (keep[...].astype(F32) + self.sums_z[z].astype(F32)).astype(BF16)

        @pl.when(z < NZ - 1)
        def _():
            self.links.arrived(True, self.sums_z.at[4], self.z_at + 4, self.pos["me"])
            keep[...] = (keep[...].astype(F32) + self.sums_z[4].astype(F32)).astype(BF16)

        self.links.start(
            not_column, keep, self.sums_x.at[0], self.x_at, self.x_at,
            self.pos["dev"](z, 1 - x, c, y),
        )

    def land(self, on_column, target):
        keep = self.block(self.pos["z"], self.pos["x"])

        @pl.when(on_column)
        def _():
            self.links.arrived(True, self.sums_x.at[0], self.x_at, self.pos["me"])
            target[...] = (keep[...].astype(F32) + self.sums_x[0].astype(F32)).astype(BF16)


class PlaneExchange:
    def __init__(self, links, n_wide, w, y):
        self.links, self.n_wide, self.w, self.y = links, n_wide, w, y
        self.at = links.sems.take(n_wide)

    def begin(self, source, target):
        self.copies = []
        for k in range(1, self.n_wide):
            peer = lax.rem(self.w + k, self.n_wide)
            self.copies.append(
                self.links.start(
                    True, source(peer), target.at[self.w], self.at + k, self.at + k,
                    (peer, self.y),
                )
            )

    def finish(self):
        for copy in self.copies:
            copy.wait_recv()


class GroupGather:
    def __init__(self, links, pos, full):
        self.links, self.pos, self.full = links, pos, full
        self.at = links.sems.take(3)

    def begin(self):
        z, x, c, y = self.pos["z"], self.pos["x"], self.pos["c"], self.pos["y"]
        ref = self.full.at[pl.ds(2 * c, 2), y]
        self.links.start(True, ref, ref, self.at, self.at, self.pos["dev"](z, x, c, 1 - y))
        self.links.start(True, ref, ref, self.at + 1, self.at + 1, self.pos["dev"](z, x, 1 - c, y))

    def relay(self):
        z, x, c, y = self.pos["z"], self.pos["x"], self.pos["c"], self.pos["y"]
        ref = self.full.at[pl.ds(2 * c, 2), 1 - y]
        self.links.arrived(True, ref, self.at, self.pos["me"])
        self.links.start(True, ref, ref, self.at + 2, self.at + 2, self.pos["dev"](z, x, 1 - c, y))

    def finish(self):
        c, y = self.pos["c"], self.pos["y"]
        other = pl.ds(2 * (1 - c), 2)
        self.links.arrived(True, self.full.at[other, y], self.at + 1, self.pos["me"])
        self.links.arrived(True, self.full.at[other, 1 - y], self.at + 2, self.pos["me"])


class GroupSum:
    def __init__(self, links, pos, full, from_core, to_pair, from_pair):
        self.links, self.pos, self.full = links, pos, full
        self.from_core, self.to_pair, self.from_pair = from_core, to_pair, from_pair
        self.at = links.sems.take(2)

    def begin(self):
        z, x, c, y = self.pos["z"], self.pos["x"], self.pos["c"], self.pos["y"]
        self.core_copy = self.links.start(
            True, self.full.at[pl.ds(2 * (1 - c), 2)], self.from_core, self.at, self.at,
            self.pos["dev"](z, x, 1 - c, y),
        )

    def relay(self):
        z, x, c, y = self.pos["z"], self.pos["x"], self.pos["c"], self.pos["y"]
        self.links.arrived(True, self.from_core, self.at, self.pos["me"])
        for s in range(2):
            self.to_pair[s] = (
                self.full[2 * c + s, 1 - y].astype(F32) + self.from_core[s, 1 - y].astype(F32)
            ).astype(BF16)
        self.pair_copy = self.links.start(
            True, self.to_pair, self.from_pair, self.at + 1, self.at + 1,
            self.pos["dev"](z, x, c, 1 - y),
        )

    def arrived(self):
        self.links.arrived(True, self.from_pair, self.at + 1, self.pos["me"])

    def total(self, s):
        c, y = self.pos["c"], self.pos["y"]
        return (
            self.full[2 * c + s, y].astype(F32)
            + self.from_core[s, y].astype(F32)
            + self.from_pair[s].astype(F32)
        )


def gelu_both(u):
    inner = GELU_C * (u + 0.044715 * u * u * u)
    tan = jnp.tanh(inner)
    slope = GELU_C * (1.0 + 3.0 * 0.044715 * u * u)
    act = 0.5 * u * (1.0 + tan)
    grad = 0.5 * (1.0 + tan) + 0.5 * u * (1.0 - tan * tan) * slope
    return act, grad


def block_kernel(
    order, n_wide,
    tok_ref, cot_ref, parcel_ref, wada_ref, bada_ref,
    wqkv_ref, wfc1_ref, src_fc2, src_proj,
    out_ref, gtok_ref, got_ref, dmall_ref, vout_ref, dsil_ref,
    p_qkv, p_fc1, j_fc2, j_proj,
    g_qkv, g_proj, g_fc1, g_fc2, w_fc2,
    i_qkv, i_fc1, i_fc2, own_qkv, own_fc1, own_fc2, o_qkv, o_fc1,
    x_qkv, x_proj, x_fc1, x_fc2, z_qkv, z_proj, z_fc1, z_fc2,
    t_qkv, t_fc1, t_fc2, t_proj, j_qkv, j_fc1,
    a_all, m_all, d_all, qkv_all, att_all, act_all, gp_all,
    sum_a, sum_b, core_a, core_b, to_a, to_b, from_a, from_b,
    attn_own, mid_own, dmid_own,
    left, part, parts, tot, modh, mods, bqkv, brow, bias,
    dmod, dm_pair, dm_low, dm_all, v_send, v_all, dm_rows, ds_send,
    send, recv, local,
):
    w, y = lax.axis_index("wide"), lax.axis_index("narrow")
    z, x, c = w // 4, (w // 2) % 2, w % 2
    chip = 2 * z + x
    quarter = 2 * y + c

    def dev(z, x, c, y):
        return ((z * 2 + x) * 2 + c, y)

    sib, pair = dev(z, x, 1 - c, y), dev(z, x, c, 1 - y)
    pos = {"z": z, "x": x, "c": c, "y": y, "dev": dev, "me": sib}
    links = Links(Sems(send, recv))
    sems = links.sems
    half_len = tok_ref.shape[1]
    width = tok_ref.shape[2]
    hd = HEAD_DIM
    hq = g_proj.shape[0]
    hw = hd * hq
    shard = own_qkv.shape[0]
    rows2 = 2 * shard
    rows = 2 * half_len
    all_rows = 4 * rows
    half = modh.shape[2]
    head_scale = 1.0 / math.sqrt(HEAD_DIM)
    da_all = act_all

    greet(
        [(True, (lax.rem(w + k, n_wide), y)) for k in range(1, n_wide)]
        + [(True, pair), (True, dev(z, x, 1 - c, 1 - y))]
    )

    def rows_of(full):
        return lambda s, xx: full.at[pl.ds(pl.multiple_of((2 * s + xx) * rows2, 16), rows2), :]

    def head_of(s, xx):
        return g_proj.at[s]

    on_column = x == y
    not_column = jnp.logical_not(on_column)
    init = sems.take(3)
    ga_qkv = Gather(links, pos, rows_of(g_qkv), True, True)
    ga_proj = GatherAcross(links, pos, head_of, on_column, not_column)
    ga_fc1 = Gather(links, pos, rows_of(g_fc1), True, True)
    ga_fc2 = Gather(links, pos, rows_of(g_fc2), True, True)
    gg_a = GroupGather(links, pos, a_all)
    gg_d = GroupGather(links, pos, d_all)
    gg_m = GroupGather(links, pos, m_all)
    gg_da = GroupGather(links, pos, da_all)
    gs_attn = GroupSum(links, pos, sum_a, core_a, to_a, from_a)
    gs_mlp = GroupSum(links, pos, sum_b, core_b, to_b, from_b)
    gs_dm = GroupSum(links, pos, sum_a, core_a, to_a, from_a)
    gs_da = GroupSum(links, pos, sum_b, core_b, to_b, from_b)
    sc_fc2 = Scatter(links, pos, rows_of(w_fc2), x_fc2, z_fc2, True, True)
    sc_fc1 = Scatter(links, pos, rows_of(g_fc2), x_fc1, z_fc1, True, True)
    sc_qkv = Scatter(links, pos, rows_of(g_qkv), x_qkv, z_qkv, True, True)
    sc_proj = ScatterAcross(links, pos, head_of, x_proj, z_proj, True, True)
    ex_head = PlaneExchange(links, n_wide, w, y)
    ex_mod = PlaneExchange(links, n_wide, w, y)
    ex_dm = PlaneExchange(links, n_wide, w, y)
    ex_v = PlaneExchange(links, n_wide, w, y)
    ex_ds = PlaneExchange(links, n_wide, w, y)
    swap_mod, swap_dm, swap_v, swap_proj = sems.take(1), sems.take(1), sems.take(1), sems.take(1)
    steps = {}

    def step(fn):
        steps[fn.__name__] = fn
        return fn

    def norm(value):
        center = value - jnp.mean(value, axis=-1, keepdims=True)
        inv = lax.rsqrt(jnp.mean(center * center, axis=-1, keepdims=True) + eps_norm)
        return center * inv, inv

    def norm_grad(grad, normed, inv):
        return inv * (
            grad
            - jnp.mean(grad, axis=-1, keepdims=True)
            - normed * jnp.mean(grad * normed, axis=-1, keepdims=True)
        )

    def mod(k, s):
        return mods[k, s : s + 1, :]

    def pick(source, count, which):
        return jnp.concatenate(
            [source[:, (4 * j + which) * hd : (4 * j + which + 1) * hd] for j in range(count)],
            axis=1,
        )

    fc2_copy = pltpu.make_async_copy(src_fc2.at[quarter], own_fc2, local.at[0])
    proj_copy = pltpu.make_async_copy(src_proj, g_proj.at[z], local.at[1])

    @step
    def init0():
        fc2_copy.start()
        do_when(on_column, proj_copy.start)
        ex_head.begin(lambda p: parcel_ref.at[p], got_ref)
        got_ref[w] = parcel_ref[w]
        value = wqkv_ref[...]
        for q in range(4):

            @pl.when(quarter == q)
            def _():
                own_qkv[...] = pick(value, 3 * hq, q)

            @pl.when(2 * y + 1 - c == q)
            def _():
                o_qkv[...] = pick(value, 3 * hq, q)

        links.start(True, o_qkv, i_qkv, init, init, sib)

    @step
    def init1():
        links.start(True, src_fc2.at[2 * y + 1 - c], i_fc2, init + 2, init + 2, sib)
        value = wfc1_ref[...]
        for q in range(4):

            @pl.when(quarter == q)
            def _():
                own_fc1[...] = pick(value, n_wide, q)

            @pl.when(2 * y + 1 - c == q)
            def _():
                o_fc1[...] = pick(value, n_wide, q)

        links.start(True, o_fc1, i_fc1, init + 1, init + 1, sib)

    def place(own, inbox, full, index):
        links.arrived(True, inbox, init + index, sib)
        mine, other = own[...].astype(F32), inbox[...].astype(F32)
        first = jnp.where(c == 0, mine, other)
        second = jnp.where(c == 0, other, mine)
        at = pl.ds(pl.multiple_of(chip * rows2, 16), rows2)
        full[at, :] = jnp.concatenate([first, second], axis=0).astype(BF16)

    @step
    def q0():
        place(own_qkv, i_qkv, g_qkv, 0)
        ga_qkv.own()

    @step
    def f0():
        place(own_fc1, i_fc1, g_fc1, 1)
        ga_fc1.own()

    @step
    def e0():
        fc2_copy.wait()
        place(own_fc2, i_fc2, g_fc2, 2)
        ga_fc2.own()

    @step
    def px():
        do_when(on_column, proj_copy.wait)
        ga_proj.across()

    steps["p0"] = ga_proj.own
    for letter, gather in (("q", ga_qkv), ("p", ga_proj), ("f", ga_fc1), ("e", ga_fc2)):
        for d in range(1, NZ):
            steps[letter + str(d)] = lambda gather=gather, d=d: gather.step(d)

    @step
    def h1():
        ex_head.finish()
        for s in range(n_wide):
            left[2 * s : 2 * s + 2, :] = got_ref[s, 0:2, 0:128]
        lhs = left[...][:, :shard].astype(BF16)
        cols = pl.ds(pl.multiple_of(y * half, 128), half)
        res = dot_nn(lhs, wada_ref[:, cols]) + bada_ref[:, cols]
        for s in range(n_wide):
            part[s] = res[2 * s : 2 * s + 2, :]
        parts[w] = part[w]
        ex_mod.begin(lambda p: part.at[p], parts)

    @step
    def hb():
        def row(lane, owners):
            return jnp.concatenate([got_ref[o, 2:3, lane : lane + hd] for o in owners], axis=1)

        every = range(n_wide)
        brow[0:1, :] = row(0, every)
        brow[1:2, :] = row(128, every)
        brow[2:3, :] = row(256, every)
        bqkv[...] = jnp.concatenate(
            [
                row(384, [2 * j + y for j in range(hq)]),
                jnp.zeros((1, hw), F32),
                row(384, [n_wide // 2 + 2 * j + y for j in range(hq)]),
            ],
            axis=1,
        )

    @step
    def h2():
        ex_mod.finish()
        total = parts[0]
        for s in range(1, n_wide):
            total = total + parts[s]
        tot[...] = total
        modh[y] = total
        links.start(True, tot, modh.at[y], swap_mod, swap_mod, pair)

    @step
    def h3():
        links.arrived(True, modh.at[1 - y], swap_mod, sib)
        for k in range(6):
            at = (k % 3) * width
            mods[k] = modh[k // 3, :, at : at + width]

    @step
    def ln1():
        for s in range(2):
            normed, inv = norm(tok_ref[s].astype(F32))
            a_all[2 * c + s, y] = (normed * (1.0 + mod(1, s)) + mod(0, s)).astype(BF16)
        gg_a.begin()

    steps["ar"], steps["af"] = gg_a.relay, gg_a.finish

    @step
    def d0():
        for s in range(2):
            d_all[2 * c + s, y] = (mod(5, s) * cot_ref[s].astype(F32)).astype(BF16)
        gg_d.begin()

    steps["dr"], steps["df"] = gg_d.relay, gg_d.finish

    @step
    def qkv():
        ga_qkv.finish()

        @pl.loop(0, 4)
        def _(i):
            res = dot_nn(a_all[i].reshape(rows, width), g_qkv[...]) + bqkv[...]
            qkv_all[i] = res.astype(BF16)

    def head_parts(packed, h):
        return [packed[:, t * hw + h * hd : t * hw + (h + 1) * hd] for t in range(3)]

    def softmax(q, k):
        scores = dot_nt(q, k) * head_scale
        top = jnp.max(scores, axis=-1, keepdims=True)
        e = jnp.exp(scores - top)
        return e * (1.0 / jnp.sum(e, axis=-1, keepdims=True))

    @step
    def att():
        @pl.loop(0, 4)
        def _(i):
            packed = qkv_all[i]
            acc = None
            for h in range(hq):
                q, k, v = head_parts(packed, h)
                p = softmax(q, k).astype(BF16)
                o = dot_nn(p, v).astype(BF16)
                att_all[h, i] = o
                term = dot_nn(o, g_proj[h])
                acc = term if acc is None else acc + term
            sum_a[i] = acc.astype(BF16).reshape(2, half_len, width)

        gs_attn.begin()

    steps["sr"] = gs_attn.relay

    @step
    def ln2():
        gs_attn.arrived()
        for s in range(2):
            attn = gs_attn.total(s) + brow[1:2, :]
            attn_own[s] = attn
            mid = tok_ref[s].astype(F32) + mod(2, s) * attn
            mid_own[s] = mid
            normed, inv = norm(mid)
            m_all[2 * c + s, y] = (normed * (1.0 + mod(4, s)) + mod(3, s)).astype(BF16)
        gg_m.begin()

    steps["mr"], steps["mf"] = gg_m.relay, gg_m.finish

    @step
    def fc1():
        ga_fc1.finish()

        @pl.loop(0, 4)
        def _(i):
            u = dot_nn(m_all[i].reshape(rows, width), g_fc1[...]) + brow[0:1, :]
            act, grad = gelu_both(u)
            act_all[i] = act.astype(BF16).reshape(2, half_len, width)
            gp_all[i] = grad.astype(BF16)

    steps["ef"] = ga_fc2.finish

    @step
    def fc2():
        @pl.loop(0, 4)
        def _(i):
            res = dot_nn(act_all[i].reshape(rows, width), g_fc2[...])
            sum_b[i] = res.astype(BF16).reshape(2, half_len, width)

        gs_mlp.begin()

    steps["ur"] = gs_mlp.relay

    def outer(left, right, full):
        lanes = width // 3

        @pl.loop(0, 3)
        def _(j):
            at = pl.ds(pl.multiple_of(j * lanes, 128), lanes)
            full[at, :] = dot_tn(left(at).reshape(all_rows, lanes), right()).astype(BF16)

    @step
    def w2():
        outer(
            lambda at: act_all[:, :, :, at], lambda: d_all[...].reshape(all_rows, width), w_fc2
        )
        sc_fc2.begin()

    @step
    def dh():
        bias[...] = jnp.zeros_like(bias)

        @pl.loop(0, 4)
        def _(i):
            d_act = dot_nt(d_all[i].reshape(rows, width), g_fc2[...])
            d_hidden = (d_act * gp_all[i].astype(F32)).astype(BF16)
            gp_all[i] = d_hidden
            bias[0:1, :] += jnp.sum(d_hidden.astype(F32), axis=0, keepdims=True)

    @step
    def dm():
        links.left(gs_attn.core_copy)

        @pl.loop(0, 4)
        def _(i):
            res = dot_nt(gp_all[i], g_fc1[...])
            sum_a[i] = res.astype(BF16).reshape(2, half_len, width)

        gs_dm.begin()

    @step
    def w1():
        for copy in ga_fc2.mine:
            links.left(copy)
        outer(
            lambda at: m_all[:, :, :, at], lambda: gp_all[...].reshape(all_rows, width), g_fc2
        )
        sc_fc1.begin()

    @step
    def tr():
        links.left(gs_attn.pair_copy)
        gs_dm.relay()

    @step
    def res():
        gs_mlp.arrived()
        for s in range(2):
            mlp = gs_mlp.total(s) + brow[2:3, :]
            out_ref[s] = (mid_own[s] + mod(5, s) * mlp).astype(BF16)
            grad_out = cot_ref[s].astype(F32)
            dmod[5, s : s + 1, :] = jnp.sum(grad_out * mlp, axis=0, keepdims=True)
            bias[2:3, :] += jnp.sum(d_all[2 * c + s, y].astype(F32), axis=0, keepdims=True)

    @step
    def ln2b():
        gs_dm.arrived()
        for s in range(2):
            d_m = gs_dm.total(s)
            normed, inv = norm(mid_own[s])
            dmod[4, s : s + 1, :] = jnp.sum(d_m * normed, axis=0, keepdims=True)
            dmod[3, s : s + 1, :] = jnp.sum(d_m, axis=0, keepdims=True)
            d_mid = cot_ref[s].astype(F32) + norm_grad(d_m * (1.0 + mod(4, s)), normed, inv)
            dmid_own[s] = d_mid
            d_attn = (mod(2, s) * d_mid).astype(BF16)
            da_all[2 * c + s, y] = d_attn
            dmod[2, s : s + 1, :] = jnp.sum(d_mid * attn_own[s], axis=0, keepdims=True)
            bias[1:2, :] += jnp.sum(d_attn.astype(F32), axis=0, keepdims=True)
        gg_da.begin()

    steps["gr"], steps["gf"] = gg_da.relay, gg_da.finish

    @step
    def attb():
        @pl.loop(0, 4)
        def _(i):
            packed = qkv_all[i]
            d_attn = da_all[i].reshape(rows, width)
            grads = [[], [], []]
            for h in range(hq):
                q, k, v = head_parts(packed, h)
                p = softmax(q, k)
                p_low = p.astype(BF16)
                d_att = dot_nt(d_attn, g_proj[h]).astype(BF16)
                d_p = dot_nt(d_att, v)
                d_s = (p * (d_p - jnp.sum(p * d_p, axis=-1, keepdims=True))).astype(BF16)
                grads[0].append(dot_nn(d_s, k) * head_scale)
                grads[1].append(dot_tn(d_s, q) * head_scale)
                grads[2].append(dot_tn(p_low, d_att))
            d_qkv = jnp.concatenate(grads[0] + grads[1] + grads[2], axis=1).astype(BF16)
            qkv_all[i] = d_qkv
            bias[3:4, 0 : 3 * hw] += jnp.sum(d_qkv.astype(F32), axis=0, keepdims=True)

    @step
    def dam():
        links.left(gs_mlp.core_copy)

        @pl.loop(0, 4)
        def _(i):
            res = dot_nt(qkv_all[i], g_qkv[...])
            sum_b[i] = res.astype(BF16).reshape(2, half_len, width)

        gs_da.begin()

    @step
    def wq():
        for copy in ga_qkv.mine:
            links.left(copy)
        outer(
            lambda at: a_all[:, :, :, at], lambda: qkv_all[...].reshape(all_rows, 3 * hw), g_qkv
        )
        sc_qkv.begin()

    @step
    def xr():
        links.left(gs_mlp.pair_copy)
        gs_da.relay()

    @step
    def wp():
        for copy in ga_proj.mine:
            links.left(copy)

        @pl.loop(0, hq)
        def _(h):
            value = att_all[h].reshape(all_rows, hd)
            g_proj[h] = dot_tn(value, da_all[...].reshape(all_rows, width)).astype(BF16)

    for letter, scatter in (("E", sc_fc2), ("F", sc_fc1), ("Q", sc_qkv), ("P", sc_proj)):
        for k, fn in enumerate(scatter.hops()):
            steps[letter + str(k)] = fn

    def join(scatter, pack, target, index):
        at = sems.take(3)
        keep_copy = pltpu.make_async_copy(pack.at[c], target.at[quarter], local.at[index])

        def begin():
            def store(keep):
                total = keep[...].astype(F32)
                pack[0] = total[:shard].astype(BF16)
                pack[1] = total[shard:].astype(BF16)

            scatter.finish(store)
            links.start(True, pack.at[1 - c], target.at[quarter], at, at, sib)
            links.start(True, pack.at[c], target.at[quarter], at + 1, at + 1, pair)
            links.start(
                True, pack.at[1 - c], target.at[quarter], at + 2, at + 2, dev(z, x, 1 - c, 1 - y)
            )
            keep_copy.start()

        def finish():
            keep_copy.wait()
            links.arrived(True, target.at[2 * y + 1 - c], at, sib)
            links.arrived(True, target.at[2 * (1 - y) + c], at + 1, sib)
            links.arrived(True, target.at[2 * (1 - y) + 1 - c], at + 2, sib)

        return begin, finish

    def spread(source, target, count):
        target[...] = jnp.concatenate(
            [source[k % 4, :, (k // 4) * hd : (k // 4 + 1) * hd] for k in range(4 * count)],
            axis=1,
        )

    steps["EJ"], steps["EG"] = join(sc_fc2, t_fc2, j_fc2, 2)
    steps["FJ"], fc1_joined = join(sc_fc1, t_fc1, j_fc1, 3)
    steps["QJ"], qkv_joined = join(sc_qkv, t_qkv, j_qkv, 4)

    @step
    def FG():
        fc1_joined()
        spread(j_fc1, p_fc1, n_wide)

    @step
    def QG():
        qkv_joined()
        spread(j_qkv, p_qkv, 3 * hq)

    steps["PJ"] = lambda: sc_proj.finish(not_column, on_column)

    @step
    def PK():
        sc_proj.land(on_column, t_proj)
        links.start(on_column, t_proj, t_proj, swap_proj, swap_proj, pair)

    @step
    def PG():
        links.arrived(not_column, t_proj, swap_proj, sib)
        j_proj[...] = t_proj[...]

    @step
    def ln1b():
        gs_da.arrived()
        for s in range(2):
            d_a = gs_da.total(s)
            normed, inv = norm(tok_ref[s].astype(F32))
            dmod[1, s : s + 1, :] = jnp.sum(d_a * normed, axis=0, keepdims=True)
            dmod[0, s : s + 1, :] = jnp.sum(d_a, axis=0, keepdims=True)
            gtok_ref[s] = dmid_own[s] + norm_grad(d_a * (1.0 + mod(1, s)), normed, inv)
        links.start(True, dmod, dm_pair, swap_dm, swap_dm, pair)

    @step
    def t1():
        links.arrived(True, dm_pair, swap_dm, sib)
        for k in range(6):
            dm_low[:, k * width : (k + 1) * width] = (dmod[k] + dm_pair[k]).astype(BF16)
        dm_all[w] = dm_low[...]
        ex_dm.begin(lambda p: dm_low, dm_all)

    @step
    def t2():
        ex_dm.finish()
        res = None
        for k in range(6):
            at = slice(k * width, (k + 1) * width)
            for s in range(n_wide):
                dm_rows[2 * s : 2 * s + 2, :] = dm_all[s, :, at].astype(F32)
            low = dm_rows[...].astype(BF16)
            dmall_ref[:, at] = low
            term = dot_nt(low, wada_ref[:, at])
            res = term if res is None else res + term
        ds_send[...] = jnp.zeros_like(ds_send)
        for s in range(n_wide):
            ds_send[s, :, 0:shard] = res[2 * s : 2 * s + 2, :]
        dsil_ref[w] = ds_send[w]
        ex_ds.begin(lambda p: ds_send.at[p], dsil_ref)

    steps["t3"] = ex_ds.finish

    @step
    def v1():
        v_send[...] = jnp.zeros_like(v_send)
        for s in range(n_wide):
            at = slice(s * hd, (s + 1) * hd)
            v_send[s, pl.ds(c, 1), 0:hd] = bias[0:1, at]
            v_send[s, 2:4, 0:hd] = bias[1:3, at]
        for j in range(hq):
            v_send[2 * j + y, pl.ds(4 + c, 1), 0:hd] = bias[3:4, j * hd : (j + 1) * hd]
            v_send[n_wide // 2 + 2 * j + y, pl.ds(4 + c, 1), 0:hd] = bias[
                3:4, 2 * hw + j * hd : 2 * hw + (j + 1) * hd
            ]
        v_all[w] = v_send[w]
        ex_v.begin(lambda p: v_send.at[p], v_all)

    @step
    def v2():
        ex_v.finish()
        total = v_all[0]
        for s in range(1, n_wide):
            total = total + v_all[s]
        vout_ref[y] = total
        links.start(True, vout_ref.at[y], vout_ref.at[y], swap_v, swap_v, pair)

    steps["v3"] = lambda: links.arrived(True, vout_ref.at[1 - y], swap_v, sib)
    steps["end"] = links.drain

    for name in order:
        steps[name]()


ORDER = (
    "init0", "px", "q0", "h1", "hb", "p0", "q1", "h2", "h3", "ln1", "q2", "p1", "q3",
    "init1", "p2", "ar", "f0", "d0", "af", "qkv", "e0", "p3", "att", "f1", "sr", "dr", "e1",
    "f2", "e2", "ln2", "f3", "e3", "mr", "mf", "df", "fc1", "ef", "fc2", "w2", "ur", "dh",
    "dm", "w1", "tr", "E0", "res", "ln2b", "F0", "gr", "E1", "E2", "gf", "attb", "F1", "F2",
    "E3", "dam", "wq", "v1", "F3", "E4", "F4", "xr", "F5", "Q0", "FJ", "wp", "P0", "P1",
    "P2", "E5", "v2", "EJ", "Q1", "Q2", "P3", "P4", "Q3", "P5", "PJ", "ln1b", "t1", "PK",
    "Q4", "EG", "Q5", "QJ", "FG", "PG", "v3", "t2", "t3", "QG", "end",
)


def fast_device(
    tokens,
    cond,
    timesteps,
    counts,
    w_ada,
    b_ada,
    w_qkv,
    b_qv,
    w_proj,
    b_proj,
    w_fc1,
    b_fc1,
    w_fc2,
    b_fc2,
    cotangent,
):
    slots, half_len, width = tokens.shape
    n_wide = lax.axis_size("wide")
    w, y = lax.axis_index("wide"), lax.axis_index("narrow")
    shard = w_ada.shape[0]
    mlp = w_fc1.shape[1]
    hq = HEADS // 4
    nq = 3 * hq * HEAD_DIM
    rows = slots * half_len
    mq = mlp // 4
    half = w_ada.shape[1] // 2

    cond_vec = cond.astype(F32) + time_features(timesteps, width)
    cond_sig = jax.nn.sigmoid(cond_vec)
    silu = (cond_vec * cond_sig).astype(BF16).astype(F32)
    chunks = jnp.pad(
        silu.reshape(slots, n_wide, shard).transpose(1, 0, 2), ((0, 0), (0, 0), (0, 640 - shard))
    )

    def tile(piece):
        return jnp.pad(piece.astype(F32), ((0, 0), (0, 128 - piece.shape[1])))

    fc1_pieces = lax.dynamic_slice_in_dim(b_fc1.reshape(4, shard), 2 * y, 2, 0)
    vector = jnp.concatenate(
        [
            tile(fc1_pieces),
            tile(jnp.broadcast_to(b_proj, (2, shard))),
            tile(jnp.broadcast_to(b_fc2, (2, shard))),
            tile(b_qv.reshape(2, shard)),
            jnp.zeros((2, 128), F32),
        ],
        axis=1,
    )
    vector = jnp.broadcast_to(vector[None], (n_wide // 2, 2, 640)).reshape(n_wide, 1, 640)
    parcel = jnp.concatenate([chunks, vector, jnp.zeros_like(vector)], axis=1)
    ada_cut = b_ada.shape[0]
    ada_bias = lax.dynamic_update_slice_in_dim(
        jnp.zeros((1, w_ada.shape[1]), F32), b_ada.astype(F32)[None], w * ada_cut, 1
    )
    live = (jnp.arange(slots, dtype=jnp.int32) < counts[0])[:, None, None]
    cot_live = jnp.where(live, cotangent, jnp.zeros_like(cotangent))

    def v16(*shape):
        return pltpu.VMEM(shape, BF16)

    def v32(*shape):
        return pltpu.VMEM(shape, F32)

    two = 2 * shard
    full = (4, 2, half_len, width)
    own = (slots, half_len, width)
    scratch = [
        v16(width, nq), v16(hq, shard, width), v16(width, mq), v16(mq, width), v16(mq, width),
        v16(shard, nq), v16(shard, mq), v16(shard, width),
        v16(shard, nq), v16(shard, mq), v16(shard, width), v16(shard, nq), v16(shard, mq),
        v16(4, two, nq), v16(1, shard, width), v16(4, two, mq), v16(4, two, width),
        v16(5, two, nq), v16(5, shard, width), v16(5, two, mq), v16(5, two, width),
        v16(2, shard, nq), v16(2, shard, mq), v16(2, shard, width), v16(shard, width),
        v16(4, shard, nq), v16(4, shard, mq),
        v16(*full), v16(*full), v16(*full),
        v16(4, rows, nq), v16(hq, 4, rows, HEAD_DIM), v16(*full), v16(4, rows, mq),
        v16(*full), v16(*full),
        v16(2, 2, half_len, width), v16(2, 2, half_len, width),
        v16(*own), v16(*own), v16(*own), v16(*own),
        v32(*own), v32(*own), v32(*own),
        v32(n_wide * slots, 128), v32(n_wide, slots, half), v32(n_wide, slots, half),
        v32(slots, half), v32(2, slots, half), v32(6, slots, width), v32(1, nq), v32(4, width),
        v32(4, width),
        v32(6, slots, width), v32(6, slots, width), v16(slots, 6 * width),
        v16(n_wide, slots, 6 * width), v32(n_wide, 8, 128), v32(n_wide, 8, 128),
        v32(n_wide * slots, width), v32(n_wide, slots, 128),
        pltpu.SemaphoreType.DMA((300,)),
        pltpu.SemaphoreType.DMA((300,)),
        pltpu.SemaphoreType.DMA((5,)),
    ]
    out, gtok, got, dm_all, v_out, d_silu, p_qkv, p_fc1, j_fc2, j_proj = pl.pallas_call(
        functools.partial(block_kernel, ORDER, n_wide),
        out_shape=(
            jax.ShapeDtypeStruct(own, BF16),
            jax.ShapeDtypeStruct(own, F32),
            jax.ShapeDtypeStruct((n_wide, 4, 640), F32),
            jax.ShapeDtypeStruct((n_wide * slots, 6 * width), BF16),
            jax.ShapeDtypeStruct((2, 8, 128), F32),
            jax.ShapeDtypeStruct((n_wide, slots, 128), F32),
            jax.ShapeDtypeStruct(w_qkv.shape, BF16),
            jax.ShapeDtypeStruct(w_fc1.shape, BF16),
            jax.ShapeDtypeStruct((4, shard, width), BF16),
            jax.ShapeDtypeStruct((shard, width), BF16),
        ),
        in_specs=[VMEM_SPEC] * 7 + [HBM_SPEC] * 2,
        out_specs=(VMEM_SPEC,) * 8 + (HBM_SPEC, VMEM_SPEC),
        scratch_shapes=scratch,
        compiler_params=pltpu.CompilerParams(
            collective_id=0, has_side_effects=True, vmem_limit_bytes=VMEM_LIMIT
        ),
    )(
        tokens, cot_live, parcel, w_ada, ada_bias, w_qkv, w_fc1,
        w_fc2.reshape(4, shard, width), w_proj,
    )
    out = jnp.where(live, out, jnp.zeros_like(out))
    silu_cols = got[:, 0:2, :shard].reshape(n_wide * slots, shard).astype(BF16)
    grad_ada = outer_sum(silu_cols, dm_all)
    grad_b_ada = jnp.sum(
        lax.dynamic_slice_in_dim(dm_all, w * ada_cut, ada_cut, 1).astype(F32), axis=0
    )
    d_silu = d_silu[:, :, :shard].transpose(1, 0, 2).reshape(slots, width)
    grad_cond = d_silu * (cond_sig + cond_vec * cond_sig * (1.0 - cond_sig))
    v_sum = (v_out[0] + v_out[1])[:, :shard]
    return (
        out,
        gtok,
        grad_cond,
        grad_ada,
        grad_b_ada,
        p_qkv.astype(F32),
        v_sum[4:6].reshape(-1),
        j_proj.astype(F32),
        v_sum[2],
        p_fc1.astype(F32),
        v_out[:, 0:2, :shard].reshape(-1),
        j_fc2.astype(F32).reshape(w_fc2.shape),
        v_sum[3],
    )


def solution(mesh):
    in_specs = (
        P("wide", "narrow", None),
        P("wide", None),
        P("wide"),
        P("wide"),
        P("wide", None),
        P("wide"),
        P("wide", None),
        P("wide"),
        P("wide", None),
        P("wide"),
        P("wide", None),
        P("wide"),
        P("wide", None),
        P("wide"),
        P("wide", "narrow", None),
    )
    out_specs = (
        P("wide", "narrow", None),
        P("wide", "narrow", None),
        P("wide", None),
        P("wide", None),
        P("wide"),
        P("wide", None),
        P("wide"),
        P("wide", None),
        P("wide"),
        P("wide", None),
        P("wide"),
        P("wide", None),
        P("wide"),
    )
    small = mesh.shape["wide"] == 16 and mesh.shape["narrow"] == 2
    per_device = fast_device if small else on_device
    return jax.shard_map(
        per_device, mesh=mesh, in_specs=in_specs, out_specs=out_specs, check_vma=False
    )
```

```python
import functools
import math

import jax
import jax.numpy as jnp
from jax import lax
from jax.experimental import pallas as pl
from jax.experimental.pallas import tpu as pltpu
from jax.sharding import PartitionSpec as P

HEADS = 16
HEAD_DIM = 72

F32 = jnp.float32
BF16 = jnp.bfloat16
eps_norm = 1e-06


def norm_rows(value):
    center = value - jnp.mean(value, axis=-1, keepdims=True)
    inv_std = lax.rsqrt(jnp.mean(center * center, axis=-1, keepdims=True) + eps_norm)
    return (center * inv_std, inv_std)


def norm_back(grad, normed, inv_std):
    return inv_std * (
        grad
        - jnp.mean(grad, axis=-1, keepdims=True)
        - normed * jnp.mean(grad * normed, axis=-1, keepdims=True)
    )


def gelu_tanh(value):
    return (
        0.5
        * value
        * (1.0 + jnp.tanh(0.7978845608028654 * (value + 0.044715 * value * value * value)))
    )


def gelu_tanh_grad(value):
    inner = 0.7978845608028654 * (value + 0.044715 * value * value * value)
    tan = jnp.tanh(inner)
    slope = 0.7978845608028654 * (1.0 + 3.0 * 0.044715 * value * value)
    return 0.5 * (1.0 + tan) + 0.5 * value * (1.0 - tan * tan) * slope


def time_features(steps, width):
    half_width = width // 2
    freqs = jnp.exp(-math.log(10000.0) * jnp.arange(half_width).astype(F32) / half_width)
    angles = steps.astype(F32)[:, None] * freqs[None, :]
    return jnp.concatenate([jnp.cos(angles), jnp.sin(angles)], axis=-1)


def mm(left, right):
    return jnp.einsum("sk,kn->sn", left, right, preferred_element_type=F32)


def mm_back(grad, weight):
    return jnp.einsum("sn,kn->sk", grad, weight, preferred_element_type=F32)


def outer_sum(left, right):
    return jnp.einsum("sk,sn->kn", left, right, preferred_element_type=F32)


def gather_wide(value, axis=0):
    return lax.all_gather(value, "wide", axis=axis, tiled=True)


def on_device(
    tokens,
    cond,
    timesteps,
    counts,
    w_ada,
    b_ada,
    w_qkv,
    b_qv,
    w_proj,
    b_proj,
    w_fc1,
    b_fc1,
    w_fc2,
    b_fc2,
    cotangent,
):
    slots, half_len, width = tokens.shape
    pair = lax.axis_size("narrow")
    n_wide = lax.axis_size("wide")
    me = lax.axis_index("narrow")
    here = lax.axis_index("wide")
    seq = half_len * pair
    rows = slots * half_len
    all_rows = slots * seq
    wh = width // pair
    heads = HEADS // pair
    mlp = w_fc1.shape[1]
    mh = mlp // pair
    shard = w_ada.shape[0]
    head_scale = 1.0 / math.sqrt(HEAD_DIM)

    qkv_half = lax.dynamic_index_in_dim(
        w_qkv.reshape(-1, 3, pair, wh), me, 2, keepdims=False
    ).reshape(-1, 3 * wh)
    fc1_half = lax.dynamic_index_in_dim(
        w_fc1.reshape(-1, n_wide, pair, mh // n_wide), me, 2, keepdims=False
    ).reshape(-1, mh)
    fc2_half = lax.dynamic_index_in_dim(
        w_fc2.reshape(pair, -1, width), me, 0, keepdims=False
    )

    cond_vec = cond.astype(F32) + time_features(timesteps, width)
    cond_sig = jax.nn.sigmoid(cond_vec)
    silu_low = (cond_vec * cond_sig).astype(BF16)
    silu_all = gather_wide(silu_low)
    silu_cols = lax.dynamic_slice_in_dim(silu_all, here * shard, shard, 1)
    mod_part = jnp.dot(silu_cols, w_ada, preferred_element_type=F32)
    biases = gather_wide(jnp.concatenate([b_ada, b_qv, b_proj, b_fc1, b_fc2])[None])
    cuts = []
    at = 0
    for piece in (b_ada, b_qv, b_proj, b_fc1, b_fc2):
        cuts.append(biases[:, at : at + piece.shape[0]].astype(F32))
        at += piece.shape[0]
    ada_bias, qv_bias, proj_bias, fc1_bias, fc2_bias = [c.reshape(-1) for c in cuts]
    fc1_bias_half = lax.dynamic_index_in_dim(
        fc1_bias.reshape(n_wide, pair, -1), me, 1, keepdims=False
    ).reshape(-1)
    qv_bias_half = lax.dynamic_index_in_dim(qv_bias.reshape(2, pair, wh), me, 1, keepdims=False)

    modulate = lax.psum_scatter(mod_part, "wide", scatter_dimension=0, tiled=True) + ada_bias
    shift_one, scale_one, gate_one, shift_two, scale_two, gate_two = [
        modulate[:, None, i * width : (i + 1) * width] for i in range(6)
    ]

    qkv_w = gather_wide(qkv_half)
    proj_w = gather_wide(w_proj)
    fc1_w = gather_wide(fc1_half)
    fc2_w = gather_wide(fc2_half)

    def both_halves(value):
        value = value.reshape(slots, half_len, -1)
        return lax.all_gather(value, "narrow", axis=1, tiled=True).reshape(all_rows, -1)

    def sum_halves(value):
        value = value.astype(BF16).reshape(slots, seq, -1)
        return (
            lax.psum_scatter(value, "narrow", scatter_dimension=1, tiled=True)
            .astype(F32)
            .reshape(slots, half_len, -1)
        )

    live_slot = (jnp.arange(slots, dtype=jnp.int32) < counts[0]).astype(F32)[:, None, None]
    tok_float = tokens.astype(F32)
    normed_one, inv_one = norm_rows(tok_float)
    a_in = (normed_one * (1.0 + scale_one) + shift_one).astype(BF16).reshape(rows, width)
    a_full = both_halves(a_in)
    qkv = mm(a_full, qkv_w)
    query = (qkv[:, :wh] + qv_bias_half[0]).astype(BF16)
    keys = qkv[:, wh : 2 * wh].astype(BF16)
    values = (qkv[:, 2 * wh :] + qv_bias_half[1]).astype(BF16)

    def to_heads(value):
        return value.reshape(slots, seq, heads, HEAD_DIM)

    query_heads, key_heads, value_heads = to_heads(query), to_heads(keys), to_heads(values)
    scores = (
        jnp.einsum("cqhe,ckhe->chqk", query_heads, key_heads, preferred_element_type=F32)
        * head_scale
    )
    log_total = jax.nn.logsumexp(scores, axis=-1, keepdims=True)
    probs = jnp.exp(scores - log_total)
    probs_low = probs.astype(BF16)
    attended = (
        jnp.einsum("chqk,ckhe->cqhe", probs_low, value_heads, preferred_element_type=F32)
        .astype(BF16)
        .reshape(slots, seq, wh)
    )
    att_own = lax.all_to_all(attended, "narrow", split_axis=1, concat_axis=2, tiled=True)
    att_own = att_own.reshape(rows, width)
    attn_out = (mm(att_own, proj_w) + proj_bias).reshape(slots, half_len, width)
    mid = tok_float + gate_one * attn_out
    normed_two, inv_two = norm_rows(mid)
    m_in = (normed_two * (1.0 + scale_two) + shift_two).astype(BF16).reshape(rows, width)
    m_full = both_halves(m_in)
    hidden = mm(m_full, fc1_w) + fc1_bias_half
    act_low = gelu_tanh(hidden).astype(BF16)
    mlp_out = sum_halves(mm(act_low, fc2_w)) + fc2_bias
    out = (live_slot * (mid + gate_two * mlp_out)).astype(BF16)

    grad_out = live_slot * cotangent.astype(F32)
    d_mlp = (gate_two * grad_out).astype(BF16).reshape(rows, width)
    d_mlp_full = both_halves(d_mlp)
    d_gate_two = jnp.sum(grad_out * mlp_out, axis=1)
    fc2_bias_sum = jnp.sum(d_mlp.astype(F32), axis=0)
    grad_fc2_part = outer_sum(act_low, d_mlp_full)
    d_hidden = (mm_back(d_mlp_full, fc2_w) * gelu_tanh_grad(hidden)).astype(BF16)
    fc1_bias_sum = jnp.sum(d_hidden.astype(F32), axis=0)
    grad_fc1_part = outer_sum(m_full, d_hidden)
    d_m_in = sum_halves(mm_back(d_hidden, fc1_w))
    d_scale_two = jnp.sum(d_m_in * normed_two, axis=1)
    d_shift_two = jnp.sum(d_m_in, axis=1)
    d_mid = grad_out + norm_back(d_m_in * (1.0 + scale_two), normed_two, inv_two)
    d_attn = (gate_one * d_mid).astype(BF16).reshape(rows, width)
    d_gate_one = jnp.sum(d_mid * attn_out, axis=1)
    proj_bias_sum = jnp.sum(d_attn.astype(F32), axis=0)
    grad_proj_part = outer_sum(att_own, d_attn)
    d_att_own = mm_back(d_attn, proj_w).astype(BF16).reshape(slots, half_len, width)
    d_att = lax.all_to_all(d_att_own, "narrow", split_axis=2, concat_axis=1, tiled=True)
    d_att = to_heads(d_att)
    d_probs = jnp.einsum("cqhe,ckhe->chqk", d_att, value_heads, preferred_element_type=F32)
    d_scores = (probs * (d_probs - jnp.sum(probs * d_probs, axis=-1, keepdims=True))).astype(BF16)
    d_query = (
        jnp.einsum("chqk,ckhe->cqhe", d_scores, key_heads, preferred_element_type=F32)
        * head_scale
    ).astype(BF16).reshape(all_rows, wh)
    d_keys = (
        jnp.einsum("chqk,cqhe->ckhe", d_scores, query_heads, preferred_element_type=F32)
        * head_scale
    ).astype(BF16).reshape(all_rows, wh)
    d_values = (
        jnp.einsum("chqk,cqhe->ckhe", probs_low, d_att, preferred_element_type=F32)
        .astype(BF16)
        .reshape(all_rows, wh)
    )
    d_qkv = jnp.concatenate([d_query, d_keys, d_values], axis=-1)
    qv_bias_sum = jnp.stack(
        [jnp.sum(d_query.astype(F32), axis=0), jnp.sum(d_values.astype(F32), axis=0)]
    )
    grad_qkv_part = outer_sum(a_full, d_qkv)
    d_a_in = sum_halves(mm_back(d_qkv, qkv_w))
    d_scale_one = jnp.sum(d_a_in * normed_one, axis=1)
    d_shift_one = jnp.sum(d_a_in, axis=1)
    grad_tokens = d_mid + norm_back(d_a_in * (1.0 + scale_one), normed_one, inv_one)

    d_modulate = jnp.concatenate(
        [d_shift_one, d_scale_one, d_gate_one, d_shift_two, d_scale_two, d_gate_two], axis=-1
    )
    def place(half, shape, axis):
        spread = jnp.zeros(shape, F32)
        return lax.dynamic_update_index_in_dim(spread, half, me, axis)

    qv_sum = place(qv_bias_sum, (2, pair, wh), 1).reshape(n_wide, -1)
    fc1_sum = place(fc1_bias_sum.reshape(n_wide, -1), (n_wide, pair, mh // n_wide), 1).reshape(
        n_wide, -1
    )
    bias_sums = jnp.concatenate(
        [
            qv_sum,
            proj_bias_sum.reshape(n_wide, -1),
            fc1_sum,
            fc2_bias_sum.reshape(n_wide, -1),
        ],
        axis=1,
    )
    bias_own = lax.psum(
        lax.psum_scatter(bias_sums, "wide", scatter_dimension=0, tiled=True), "narrow"
    ).reshape(-1)
    bias_grads = []
    at = 0
    for piece in (b_qv, b_proj, b_fc1, b_fc2):
        bias_grads.append(bias_own[at : at + piece.shape[0]])
        at += piece.shape[0]

    d_mod_low = lax.psum(d_modulate, "narrow").astype(BF16)
    d_mod_all = gather_wide(d_mod_low)
    grad_ada = outer_sum(silu_cols, d_mod_all)
    ada_cut = b_ada.shape[0]
    grad_ada_bias = jnp.sum(
        lax.dynamic_slice_in_dim(d_mod_all, here * ada_cut, ada_cut, 1).astype(F32), axis=0
    )
    d_silu_cols = mm_back(d_mod_all, w_ada)
    d_silu = lax.all_to_all(d_silu_cols, "wide", split_axis=0, concat_axis=1, tiled=True)
    grad_cond = d_silu * (cond_sig + cond_vec * cond_sig * (1.0 - cond_sig))

    def scatter_wide(part):
        return lax.psum_scatter(part.astype(BF16), "wide", scatter_dimension=0, tiled=True)

    def join_pair(piece):
        return lax.all_gather(piece, "narrow", axis=0, tiled=False).astype(F32)

    fc2_own = join_pair(scatter_wide(grad_fc2_part)).reshape(-1, width)
    fc1_own = join_pair(scatter_wide(grad_fc1_part)).reshape(pair, shard, n_wide, -1)
    fc1_own = fc1_own.transpose(1, 2, 0, 3).reshape(shard, mlp)
    proj_own = jnp.sum(join_pair(scatter_wide(grad_proj_part)), axis=0)
    qkv_own = join_pair(scatter_wide(grad_qkv_part)).reshape(pair, shard, 3, wh)
    qkv_own = qkv_own.transpose(1, 2, 0, 3).reshape(shard, 3 * width)

    return (
        out,
        grad_tokens,
        grad_cond,
        grad_ada,
        grad_ada_bias,
        qkv_own,
        bias_grads[0],
        proj_own,
        bias_grads[1],
        fc1_own,
        bias_grads[2],
        fc2_own,
        bias_grads[3],
    )


MESH = pl.DeviceIdType.MESH
NZ = 4
GELU_C = 0.7978845608028654
HBM_SPEC = pl.BlockSpec(memory_space=pl.ANY)
VMEM_SPEC = pl.BlockSpec(memory_space=pltpu.VMEM)
VMEM_LIMIT = 63 << 20


def dot_nn(a, b):
    return lax.dot_general(a, b, (((1,), (0,)), ((), ())), preferred_element_type=F32)


def dot_nt(a, b):
    return lax.dot_general(a, b, (((1,), (1,)), ((), ())), preferred_element_type=F32)


def dot_tn(a, b):
    return lax.dot_general(a, b, (((0,), (0,)), ((), ())), preferred_element_type=F32)


def do_when(cond, fn):
    if cond is True:
        fn()
    else:
        pl.when(cond)(fn)


def both(a, b):
    if a is True:
        return b
    if b is True:
        return a
    return jnp.logical_and(a, b)


def greet(peers):
    barrier = pltpu.get_barrier_semaphore()
    total = 0
    for cond, dev in peers:
        do_when(
            cond,
            lambda dev=dev: pl.semaphore_signal(
                barrier, inc=1, device_id=dev, device_id_type=MESH
            ),
        )
        total = total + (1 if cond is True else cond.astype(jnp.int32))
    pl.semaphore_wait(barrier, total)


class Sems:
    def __init__(self, send, recv):
        self.send, self.recv, self.n = send, recv, 0

    def take(self, count):
        at = self.n
        self.n += count
        return at


class Links:
    def __init__(self, sems):
        self.sems = sems
        self.sent = []

    def copy(self, src, dst, index, dev):
        return pltpu.make_async_remote_copy(
            src_ref=src,
            dst_ref=dst,
            send_sem=self.sems.send.at[index],
            recv_sem=self.sems.recv.at[index],
            device_id=dev,
            device_id_type=MESH,
        )

    def start(self, cond, src, dst, send_index, recv_index, dev):
        copy = pltpu.make_async_remote_copy(
            src_ref=src,
            dst_ref=dst,
            send_sem=self.sems.send.at[send_index],
            recv_sem=self.sems.recv.at[recv_index],
            device_id=dev,
            device_id_type=MESH,
        )
        do_when(cond, copy.start)
        self.sent.append((cond, copy))
        return copy

    def arrived(self, cond, ref, index, dev):
        copy = self.copy(ref, ref, index, dev)
        do_when(cond, copy.wait_recv)

    def left(self, copy):
        for cond, one in self.sent:
            if one is copy:
                do_when(cond, one.wait_send)
        self.sent = [entry for entry in self.sent if entry[1] is not copy]

    def drain(self):
        for cond, copy in self.sent:
            do_when(cond, copy.wait_send)
        self.sent = []


class Gather:
    def __init__(self, links, pos, block, source, sink):
        self.links, self.pos, self.block = links, pos, block
        self.source, self.sink = source, sink
        take = links.sems.take
        self.z_at, self.x_at, self.up_at, self.down_at = take(4), take(4), take(4), take(4)
        self.mine = []

    def along_z(self, cond, s, up, down):
        z, x, c, y = self.pos["z"], self.pos["x"], self.pos["c"], self.pos["y"]
        ref = self.block(s, x)
        for wanted, inside, at, to in (
            (up, z < NZ - 1, self.up_at, z + 1),
            (down, z > 0, self.down_at, z - 1),
        ):
            if wanted:
                self.mine.append(
                    self.links.start(
                        both(cond, inside), ref, ref, at + s, self.z_at + s,
                        self.pos["dev"](to, x, c, y),
                    )
                )

    def forward(self, cond, s, up, down):
        z, x, c, y = self.pos["z"], self.pos["x"], self.pos["c"], self.pos["y"]
        self.along_z(cond, s, up, down)
        ref = self.block(s, x)
        self.mine.append(
            self.links.start(
                cond, ref, ref, self.x_at + s, self.x_at + s, self.pos["dev"](z, 1 - x, c, y)
            )
        )

    def own(self):
        self.forward(self.source, self.pos["z"], True, True)

    def step(self, d):
        z, x = self.pos["z"], self.pos["x"]
        cond = both(self.source, z >= d)
        s = jnp.maximum(z - d, 0)
        self.links.arrived(cond, self.block(s, x), self.z_at + s, self.pos["me"])
        self.forward(cond, s, True, False)
        cond = both(self.source, z <= NZ - 1 - d)
        s = jnp.minimum(z + d, NZ - 1)
        self.links.arrived(cond, self.block(s, x), self.z_at + s, self.pos["me"])
        self.forward(cond, s, False, True)

    def finish(self):
        x = self.pos["x"]
        for s in range(NZ):
            self.links.arrived(self.sink, self.block(s, 1 - x), self.x_at + s, self.pos["me"])


class GatherAcross(Gather):
    def __init__(self, links, pos, block, on_column, not_column):
        super().__init__(links, pos, block, True, True)
        self.on_column, self.not_column = on_column, not_column

    def forward(self, cond, s, up, down):
        self.along_z(cond, s, up, down)

    def across(self):
        z, x, c, y = self.pos["z"], self.pos["x"], self.pos["c"], self.pos["y"]
        ref = self.block(z, x)
        self.mine.append(
            self.links.start(
                self.on_column, ref, ref, self.x_at, self.x_at, self.pos["dev"](z, 1 - x, c, y)
            )
        )

    def own(self):
        z, x = self.pos["z"], self.pos["x"]
        self.links.arrived(self.not_column, self.block(z, x), self.x_at, self.pos["me"])
        self.forward(True, z, True, True)

    def finish(self):
        pass


class Scatter:
    def __init__(self, links, pos, block, sums_x, sums_z, source, sink):
        self.links, self.pos, self.block = links, pos, block
        self.sums_x, self.sums_z = sums_x, sums_z
        self.source, self.sink = source, sink
        take = links.sems.take
        self.x_at, self.z_at, self.up_at, self.down_at = take(4), take(5), take(4), take(4)

    def begin(self):
        z, x, c, y = self.pos["z"], self.pos["x"], self.pos["c"], self.pos["y"]
        for s in (3, 0, 2, 1):
            self.links.start(
                self.source, self.block(s, 1 - x), self.sums_x.at[s], self.x_at + s,
                self.x_at + s, self.pos["dev"](z, 1 - x, c, y),
            )

    def add_x(self, s):
        self.links.arrived(True, self.sums_x.at[s], self.x_at + s, self.pos["me"])
        return self.block(s, self.pos["x"])[...].astype(F32) + self.sums_x[s].astype(F32)

    def hop(self, s, up):
        z, x, c, y = self.pos["z"], self.pos["x"], self.pos["c"], self.pos["y"]
        cond = both(self.sink, (z < s) if up else (z > s))

        def run():
            ref = self.block(s, x)
            ref[...] = self.add_x(s).astype(BF16)
            inner = (z > 0) if up else (z < NZ - 1)

            @pl.when(inner)
            def _():
                self.links.arrived(True, self.sums_z.at[s], self.z_at + s, self.pos["me"])
                ref[...] = (ref[...].astype(F32) + self.sums_z[s].astype(F32)).astype(BF16)

        do_when(cond, run)
        near = (z == s - 1) if up else (z == s + 1)
        slot = s if up else jnp.where(near, 4, s)
        to = self.pos["dev"](z + 1 if up else z - 1, x, c, y)
        at = (self.up_at if up else self.down_at) + s
        self.links.start(
            cond, self.block(s, x), self.sums_z.at[slot], at, self.z_at + slot, to
        )

    def finish(self, store):
        z, x = self.pos["z"], self.pos["x"]
        keep = self.block(z, x)

        def run():
            total = keep[...].astype(F32)
            self.links.arrived(True, self.sums_x.at[z], self.x_at + z, self.pos["me"])
            total = total + self.sums_x[z].astype(F32)
            keep[...] = total.astype(BF16)

            @pl.when(z > 0)
            def _():
                self.links.arrived(True, self.sums_z.at[z], self.z_at + z, self.pos["me"])
                keep[...] = (keep[...].astype(F32) + self.sums_z[z].astype(F32)).astype(BF16)

            @pl.when(z < NZ - 1)
            def _():
                self.links.arrived(True, self.sums_z.at[4], self.z_at + 4, self.pos["me"])
                keep[...] = (keep[...].astype(F32) + self.sums_z[4].astype(F32)).astype(BF16)

            store(keep)

        do_when(self.sink, run)

    def hops(self):
        out = []
        for k in range(3):
            out.append(lambda k=k: self.hop(3 - k, True))
            out.append(lambda k=k: self.hop(k, False))
        return out


class ScatterAcross(Scatter):
    def begin(self):
        pass

    def add_x(self, s):
        return self.block(s, self.pos["x"])[...].astype(F32)

    def finish(self, not_column, on_column):
        z, x, c, y = self.pos["z"], self.pos["x"], self.pos["c"], self.pos["y"]
        keep = self.block(z, x)

        @pl.when(z > 0)
        def _():
            self.links.arrived(True, self.sums_z.at[z], self.z_at + z, self.pos["me"])
            keep[...] = (keep[...].astype(F32) + self.sums_z[z].astype(F32)).astype(BF16)

        @pl.when(z < NZ - 1)
        def _():
            self.links.arrived(True, self.sums_z.at[4], self.z_at + 4, self.pos["me"])
            keep[...] = (keep[...].astype(F32) + self.sums_z[4].astype(F32)).astype(BF16)

        self.links.start(
            not_column, keep, self.sums_x.at[0], self.x_at, self.x_at,
            self.pos["dev"](z, 1 - x, c, y),
        )

    def land(self, on_column, target):
        keep = self.block(self.pos["z"], self.pos["x"])

        @pl.when(on_column)
        def _():
            self.links.arrived(True, self.sums_x.at[0], self.x_at, self.pos["me"])
            target[...] = (keep[...].astype(F32) + self.sums_x[0].astype(F32)).astype(BF16)


class PlaneExchange:
    def __init__(self, links, n_wide, w, y):
        self.links, self.n_wide, self.w, self.y = links, n_wide, w, y
        self.at = links.sems.take(n_wide)

    def begin(self, source, target):
        self.copies = []
        for k in range(1, self.n_wide):
            peer = lax.rem(self.w + k, self.n_wide)
            self.copies.append(
                self.links.start(
                    True, source(peer), target.at[self.w], self.at + k, self.at + k,
                    (peer, self.y),
                )
            )

    def finish(self):
        for copy in self.copies:
            copy.wait_recv()


class GroupGather:
    def __init__(self, links, pos, full):
        self.links, self.pos, self.full = links, pos, full
        self.at = links.sems.take(3)

    def begin(self):
        z, x, c, y = self.pos["z"], self.pos["x"], self.pos["c"], self.pos["y"]
        ref = self.full.at[pl.ds(2 * c, 2), y]
        self.links.start(True, ref, ref, self.at, self.at, self.pos["dev"](z, x, c, 1 - y))
        self.links.start(True, ref, ref, self.at + 1, self.at + 1, self.pos["dev"](z, x, 1 - c, y))

    def relay(self):
        z, x, c, y = self.pos["z"], self.pos["x"], self.pos["c"], self.pos["y"]
        ref = self.full.at[pl.ds(2 * c, 2), 1 - y]
        self.links.arrived(True, ref, self.at, self.pos["me"])
        self.links.start(True, ref, ref, self.at + 2, self.at + 2, self.pos["dev"](z, x, 1 - c, y))

    def finish(self):
        c, y = self.pos["c"], self.pos["y"]
        other = pl.ds(2 * (1 - c), 2)
        self.links.arrived(True, self.full.at[other, y], self.at + 1, self.pos["me"])
        self.links.arrived(True, self.full.at[other, 1 - y], self.at + 2, self.pos["me"])


class GroupSum:
    def __init__(self, links, pos, full, from_core, to_pair, from_pair):
        self.links, self.pos, self.full = links, pos, full
        self.from_core, self.to_pair, self.from_pair = from_core, to_pair, from_pair
        self.at = links.sems.take(2)

    def begin(self):
        z, x, c, y = self.pos["z"], self.pos["x"], self.pos["c"], self.pos["y"]
        self.core_copy = self.links.start(
            True, self.full.at[pl.ds(2 * (1 - c), 2)], self.from_core, self.at, self.at,
            self.pos["dev"](z, x, 1 - c, y),
        )

    def relay(self):
        z, x, c, y = self.pos["z"], self.pos["x"], self.pos["c"], self.pos["y"]
        self.links.arrived(True, self.from_core, self.at, self.pos["me"])
        for s in range(2):
            self.to_pair[s] = (
                self.full[2 * c + s, 1 - y].astype(F32) + self.from_core[s, 1 - y].astype(F32)
            ).astype(BF16)
        self.pair_copy = self.links.start(
            True, self.to_pair, self.from_pair, self.at + 1, self.at + 1,
            self.pos["dev"](z, x, c, 1 - y),
        )

    def arrived(self):
        self.links.arrived(True, self.from_pair, self.at + 1, self.pos["me"])

    def total(self, s):
        c, y = self.pos["c"], self.pos["y"]
        return (
            self.full[2 * c + s, y].astype(F32)
            + self.from_core[s, y].astype(F32)
            + self.from_pair[s].astype(F32)
        )


def gelu_both(u):
    inner = GELU_C * (u + 0.044715 * u * u * u)
    tan = jnp.tanh(inner)
    slope = GELU_C * (1.0 + 3.0 * 0.044715 * u * u)
    act = 0.5 * u * (1.0 + tan)
    grad = 0.5 * (1.0 + tan) + 0.5 * u * (1.0 - tan * tan) * slope
    return act, grad


def block_kernel(
    order, n_wide,
    tok_ref, cot_ref, parcel_ref, wada_ref, bada_ref,
    wqkv_ref, wfc1_ref, src_fc2, src_proj,
    out_ref, gtok_ref, got_ref, dmall_ref, vout_ref, dsil_ref,
    p_qkv, p_fc1, j_fc2, j_proj,
    g_qkv, g_proj, g_fc1, g_fc2, w_fc2,
    i_qkv, i_fc1, i_fc2, own_qkv, own_fc1, own_fc2, o_qkv, o_fc1,
    x_qkv, x_proj, x_fc1, x_fc2, z_qkv, z_proj, z_fc1, z_fc2,
    t_qkv, t_fc1, t_fc2, t_proj, j_qkv, j_fc1,
    a_all, m_all, d_all, qkv_all, att_all, act_all, gp_all,
    sum_a, sum_b, core_a, core_b, to_a, to_b, from_a, from_b,
    attn_own, mid_own, dmid_own,
    left, part, parts, tot, modh, mods, bqkv, brow, bias,
    dmod, dm_pair, dm_low, dm_all, v_send, v_all, dm_rows, ds_send,
    send, recv, local,
):
    w, y = lax.axis_index("wide"), lax.axis_index("narrow")
    z, x, c = w // 4, (w // 2) % 2, w % 2
    chip = 2 * z + x
    quarter = 2 * y + c

    def dev(z, x, c, y):
        return ((z * 2 + x) * 2 + c, y)

    sib, pair = dev(z, x, 1 - c, y), dev(z, x, c, 1 - y)
    pos = {"z": z, "x": x, "c": c, "y": y, "dev": dev, "me": sib}
    links = Links(Sems(send, recv))
    sems = links.sems
    half_len = tok_ref.shape[1]
    width = tok_ref.shape[2]
    hd = HEAD_DIM
    hq = g_proj.shape[0]
    hw = hd * hq
    shard = own_qkv.shape[0]
    rows2 = 2 * shard
    rows = 2 * half_len
    all_rows = 4 * rows
    half = modh.shape[2]
    head_scale = 1.0 / math.sqrt(HEAD_DIM)
    da_all = act_all

    greet(
        [(True, (lax.rem(w + k, n_wide), y)) for k in range(1, n_wide)]
        + [(True, pair), (True, dev(z, x, 1 - c, 1 - y))]
    )

    def rows_of(full):
        return lambda s, xx: full.at[pl.ds(pl.multiple_of((2 * s + xx) * rows2, 16), rows2), :]

    def head_of(s, xx):
        return g_proj.at[s]

    on_column = x == y
    not_column = jnp.logical_not(on_column)
    init = sems.take(3)
    ga_qkv = Gather(links, pos, rows_of(g_qkv), True, True)
    ga_proj = GatherAcross(links, pos, head_of, on_column, not_column)
    ga_fc1 = Gather(links, pos, rows_of(g_fc1), True, True)
    ga_fc2 = Gather(links, pos, rows_of(g_fc2), True, True)
    gg_a = GroupGather(links, pos, a_all)
    gg_d = GroupGather(links, pos, d_all)
    gg_m = GroupGather(links, pos, m_all)
    gg_da = GroupGather(links, pos, da_all)
    gs_attn = GroupSum(links, pos, sum_a, core_a, to_a, from_a)
    gs_mlp = GroupSum(links, pos, sum_b, core_b, to_b, from_b)
    gs_dm = GroupSum(links, pos, sum_a, core_a, to_a, from_a)
    gs_da = GroupSum(links, pos, sum_b, core_b, to_b, from_b)
    sc_fc2 = Scatter(links, pos, rows_of(w_fc2), x_fc2, z_fc2, True, True)
    sc_fc1 = Scatter(links, pos, rows_of(g_fc2), x_fc1, z_fc1, True, True)
    sc_qkv = Scatter(links, pos, rows_of(g_qkv), x_qkv, z_qkv, True, True)
    sc_proj = ScatterAcross(links, pos, head_of, x_proj, z_proj, True, True)
    ex_head = PlaneExchange(links, n_wide, w, y)
    ex_mod = PlaneExchange(links, n_wide, w, y)
    ex_dm = PlaneExchange(links, n_wide, w, y)
    ex_v = PlaneExchange(links, n_wide, w, y)
    ex_ds = PlaneExchange(links, n_wide, w, y)
    swap_mod, swap_dm, swap_v, swap_proj = sems.take(1), sems.take(1), sems.take(1), sems.take(1)
    steps = {}

    def step(fn):
        steps[fn.__name__] = fn
        return fn

    def norm(value):
        center = value - jnp.mean(value, axis=-1, keepdims=True)
        inv = lax.rsqrt(jnp.mean(center * center, axis=-1, keepdims=True) + eps_norm)
        return center * inv, inv

    def norm_grad(grad, normed, inv):
        return inv * (
            grad
            - jnp.mean(grad, axis=-1, keepdims=True)
            - normed * jnp.mean(grad * normed, axis=-1, keepdims=True)
        )

    def mod(k, s):
        return mods[k, s : s + 1, :]

    def pick(source, count, which):
        return jnp.concatenate(
            [source[:, (4 * j + which) * hd : (4 * j + which + 1) * hd] for j in range(count)],
            axis=1,
        )

    fc2_copy = pltpu.make_async_copy(src_fc2.at[quarter], own_fc2, local.at[0])
    proj_copy = pltpu.make_async_copy(src_proj, g_proj.at[z], local.at[1])

    @step
    def init0():
        fc2_copy.start()
        do_when(on_column, proj_copy.start)
        ex_head.begin(lambda p: parcel_ref.at[p], got_ref)
        got_ref[w] = parcel_ref[w]
        value = wqkv_ref[...]
        for q in range(4):

            @pl.when(quarter == q)
            def _():
                own_qkv[...] = pick(value, 3 * hq, q)

            @pl.when(2 * y + 1 - c == q)
            def _():
                o_qkv[...] = pick(value, 3 * hq, q)

        links.start(True, o_qkv, i_qkv, init, init, sib)

    @step
    def init1():
        links.start(True, src_fc2.at[2 * y + 1 - c], i_fc2, init + 2, init + 2, sib)
        value = wfc1_ref[...]
        for q in range(4):

            @pl.when(quarter == q)
            def _():
                own_fc1[...] = pick(value, n_wide, q)

            @pl.when(2 * y + 1 - c == q)
            def _():
                o_fc1[...] = pick(value, n_wide, q)

        links.start(True, o_fc1, i_fc1, init + 1, init + 1, sib)

    def place(own, inbox, full, index):
        links.arrived(True, inbox, init + index, sib)
        mine, other = own[...].astype(F32), inbox[...].astype(F32)
        first = jnp.where(c == 0, mine, other)
        second = jnp.where(c == 0, other, mine)
        at = pl.ds(pl.multiple_of(chip * rows2, 16), rows2)
        full[at, :] = jnp.concatenate([first, second], axis=0).astype(BF16)

    @step
    def q0():
        place(own_qkv, i_qkv, g_qkv, 0)
        ga_qkv.own()

    @step
    def f0():
        place(own_fc1, i_fc1, g_fc1, 1)
        ga_fc1.own()

    @step
    def e0():
        fc2_copy.wait()
        place(own_fc2, i_fc2, g_fc2, 2)
        ga_fc2.own()

    @step
    def px():
        do_when(on_column, proj_copy.wait)
        ga_proj.across()

    steps["p0"] = ga_proj.own
    for letter, gather in (("q", ga_qkv), ("p", ga_proj), ("f", ga_fc1), ("e", ga_fc2)):
        for d in range(1, NZ):
            steps[letter + str(d)] = lambda gather=gather, d=d: gather.step(d)

    @step
    def h1():
        ex_head.finish()
        for s in range(n_wide):
            left[2 * s : 2 * s + 2, :] = got_ref[s, 0:2, 0:128]
        lhs = left[...][:, :shard].astype(BF16)
        cols = pl.ds(pl.multiple_of(y * half, 128), half)
        res = dot_nn(lhs, wada_ref[:, cols]) + bada_ref[:, cols]
        for s in range(n_wide):
            part[s] = res[2 * s : 2 * s + 2, :]
        parts[w] = part[w]
        ex_mod.begin(lambda p: part.at[p], parts)

    @step
    def hb():
        def row(lane, owners):
            return jnp.concatenate([got_ref[o, 2:3, lane : lane + hd] for o in owners], axis=1)

        every = range(n_wide)
        brow[0:1, :] = row(0, every)
        brow[1:2, :] = row(128, every)
        brow[2:3, :] = row(256, every)
        bqkv[...] = jnp.concatenate(
            [
                row(384, [2 * j + y for j in range(hq)]),
                jnp.zeros((1, hw), F32),
                row(384, [n_wide // 2 + 2 * j + y for j in range(hq)]),
            ],
            axis=1,
        )

    @step
    def h2():
        ex_mod.finish()
        total = parts[0]
        for s in range(1, n_wide):
            total = total + parts[s]
        tot[...] = total
        modh[y] = total
        links.start(True, tot, modh.at[y], swap_mod, swap_mod, pair)

    @step
    def h3():
        links.arrived(True, modh.at[1 - y], swap_mod, sib)
        for k in range(6):
            at = (k % 3) * width
            mods[k] = modh[k // 3, :, at : at + width]

    @step
    def ln1():
        for s in range(2):
            normed, inv = norm(tok_ref[s].astype(F32))
            a_all[2 * c + s, y] = (normed * (1.0 + mod(1, s)) + mod(0, s)).astype(BF16)
        gg_a.begin()

    steps["ar"], steps["af"] = gg_a.relay, gg_a.finish

    @step
    def d0():
        for s in range(2):
            d_all[2 * c + s, y] = (mod(5, s) * cot_ref[s].astype(F32)).astype(BF16)
        gg_d.begin()

    steps["dr"], steps["df"] = gg_d.relay, gg_d.finish

    @step
    def qkv():
        ga_qkv.finish()

        @pl.loop(0, 4)
        def _(i):
            res = dot_nn(a_all[i].reshape(rows, width), g_qkv[...]) + bqkv[...]
            qkv_all[i] = res.astype(BF16)

    def head_parts(packed, h):
        return [packed[:, t * hw + h * hd : t * hw + (h + 1) * hd] for t in range(3)]

    def softmax(q, k):
        scores = dot_nt(q, k) * head_scale
        top = jnp.max(scores, axis=-1, keepdims=True)
        e = jnp.exp(scores - top)
        return e * (1.0 / jnp.sum(e, axis=-1, keepdims=True))

    @step
    def att():
        @pl.loop(0, 4)
        def _(i):
            packed = qkv_all[i]
            acc = None
            for h in range(hq):
                q, k, v = head_parts(packed, h)
                p = softmax(q, k).astype(BF16)
                o = dot_nn(p, v).astype(BF16)
                att_all[h, i] = o
                term = dot_nn(o, g_proj[h])
                acc = term if acc is None else acc + term
            sum_a[i] = acc.astype(BF16).reshape(2, half_len, width)

        gs_attn.begin()

    steps["sr"] = gs_attn.relay

    @step
    def ln2():
        gs_attn.arrived()
        for s in range(2):
            attn = gs_attn.total(s) + brow[1:2, :]
            attn_own[s] = attn
            mid = tok_ref[s].astype(F32) + mod(2, s) * attn
            mid_own[s] = mid
            normed, inv = norm(mid)
            m_all[2 * c + s, y] = (normed * (1.0 + mod(4, s)) + mod(3, s)).astype(BF16)
        gg_m.begin()

    steps["mr"], steps["mf"] = gg_m.relay, gg_m.finish

    @step
    def fc1():
        ga_fc1.finish()

        @pl.loop(0, 4)
        def _(i):
            u = dot_nn(m_all[i].reshape(rows, width), g_fc1[...]) + brow[0:1, :]
            act, grad = gelu_both(u)
            act_all[i] = act.astype(BF16).reshape(2, half_len, width)
            gp_all[i] = grad.astype(BF16)

    steps["ef"] = ga_fc2.finish

    @step
    def fc2():
        @pl.loop(0, 4)
        def _(i):
            res = dot_nn(act_all[i].reshape(rows, width), g_fc2[...])
            sum_b[i] = res.astype(BF16).reshape(2, half_len, width)

        gs_mlp.begin()

    steps["ur"] = gs_mlp.relay

    def outer(left, right, full):
        lanes = width // 3

        @pl.loop(0, 3)
        def _(j):
            at = pl.ds(pl.multiple_of(j * lanes, 128), lanes)
            full[at, :] = dot_tn(left(at).reshape(all_rows, lanes), right()).astype(BF16)

    @step
    def w2():
        outer(
            lambda at: act_all[:, :, :, at], lambda: d_all[...].reshape(all_rows, width), w_fc2
        )
        sc_fc2.begin()

    @step
    def dh():
        bias[...] = jnp.zeros_like(bias)

        @pl.loop(0, 4)
        def _(i):
            d_act = dot_nt(d_all[i].reshape(rows, width), g_fc2[...])
            d_hidden = (d_act * gp_all[i].astype(F32)).astype(BF16)
            gp_all[i] = d_hidden
            bias[0:1, :] += jnp.sum(d_hidden.astype(F32), axis=0, keepdims=True)

    @step
    def dm():
        links.left(gs_attn.core_copy)

        @pl.loop(0, 4)
        def _(i):
            res = dot_nt(gp_all[i], g_fc1[...])
            sum_a[i] = res.astype(BF16).reshape(2, half_len, width)

        gs_dm.begin()

    @step
    def w1():
        for copy in ga_fc2.mine:
            links.left(copy)
        outer(
            lambda at: m_all[:, :, :, at], lambda: gp_all[...].reshape(all_rows, width), g_fc2
        )
        sc_fc1.begin()

    @step
    def tr():
        links.left(gs_attn.pair_copy)
        gs_dm.relay()

    @step
    def res():
        gs_mlp.arrived()
        for s in range(2):
            mlp = gs_mlp.total(s) + brow[2:3, :]
            out_ref[s] = (mid_own[s] + mod(5, s) * mlp).astype(BF16)
            grad_out = cot_ref[s].astype(F32)
            dmod[5, s : s + 1, :] = jnp.sum(grad_out * mlp, axis=0, keepdims=True)
            bias[2:3, :] += jnp.sum(d_all[2 * c + s, y].astype(F32), axis=0, keepdims=True)

    @step
    def ln2b():
        gs_dm.arrived()
        for s in range(2):
            d_m = gs_dm.total(s)
            normed, inv = norm(mid_own[s])
            dmod[4, s : s + 1, :] = jnp.sum(d_m * normed, axis=0, keepdims=True)
            dmod[3, s : s + 1, :] = jnp.sum(d_m, axis=0, keepdims=True)
            d_mid = cot_ref[s].astype(F32) + norm_grad(d_m * (1.0 + mod(4, s)), normed, inv)
            dmid_own[s] = d_mid
            d_attn = (mod(2, s) * d_mid).astype(BF16)
            da_all[2 * c + s, y] = d_attn
            dmod[2, s : s + 1, :] = jnp.sum(d_mid * attn_own[s], axis=0, keepdims=True)
            bias[1:2, :] += jnp.sum(d_attn.astype(F32), axis=0, keepdims=True)
        gg_da.begin()

    steps["gr"], steps["gf"] = gg_da.relay, gg_da.finish

    @step
    def attb():
        @pl.loop(0, 4)
        def _(i):
            packed = qkv_all[i]
            d_attn = da_all[i].reshape(rows, width)
            grads = [[], [], []]
            for h in range(hq):
                q, k, v = head_parts(packed, h)
                p = softmax(q, k)
                p_low = p.astype(BF16)
                d_att = dot_nt(d_attn, g_proj[h]).astype(BF16)
                d_p = dot_nt(d_att, v)
                d_s = (p * (d_p - jnp.sum(p * d_p, axis=-1, keepdims=True))).astype(BF16)
                grads[0].append(dot_nn(d_s, k) * head_scale)
                grads[1].append(dot_tn(d_s, q) * head_scale)
                grads[2].append(dot_tn(p_low, d_att))
            d_qkv = jnp.concatenate(grads[0] + grads[1] + grads[2], axis=1).astype(BF16)
            qkv_all[i] = d_qkv
            bias[3:4, 0 : 3 * hw] += jnp.sum(d_qkv.astype(F32), axis=0, keepdims=True)

    @step
    def dam():
        links.left(gs_mlp.core_copy)

        @pl.loop(0, 4)
        def _(i):
            res = dot_nt(qkv_all[i], g_qkv[...])
            sum_b[i] = res.astype(BF16).reshape(2, half_len, width)

        gs_da.begin()

    @step
    def wq():
        for copy in ga_qkv.mine:
            links.left(copy)
        outer(
            lambda at: a_all[:, :, :, at], lambda: qkv_all[...].reshape(all_rows, 3 * hw), g_qkv
        )
        sc_qkv.begin()

    @step
    def xr():
        links.left(gs_mlp.pair_copy)
        gs_da.relay()

    @step
    def wp():
        for copy in ga_proj.mine:
            links.left(copy)

        @pl.loop(0, hq)
        def _(h):
            value = att_all[h].reshape(all_rows, hd)
            g_proj[h] = dot_tn(value, da_all[...].reshape(all_rows, width)).astype(BF16)

    for letter, scatter in (("E", sc_fc2), ("F", sc_fc1), ("Q", sc_qkv), ("P", sc_proj)):
        for k, fn in enumerate(scatter.hops()):
            steps[letter + str(k)] = fn

    def join(scatter, pack, target, index):
        at = sems.take(3)
        keep_copy = pltpu.make_async_copy(pack.at[c], target.at[quarter], local.at[index])

        def begin():
            def store(keep):
                total = keep[...].astype(F32)
                pack[0] = total[:shard].astype(BF16)
                pack[1] = total[shard:].astype(BF16)

            scatter.finish(store)
            links.start(True, pack.at[1 - c], target.at[quarter], at, at, sib)
            links.start(True, pack.at[c], target.at[quarter], at + 1, at + 1, pair)
            links.start(
                True, pack.at[1 - c], target.at[quarter], at + 2, at + 2, dev(z, x, 1 - c, 1 - y)
            )
            keep_copy.start()

        def finish():
            keep_copy.wait()
            links.arrived(True, target.at[2 * y + 1 - c], at, sib)
            links.arrived(True, target.at[2 * (1 - y) + c], at + 1, sib)
            links.arrived(True, target.at[2 * (1 - y) + 1 - c], at + 2, sib)

        return begin, finish

    def spread(source, target, count):
        target[...] = jnp.concatenate(
            [source[k % 4, :, (k // 4) * hd : (k // 4 + 1) * hd] for k in range(4 * count)],
            axis=1,
        )

    steps["EJ"], steps["EG"] = join(sc_fc2, t_fc2, j_fc2, 2)
    steps["FJ"], fc1_joined = join(sc_fc1, t_fc1, j_fc1, 3)
    steps["QJ"], qkv_joined = join(sc_qkv, t_qkv, j_qkv, 4)

    @step
    def FG():
        fc1_joined()
        spread(j_fc1, p_fc1, n_wide)

    @step
    def QG():
        qkv_joined()
        spread(j_qkv, p_qkv, 3 * hq)

    steps["PJ"] = lambda: sc_proj.finish(not_column, on_column)

    @step
    def PK():
        sc_proj.land(on_column, t_proj)
        links.start(on_column, t_proj, t_proj, swap_proj, swap_proj, pair)

    @step
    def PG():
        links.arrived(not_column, t_proj, swap_proj, sib)
        j_proj[...] = t_proj[...]

    @step
    def ln1b():
        gs_da.arrived()
        for s in range(2):
            d_a = gs_da.total(s)
            normed, inv = norm(tok_ref[s].astype(F32))
            dmod[1, s : s + 1, :] = jnp.sum(d_a * normed, axis=0, keepdims=True)
            dmod[0, s : s + 1, :] = jnp.sum(d_a, axis=0, keepdims=True)
            gtok_ref[s] = dmid_own[s] + norm_grad(d_a * (1.0 + mod(1, s)), normed, inv)
        links.start(True, dmod, dm_pair, swap_dm, swap_dm, pair)

    @step
    def t1():
        links.arrived(True, dm_pair, swap_dm, sib)
        for k in range(6):
            dm_low[:, k * width : (k + 1) * width] = (dmod[k] + dm_pair[k]).astype(BF16)
        dm_all[w] = dm_low[...]
        ex_dm.begin(lambda p: dm_low, dm_all)

    @step
    def t2():
        ex_dm.finish()
        res = None
        for k in range(6):
            at = slice(k * width, (k + 1) * width)
            for s in range(n_wide):
                dm_rows[2 * s : 2 * s + 2, :] = dm_all[s, :, at].astype(F32)
            low = dm_rows[...].astype(BF16)
            dmall_ref[:, at] = low
            term = dot_nt(low, wada_ref[:, at])
            res = term if res is None else res + term
        ds_send[...] = jnp.zeros_like(ds_send)
        for s in range(n_wide):
            ds_send[s, :, 0:shard] = res[2 * s : 2 * s + 2, :]
        dsil_ref[w] = ds_send[w]
        ex_ds.begin(lambda p: ds_send.at[p], dsil_ref)

    steps["t3"] = ex_ds.finish

    @step
    def v1():
        v_send[...] = jnp.zeros_like(v_send)
        for s in range(n_wide):
            at = slice(s * hd, (s + 1) * hd)
            v_send[s, pl.ds(c, 1), 0:hd] = bias[0:1, at]
            v_send[s, 2:4, 0:hd] = bias[1:3, at]
        for j in range(hq):
            v_send[2 * j + y, pl.ds(4 + c, 1), 0:hd] = bias[3:4, j * hd : (j + 1) * hd]
            v_send[n_wide // 2 + 2 * j + y, pl.ds(4 + c, 1), 0:hd] = bias[
                3:4, 2 * hw + j * hd : 2 * hw + (j + 1) * hd
            ]
        v_all[w] = v_send[w]
        ex_v.begin(lambda p: v_send.at[p], v_all)

    @step
    def v2():
        ex_v.finish()
        total = v_all[0]
        for s in range(1, n_wide):
            total = total + v_all[s]
        vout_ref[y] = total
        links.start(True, vout_ref.at[y], vout_ref.at[y], swap_v, swap_v, pair)

    steps["v3"] = lambda: links.arrived(True, vout_ref.at[1 - y], swap_v, sib)
    steps["end"] = links.drain

    for name in order:
        steps[name]()


ORDER = (
    "init0", "px", "q0", "h1", "hb", "p0", "q1", "h2", "h3", "ln1", "q2", "p1", "q3",
    "init1", "p2", "ar", "f0", "d0", "af", "qkv", "e0", "p3", "att", "f1", "sr", "dr", "e1",
    "f2", "e2", "ln2", "f3", "e3", "mr", "mf", "df", "fc1", "ef", "fc2", "w2", "ur", "dh",
    "dm", "w1", "tr", "E0", "res", "ln2b", "F0", "gr", "E1", "E2", "gf", "attb", "F1", "F2",
    "E3", "dam", "wq", "v1", "F3", "E4", "F4", "xr", "F5", "Q0", "FJ", "wp", "P0", "P1",
    "P2", "E5", "v2", "EJ", "Q1", "Q2", "P3", "P4", "Q3", "P5", "PJ", "ln1b", "t1", "PK",
    "Q4", "FG", "Q5", "QJ", "EG", "PG", "v3", "t2", "t3", "QG", "end",
)


def fast_device(
    tokens,
    cond,
    timesteps,
    counts,
    w_ada,
    b_ada,
    w_qkv,
    b_qv,
    w_proj,
    b_proj,
    w_fc1,
    b_fc1,
    w_fc2,
    b_fc2,
    cotangent,
):
    slots, half_len, width = tokens.shape
    n_wide = lax.axis_size("wide")
    w, y = lax.axis_index("wide"), lax.axis_index("narrow")
    shard = w_ada.shape[0]
    mlp = w_fc1.shape[1]
    hq = HEADS // 4
    nq = 3 * hq * HEAD_DIM
    rows = slots * half_len
    mq = mlp // 4
    half = w_ada.shape[1] // 2

    cond_vec = cond.astype(F32) + time_features(timesteps, width)
    cond_sig = jax.nn.sigmoid(cond_vec)
    silu = (cond_vec * cond_sig).astype(BF16).astype(F32)
    chunks = jnp.pad(
        silu.reshape(slots, n_wide, shard).transpose(1, 0, 2), ((0, 0), (0, 0), (0, 640 - shard))
    )

    def tile(piece):
        return jnp.pad(piece.astype(F32), ((0, 0), (0, 128 - piece.shape[1])))

    fc1_pieces = lax.dynamic_slice_in_dim(b_fc1.reshape(4, shard), 2 * y, 2, 0)
    vector = jnp.concatenate(
        [
            tile(fc1_pieces),
            tile(jnp.broadcast_to(b_proj, (2, shard))),
            tile(jnp.broadcast_to(b_fc2, (2, shard))),
            tile(b_qv.reshape(2, shard)),
            jnp.zeros((2, 128), F32),
        ],
        axis=1,
    )
    vector = jnp.broadcast_to(vector[None], (n_wide // 2, 2, 640)).reshape(n_wide, 1, 640)
    parcel = jnp.concatenate([chunks, vector, jnp.zeros_like(vector)], axis=1)
    ada_cut = b_ada.shape[0]
    ada_bias = lax.dynamic_update_slice_in_dim(
        jnp.zeros((1, w_ada.shape[1]), F32), b_ada.astype(F32)[None], w * ada_cut, 1
    )
    live = (jnp.arange(slots, dtype=jnp.int32) < counts[0])[:, None, None]
    cot_live = jnp.where(live, cotangent, jnp.zeros_like(cotangent))

    def v16(*shape):
        return pltpu.VMEM(shape, BF16)

    def v32(*shape):
        return pltpu.VMEM(shape, F32)

    two = 2 * shard
    full = (4, 2, half_len, width)
    own = (slots, half_len, width)
    scratch = [
        v16(width, nq), v16(hq, shard, width), v16(width, mq), v16(mq, width), v16(mq, width),
        v16(shard, nq), v16(shard, mq), v16(shard, width),
        v16(shard, nq), v16(shard, mq), v16(shard, width), v16(shard, nq), v16(shard, mq),
        v16(4, two, nq), v16(1, shard, width), v16(4, two, mq), v16(4, two, width),
        v16(5, two, nq), v16(5, shard, width), v16(5, two, mq), v16(5, two, width),
        v16(2, shard, nq), v16(2, shard, mq), v16(2, shard, width), v16(shard, width),
        v16(4, shard, nq), v16(4, shard, mq),
        v16(*full), v16(*full), v16(*full),
        v16(4, rows, nq), v16(hq, 4, rows, HEAD_DIM), v16(*full), v16(4, rows, mq),
        v16(*full), v16(*full),
        v16(2, 2, half_len, width), v16(2, 2, half_len, width),
        v16(*own), v16(*own), v16(*own), v16(*own),
        v32(*own), v32(*own), v32(*own),
        v32(n_wide * slots, 128), v32(n_wide, slots, half), v32(n_wide, slots, half),
        v32(slots, half), v32(2, slots, half), v32(6, slots, width), v32(1, nq), v32(4, width),
        v32(4, width),
        v32(6, slots, width), v32(6, slots, width), v16(slots, 6 * width),
        v16(n_wide, slots, 6 * width), v32(n_wide, 8, 128), v32(n_wide, 8, 128),
        v32(n_wide * slots, width), v32(n_wide, slots, 128),
        pltpu.SemaphoreType.DMA((300,)),
        pltpu.SemaphoreType.DMA((300,)),
        pltpu.SemaphoreType.DMA((5,)),
    ]
    out, gtok, got, dm_all, v_out, d_silu, p_qkv, p_fc1, j_fc2, j_proj = pl.pallas_call(
        functools.partial(block_kernel, ORDER, n_wide),
        out_shape=(
            jax.ShapeDtypeStruct(own, BF16),
            jax.ShapeDtypeStruct(own, F32),
            jax.ShapeDtypeStruct((n_wide, 4, 640), F32),
            jax.ShapeDtypeStruct((n_wide * slots, 6 * width), BF16),
            jax.ShapeDtypeStruct((2, 8, 128), F32),
            jax.ShapeDtypeStruct((n_wide, slots, 128), F32),
            jax.ShapeDtypeStruct(w_qkv.shape, BF16),
            jax.ShapeDtypeStruct(w_fc1.shape, BF16),
            jax.ShapeDtypeStruct((4, shard, width), BF16),
            jax.ShapeDtypeStruct((shard, width), BF16),
        ),
        in_specs=[VMEM_SPEC] * 7 + [HBM_SPEC] * 2,
        out_specs=(VMEM_SPEC,) * 8 + (HBM_SPEC, VMEM_SPEC),
        scratch_shapes=scratch,
        compiler_params=pltpu.CompilerParams(
            collective_id=0, has_side_effects=True, vmem_limit_bytes=VMEM_LIMIT
        ),
    )(
        tokens, cot_live, parcel, w_ada, ada_bias, w_qkv, w_fc1,
        w_fc2.reshape(4, shard, width), w_proj,
    )
    out = jnp.where(live, out, jnp.zeros_like(out))
    silu_cols = got[:, 0:2, :shard].reshape(n_wide * slots, shard).astype(BF16)
    grad_ada = outer_sum(silu_cols, dm_all)
    grad_b_ada = jnp.sum(
        lax.dynamic_slice_in_dim(dm_all, w * ada_cut, ada_cut, 1).astype(F32), axis=0
    )
    d_silu = d_silu[:, :, :shard].transpose(1, 0, 2).reshape(slots, width)
    grad_cond = d_silu * (cond_sig + cond_vec * cond_sig * (1.0 - cond_sig))
    v_sum = (v_out[0] + v_out[1])[:, :shard]
    return (
        out,
        gtok,
        grad_cond,
        grad_ada,
        grad_b_ada,
        p_qkv.astype(F32),
        v_sum[4:6].reshape(-1),
        j_proj.astype(F32),
        v_sum[2],
        p_fc1.astype(F32),
        v_out[:, 0:2, :shard].reshape(-1),
        j_fc2.astype(F32).reshape(w_fc2.shape),
        v_sum[3],
    )


def solution(mesh):
    in_specs = (
        P("wide", "narrow", None),
        P("wide", None),
        P("wide"),
        P("wide"),
        P("wide", None),
        P("wide"),
        P("wide", None),
        P("wide"),
        P("wide", None),
        P("wide"),
        P("wide", None),
        P("wide"),
        P("wide", None),
        P("wide"),
        P("wide", "narrow", None),
    )
    out_specs = (
        P("wide", "narrow", None),
        P("wide", "narrow", None),
        P("wide", None),
        P("wide", None),
        P("wide"),
        P("wide", None),
        P("wide"),
        P("wide", None),
        P("wide"),
        P("wide", None),
        P("wide"),
        P("wide", None),
        P("wide"),
    )
    small = mesh.shape["wide"] == 16 and mesh.shape["narrow"] == 2
    per_device = fast_device if small else on_device
    return jax.shard_map(
        per_device, mesh=mesh, in_specs=in_specs, out_specs=out_specs, check_vma=False
    )
```

```python
import functools
import math

import jax
import jax.numpy as jnp
from jax import lax
from jax.experimental import pallas as pl
from jax.experimental.pallas import tpu as pltpu
from jax.sharding import PartitionSpec as P

HEADS = 16
HEAD_DIM = 72

F32 = jnp.float32
BF16 = jnp.bfloat16
eps_norm = 1e-06


def norm_rows(value):
    center = value - jnp.mean(value, axis=-1, keepdims=True)
    inv_std = lax.rsqrt(jnp.mean(center * center, axis=-1, keepdims=True) + eps_norm)
    return (center * inv_std, inv_std)


def norm_back(grad, normed, inv_std):
    return inv_std * (
        grad
        - jnp.mean(grad, axis=-1, keepdims=True)
        - normed * jnp.mean(grad * normed, axis=-1, keepdims=True)
    )


def gelu_tanh(value):
    return (
        0.5
        * value
        * (1.0 + jnp.tanh(0.7978845608028654 * (value + 0.044715 * value * value * value)))
    )


def gelu_tanh_grad(value):
    inner = 0.7978845608028654 * (value + 0.044715 * value * value * value)
    tan = jnp.tanh(inner)
    slope = 0.7978845608028654 * (1.0 + 3.0 * 0.044715 * value * value)
    return 0.5 * (1.0 + tan) + 0.5 * value * (1.0 - tan * tan) * slope


def time_features(steps, width):
    half_width = width // 2
    freqs = jnp.exp(-math.log(10000.0) * jnp.arange(half_width).astype(F32) / half_width)
    angles = steps.astype(F32)[:, None] * freqs[None, :]
    return jnp.concatenate([jnp.cos(angles), jnp.sin(angles)], axis=-1)


def mm(left, right):
    return jnp.einsum("sk,kn->sn", left, right, preferred_element_type=F32)


def mm_back(grad, weight):
    return jnp.einsum("sn,kn->sk", grad, weight, preferred_element_type=F32)


def outer_sum(left, right):
    return jnp.einsum("sk,sn->kn", left, right, preferred_element_type=F32)


def gather_wide(value, axis=0):
    return lax.all_gather(value, "wide", axis=axis, tiled=True)


def on_device(
    tokens,
    cond,
    timesteps,
    counts,
    w_ada,
    b_ada,
    w_qkv,
    b_qv,
    w_proj,
    b_proj,
    w_fc1,
    b_fc1,
    w_fc2,
    b_fc2,
    cotangent,
):
    slots, half_len, width = tokens.shape
    pair = lax.axis_size("narrow")
    n_wide = lax.axis_size("wide")
    me = lax.axis_index("narrow")
    here = lax.axis_index("wide")
    seq = half_len * pair
    rows = slots * half_len
    all_rows = slots * seq
    wh = width // pair
    heads = HEADS // pair
    mlp = w_fc1.shape[1]
    mh = mlp // pair
    shard = w_ada.shape[0]
    head_scale = 1.0 / math.sqrt(HEAD_DIM)

    qkv_half = lax.dynamic_index_in_dim(
        w_qkv.reshape(-1, 3, pair, wh), me, 2, keepdims=False
    ).reshape(-1, 3 * wh)
    fc1_half = lax.dynamic_index_in_dim(
        w_fc1.reshape(-1, n_wide, pair, mh // n_wide), me, 2, keepdims=False
    ).reshape(-1, mh)
    fc2_half = lax.dynamic_index_in_dim(
        w_fc2.reshape(pair, -1, width), me, 0, keepdims=False
    )

    cond_vec = cond.astype(F32) + time_features(timesteps, width)
    cond_sig = jax.nn.sigmoid(cond_vec)
    silu_low = (cond_vec * cond_sig).astype(BF16)
    silu_all = gather_wide(silu_low)
    silu_cols = lax.dynamic_slice_in_dim(silu_all, here * shard, shard, 1)
    mod_part = jnp.dot(silu_cols, w_ada, preferred_element_type=F32)
    biases = gather_wide(jnp.concatenate([b_ada, b_qv, b_proj, b_fc1, b_fc2])[None])
    cuts = []
    at = 0
    for piece in (b_ada, b_qv, b_proj, b_fc1, b_fc2):
        cuts.append(biases[:, at : at + piece.shape[0]].astype(F32))
        at += piece.shape[0]
    ada_bias, qv_bias, proj_bias, fc1_bias, fc2_bias = [c.reshape(-1) for c in cuts]
    fc1_bias_half = lax.dynamic_index_in_dim(
        fc1_bias.reshape(n_wide, pair, -1), me, 1, keepdims=False
    ).reshape(-1)
    qv_bias_half = lax.dynamic_index_in_dim(qv_bias.reshape(2, pair, wh), me, 1, keepdims=False)

    modulate = lax.psum_scatter(mod_part, "wide", scatter_dimension=0, tiled=True) + ada_bias
    shift_one, scale_one, gate_one, shift_two, scale_two, gate_two = [
        modulate[:, None, i * width : (i + 1) * width] for i in range(6)
    ]

    qkv_w = gather_wide(qkv_half)
    proj_w = gather_wide(w_proj)
    fc1_w = gather_wide(fc1_half)
    fc2_w = gather_wide(fc2_half)

    def both_halves(value):
        value = value.reshape(slots, half_len, -1)
        return lax.all_gather(value, "narrow", axis=1, tiled=True).reshape(all_rows, -1)

    def sum_halves(value):
        value = value.astype(BF16).reshape(slots, seq, -1)
        return (
            lax.psum_scatter(value, "narrow", scatter_dimension=1, tiled=True)
            .astype(F32)
            .reshape(slots, half_len, -1)
        )

    live_slot = (jnp.arange(slots, dtype=jnp.int32) < counts[0]).astype(F32)[:, None, None]
    tok_float = tokens.astype(F32)
    normed_one, inv_one = norm_rows(tok_float)
    a_in = (normed_one * (1.0 + scale_one) + shift_one).astype(BF16).reshape(rows, width)
    a_full = both_halves(a_in)
    qkv = mm(a_full, qkv_w)
    query = (qkv[:, :wh] + qv_bias_half[0]).astype(BF16)
    keys = qkv[:, wh : 2 * wh].astype(BF16)
    values = (qkv[:, 2 * wh :] + qv_bias_half[1]).astype(BF16)

    def to_heads(value):
        return value.reshape(slots, seq, heads, HEAD_DIM)

    query_heads, key_heads, value_heads = to_heads(query), to_heads(keys), to_heads(values)
    scores = (
        jnp.einsum("cqhe,ckhe->chqk", query_heads, key_heads, preferred_element_type=F32)
        * head_scale
    )
    log_total = jax.nn.logsumexp(scores, axis=-1, keepdims=True)
    probs = jnp.exp(scores - log_total)
    probs_low = probs.astype(BF16)
    attended = (
        jnp.einsum("chqk,ckhe->cqhe", probs_low, value_heads, preferred_element_type=F32)
        .astype(BF16)
        .reshape(slots, seq, wh)
    )
    att_own = lax.all_to_all(attended, "narrow", split_axis=1, concat_axis=2, tiled=True)
    att_own = att_own.reshape(rows, width)
    attn_out = (mm(att_own, proj_w) + proj_bias).reshape(slots, half_len, width)
    mid = tok_float + gate_one * attn_out
    normed_two, inv_two = norm_rows(mid)
    m_in = (normed_two * (1.0 + scale_two) + shift_two).astype(BF16).reshape(rows, width)
    m_full = both_halves(m_in)
    hidden = mm(m_full, fc1_w) + fc1_bias_half
    act_low = gelu_tanh(hidden).astype(BF16)
    mlp_out = sum_halves(mm(act_low, fc2_w)) + fc2_bias
    out = (live_slot * (mid + gate_two * mlp_out)).astype(BF16)

    grad_out = live_slot * cotangent.astype(F32)
    d_mlp = (gate_two * grad_out).astype(BF16).reshape(rows, width)
    d_mlp_full = both_halves(d_mlp)
    d_gate_two = jnp.sum(grad_out * mlp_out, axis=1)
    fc2_bias_sum = jnp.sum(d_mlp.astype(F32), axis=0)
    grad_fc2_part = outer_sum(act_low, d_mlp_full)
    d_hidden = (mm_back(d_mlp_full, fc2_w) * gelu_tanh_grad(hidden)).astype(BF16)
    fc1_bias_sum = jnp.sum(d_hidden.astype(F32), axis=0)
    grad_fc1_part = outer_sum(m_full, d_hidden)
    d_m_in = sum_halves(mm_back(d_hidden, fc1_w))
    d_scale_two = jnp.sum(d_m_in * normed_two, axis=1)
    d_shift_two = jnp.sum(d_m_in, axis=1)
    d_mid = grad_out + norm_back(d_m_in * (1.0 + scale_two), normed_two, inv_two)
    d_attn = (gate_one * d_mid).astype(BF16).reshape(rows, width)
    d_gate_one = jnp.sum(d_mid * attn_out, axis=1)
    proj_bias_sum = jnp.sum(d_attn.astype(F32), axis=0)
    grad_proj_part = outer_sum(att_own, d_attn)
    d_att_own = mm_back(d_attn, proj_w).astype(BF16).reshape(slots, half_len, width)
    d_att = lax.all_to_all(d_att_own, "narrow", split_axis=2, concat_axis=1, tiled=True)
    d_att = to_heads(d_att)
    d_probs = jnp.einsum("cqhe,ckhe->chqk", d_att, value_heads, preferred_element_type=F32)
    d_scores = (probs * (d_probs - jnp.sum(probs * d_probs, axis=-1, keepdims=True))).astype(BF16)
    d_query = (
        jnp.einsum("chqk,ckhe->cqhe", d_scores, key_heads, preferred_element_type=F32)
        * head_scale
    ).astype(BF16).reshape(all_rows, wh)
    d_keys = (
        jnp.einsum("chqk,cqhe->ckhe", d_scores, query_heads, preferred_element_type=F32)
        * head_scale
    ).astype(BF16).reshape(all_rows, wh)
    d_values = (
        jnp.einsum("chqk,cqhe->ckhe", probs_low, d_att, preferred_element_type=F32)
        .astype(BF16)
        .reshape(all_rows, wh)
    )
    d_qkv = jnp.concatenate([d_query, d_keys, d_values], axis=-1)
    qv_bias_sum = jnp.stack(
        [jnp.sum(d_query.astype(F32), axis=0), jnp.sum(d_values.astype(F32), axis=0)]
    )
    grad_qkv_part = outer_sum(a_full, d_qkv)
    d_a_in = sum_halves(mm_back(d_qkv, qkv_w))
    d_scale_one = jnp.sum(d_a_in * normed_one, axis=1)
    d_shift_one = jnp.sum(d_a_in, axis=1)
    grad_tokens = d_mid + norm_back(d_a_in * (1.0 + scale_one), normed_one, inv_one)

    d_modulate = jnp.concatenate(
        [d_shift_one, d_scale_one, d_gate_one, d_shift_two, d_scale_two, d_gate_two], axis=-1
    )
    def place(half, shape, axis):
        spread = jnp.zeros(shape, F32)
        return lax.dynamic_update_index_in_dim(spread, half, me, axis)

    qv_sum = place(qv_bias_sum, (2, pair, wh), 1).reshape(n_wide, -1)
    fc1_sum = place(fc1_bias_sum.reshape(n_wide, -1), (n_wide, pair, mh // n_wide), 1).reshape(
        n_wide, -1
    )
    bias_sums = jnp.concatenate(
        [
            qv_sum,
            proj_bias_sum.reshape(n_wide, -1),
            fc1_sum,
            fc2_bias_sum.reshape(n_wide, -1),
        ],
        axis=1,
    )
    bias_own = lax.psum(
        lax.psum_scatter(bias_sums, "wide", scatter_dimension=0, tiled=True), "narrow"
    ).reshape(-1)
    bias_grads = []
    at = 0
    for piece in (b_qv, b_proj, b_fc1, b_fc2):
        bias_grads.append(bias_own[at : at + piece.shape[0]])
        at += piece.shape[0]

    d_mod_low = lax.psum(d_modulate, "narrow").astype(BF16)
    d_mod_all = gather_wide(d_mod_low)
    grad_ada = outer_sum(silu_cols, d_mod_all)
    ada_cut = b_ada.shape[0]
    grad_ada_bias = jnp.sum(
        lax.dynamic_slice_in_dim(d_mod_all, here * ada_cut, ada_cut, 1).astype(F32), axis=0
    )
    d_silu_cols = mm_back(d_mod_all, w_ada)
    d_silu = lax.all_to_all(d_silu_cols, "wide", split_axis=0, concat_axis=1, tiled=True)
    grad_cond = d_silu * (cond_sig + cond_vec * cond_sig * (1.0 - cond_sig))

    def scatter_wide(part):
        return lax.psum_scatter(part.astype(BF16), "wide", scatter_dimension=0, tiled=True)

    def join_pair(piece):
        return lax.all_gather(piece, "narrow", axis=0, tiled=False).astype(F32)

    fc2_own = join_pair(scatter_wide(grad_fc2_part)).reshape(-1, width)
    fc1_own = join_pair(scatter_wide(grad_fc1_part)).reshape(pair, shard, n_wide, -1)
    fc1_own = fc1_own.transpose(1, 2, 0, 3).reshape(shard, mlp)
    proj_own = jnp.sum(join_pair(scatter_wide(grad_proj_part)), axis=0)
    qkv_own = join_pair(scatter_wide(grad_qkv_part)).reshape(pair, shard, 3, wh)
    qkv_own = qkv_own.transpose(1, 2, 0, 3).reshape(shard, 3 * width)

    return (
        out,
        grad_tokens,
        grad_cond,
        grad_ada,
        grad_ada_bias,
        qkv_own,
        bias_grads[0],
        proj_own,
        bias_grads[1],
        fc1_own,
        bias_grads[2],
        fc2_own,
        bias_grads[3],
    )


MESH = pl.DeviceIdType.MESH
NZ = 4
GELU_C = 0.7978845608028654
HBM_SPEC = pl.BlockSpec(memory_space=pl.ANY)
VMEM_SPEC = pl.BlockSpec(memory_space=pltpu.VMEM)
VMEM_LIMIT = 63 << 20


def dot_nn(a, b):
    return lax.dot_general(a, b, (((1,), (0,)), ((), ())), preferred_element_type=F32)


def dot_nt(a, b):
    return lax.dot_general(a, b, (((1,), (1,)), ((), ())), preferred_element_type=F32)


def dot_tn(a, b):
    return lax.dot_general(a, b, (((0,), (0,)), ((), ())), preferred_element_type=F32)


def do_when(cond, fn):
    if cond is True:
        fn()
    else:
        pl.when(cond)(fn)


def both(a, b):
    if a is True:
        return b
    if b is True:
        return a
    return jnp.logical_and(a, b)


def greet(peers):
    barrier = pltpu.get_barrier_semaphore()
    total = 0
    for cond, dev in peers:
        do_when(
            cond,
            lambda dev=dev: pl.semaphore_signal(
                barrier, inc=1, device_id=dev, device_id_type=MESH
            ),
        )
        total = total + (1 if cond is True else cond.astype(jnp.int32))
    pl.semaphore_wait(barrier, total)


class Sems:
    def __init__(self, send, recv):
        self.send, self.recv, self.n = send, recv, 0

    def take(self, count):
        at = self.n
        self.n += count
        return at


class Links:
    def __init__(self, sems):
        self.sems = sems
        self.sent = []

    def copy(self, src, dst, index, dev):
        return pltpu.make_async_remote_copy(
            src_ref=src,
            dst_ref=dst,
            send_sem=self.sems.send.at[index],
            recv_sem=self.sems.recv.at[index],
            device_id=dev,
            device_id_type=MESH,
        )

    def start(self, cond, src, dst, send_index, recv_index, dev):
        copy = pltpu.make_async_remote_copy(
            src_ref=src,
            dst_ref=dst,
            send_sem=self.sems.send.at[send_index],
            recv_sem=self.sems.recv.at[recv_index],
            device_id=dev,
            device_id_type=MESH,
        )
        do_when(cond, copy.start)
        self.sent.append((cond, copy))
        return copy

    def arrived(self, cond, ref, index, dev):
        copy = self.copy(ref, ref, index, dev)
        do_when(cond, copy.wait_recv)

    def left(self, copy):
        for cond, one in self.sent:
            if one is copy:
                do_when(cond, one.wait_send)
        self.sent = [entry for entry in self.sent if entry[1] is not copy]

    def drain(self):
        for cond, copy in self.sent:
            do_when(cond, copy.wait_send)
        self.sent = []


class Gather:
    def __init__(self, links, pos, block, source, sink):
        self.links, self.pos, self.block = links, pos, block
        self.source, self.sink = source, sink
        take = links.sems.take
        self.z_at, self.x_at, self.up_at, self.down_at = take(4), take(4), take(4), take(4)
        self.mine = []

    def along_z(self, cond, s, up, down):
        z, x, c, y = self.pos["z"], self.pos["x"], self.pos["c"], self.pos["y"]
        ref = self.block(s, x)
        for wanted, inside, at, to in (
            (up, z < NZ - 1, self.up_at, z + 1),
            (down, z > 0, self.down_at, z - 1),
        ):
            if wanted:
                self.mine.append(
                    self.links.start(
                        both(cond, inside), ref, ref, at + s, self.z_at + s,
                        self.pos["dev"](to, x, c, y),
                    )
                )

    def forward(self, cond, s, up, down):
        z, x, c, y = self.pos["z"], self.pos["x"], self.pos["c"], self.pos["y"]
        self.along_z(cond, s, up, down)
        ref = self.block(s, x)
        self.mine.append(
            self.links.start(
                cond, ref, ref, self.x_at + s, self.x_at + s, self.pos["dev"](z, 1 - x, c, y)
            )
        )

    def own(self):
        self.forward(self.source, self.pos["z"], True, True)

    def step(self, d):
        z, x = self.pos["z"], self.pos["x"]
        cond = both(self.source, z >= d)
        s = jnp.maximum(z - d, 0)
        self.links.arrived(cond, self.block(s, x), self.z_at + s, self.pos["me"])
        self.forward(cond, s, True, False)
        cond = both(self.source, z <= NZ - 1 - d)
        s = jnp.minimum(z + d, NZ - 1)
        self.links.arrived(cond, self.block(s, x), self.z_at + s, self.pos["me"])
        self.forward(cond, s, False, True)

    def finish(self):
        x = self.pos["x"]
        for s in range(NZ):
            self.links.arrived(self.sink, self.block(s, 1 - x), self.x_at + s, self.pos["me"])


class GatherAcross(Gather):
    def __init__(self, links, pos, block, on_column, not_column):
        super().__init__(links, pos, block, True, True)
        self.on_column, self.not_column = on_column, not_column

    def forward(self, cond, s, up, down):
        self.along_z(cond, s, up, down)

    def across(self):
        z, x, c, y = self.pos["z"], self.pos["x"], self.pos["c"], self.pos["y"]
        ref = self.block(z, x)
        self.mine.append(
            self.links.start(
                self.on_column, ref, ref, self.x_at, self.x_at, self.pos["dev"](z, 1 - x, c, y)
            )
        )

    def own(self):
        z, x = self.pos["z"], self.pos["x"]
        self.links.arrived(self.not_column, self.block(z, x), self.x_at, self.pos["me"])
        self.forward(True, z, True, True)

    def finish(self):
        pass


class Scatter:
    def __init__(self, links, pos, block, sums_x, sums_z, source, sink):
        self.links, self.pos, self.block = links, pos, block
        self.sums_x, self.sums_z = sums_x, sums_z
        self.source, self.sink = source, sink
        take = links.sems.take
        self.x_at, self.z_at, self.up_at, self.down_at = take(4), take(5), take(4), take(4)

    def begin(self):
        z, x, c, y = self.pos["z"], self.pos["x"], self.pos["c"], self.pos["y"]
        far = jnp.where(z < 2, 3, 0)
        middle = jnp.where(z == 0, 2, jnp.where(z == 3, 1, 3 - far))
        near = jnp.where(z % 2 == 0, 1, 2)
        for s in (far, middle, near, z):
            self.links.start(
                self.source, self.block(s, 1 - x), self.sums_x.at[s], self.x_at + s,
                self.x_at + s, self.pos["dev"](z, 1 - x, c, y),
            )

    def add_x(self, s):
        self.links.arrived(True, self.sums_x.at[s], self.x_at + s, self.pos["me"])
        return self.block(s, self.pos["x"])[...].astype(F32) + self.sums_x[s].astype(F32)

    def hop(self, here, s, up):
        z, x, c, y = self.pos["z"], self.pos["x"], self.pos["c"], self.pos["y"]
        first = here == (0 if up else NZ - 1)
        ref = self.block(s, x)

        def run():
            total = self.add_x(s)
            if not first:
                self.links.arrived(True, self.sums_z.at[s], self.z_at + s, self.pos["me"])
                total = total + self.sums_z[s].astype(F32)
            ref[...] = total.astype(BF16)

        cond = z == here
        do_when(cond, run)
        to = here + 1 if up else here - 1
        slot = 4 if s == to and not up else s
        at = (self.up_at if up else self.down_at) + s
        self.links.start(
            cond, ref, self.sums_z.at[slot], at, self.z_at + slot, self.pos["dev"](to, x, c, y)
        )

    def finish(self, store):
        z, x = self.pos["z"], self.pos["x"]
        keep = self.block(z, x)

        def run():
            total = keep[...].astype(F32)
            self.links.arrived(True, self.sums_x.at[z], self.x_at + z, self.pos["me"])
            total = total + self.sums_x[z].astype(F32)
            keep[...] = total.astype(BF16)

            @pl.when(z > 0)
            def _():
                self.links.arrived(True, self.sums_z.at[z], self.z_at + z, self.pos["me"])
                keep[...] = (keep[...].astype(F32) + self.sums_z[z].astype(F32)).astype(BF16)

            @pl.when(z < NZ - 1)
            def _():
                self.links.arrived(True, self.sums_z.at[4], self.z_at + 4, self.pos["me"])
                keep[...] = (keep[...].astype(F32) + self.sums_z[4].astype(F32)).astype(BF16)

            store(keep)

        do_when(self.sink, run)

    def hops(self):
        out = {}
        for here in range(NZ - 1):
            for s in range(here + 1, NZ):

                def both_ways(here=here, s=s):
                    self.hop(here, s, True)
                    self.hop(NZ - 1 - here, NZ - 1 - s, False)

                out[str(s) + str(here)] = both_ways
        return out


class ScatterAcross(Scatter):
    def begin(self):
        pass

    def add_x(self, s):
        return self.block(s, self.pos["x"])[...].astype(F32)

    def finish(self, not_column, on_column):
        z, x, c, y = self.pos["z"], self.pos["x"], self.pos["c"], self.pos["y"]
        keep = self.block(z, x)

        @pl.when(z > 0)
        def _():
            self.links.arrived(True, self.sums_z.at[z], self.z_at + z, self.pos["me"])
            keep[...] = (keep[...].astype(F32) + self.sums_z[z].astype(F32)).astype(BF16)

        @pl.when(z < NZ - 1)
        def _():
            self.links.arrived(True, self.sums_z.at[4], self.z_at + 4, self.pos["me"])
            keep[...] = (keep[...].astype(F32) + self.sums_z[4].astype(F32)).astype(BF16)

        self.links.start(
            not_column, keep, self.sums_x.at[0], self.x_at, self.x_at,
            self.pos["dev"](z, 1 - x, c, y),
        )

    def land(self, on_column, target):
        keep = self.block(self.pos["z"], self.pos["x"])

        @pl.when(on_column)
        def _():
            self.links.arrived(True, self.sums_x.at[0], self.x_at, self.pos["me"])
            target[...] = (keep[...].astype(F32) + self.sums_x[0].astype(F32)).astype(BF16)


class PlaneExchange:
    def __init__(self, links, n_wide, w, y):
        self.links, self.n_wide, self.w, self.y = links, n_wide, w, y
        self.at = links.sems.take(n_wide)

    def begin(self, source, target):
        self.copies = []
        for k in range(1, self.n_wide):
            peer = lax.rem(self.w + k, self.n_wide)
            self.copies.append(
                self.links.start(
                    True, source(peer), target.at[self.w], self.at + k, self.at + k,
                    (peer, self.y),
                )
            )

    def finish(self):
        for copy in self.copies:
            copy.wait_recv()


class GroupGather:
    def __init__(self, links, pos, full):
        self.links, self.pos, self.full = links, pos, full
        self.at = links.sems.take(3)

    def begin(self):
        z, x, c, y = self.pos["z"], self.pos["x"], self.pos["c"], self.pos["y"]
        ref = self.full.at[pl.ds(2 * c, 2), y]
        self.links.start(True, ref, ref, self.at, self.at, self.pos["dev"](z, x, c, 1 - y))
        self.links.start(True, ref, ref, self.at + 1, self.at + 1, self.pos["dev"](z, x, 1 - c, y))

    def relay(self):
        z, x, c, y = self.pos["z"], self.pos["x"], self.pos["c"], self.pos["y"]
        ref = self.full.at[pl.ds(2 * c, 2), 1 - y]
        self.links.arrived(True, ref, self.at, self.pos["me"])
        self.links.start(True, ref, ref, self.at + 2, self.at + 2, self.pos["dev"](z, x, 1 - c, y))

    def finish(self):
        c, y = self.pos["c"], self.pos["y"]
        other = pl.ds(2 * (1 - c), 2)
        self.links.arrived(True, self.full.at[other, y], self.at + 1, self.pos["me"])
        self.links.arrived(True, self.full.at[other, 1 - y], self.at + 2, self.pos["me"])


class GroupSum:
    def __init__(self, links, pos, full, from_core, to_pair, from_pair):
        self.links, self.pos, self.full = links, pos, full
        self.from_core, self.to_pair, self.from_pair = from_core, to_pair, from_pair
        self.at = links.sems.take(2)

    def begin(self):
        z, x, c, y = self.pos["z"], self.pos["x"], self.pos["c"], self.pos["y"]
        self.core_copy = self.links.start(
            True, self.full.at[pl.ds(2 * (1 - c), 2)], self.from_core, self.at, self.at,
            self.pos["dev"](z, x, 1 - c, y),
        )

    def relay(self):
        z, x, c, y = self.pos["z"], self.pos["x"], self.pos["c"], self.pos["y"]
        self.links.arrived(True, self.from_core, self.at, self.pos["me"])
        for s in range(2):
            self.to_pair[s] = (
                self.full[2 * c + s, 1 - y].astype(F32) + self.from_core[s, 1 - y].astype(F32)
            ).astype(BF16)
        self.pair_copy = self.links.start(
            True, self.to_pair, self.from_pair, self.at + 1, self.at + 1,
            self.pos["dev"](z, x, c, 1 - y),
        )

    def arrived(self):
        self.links.arrived(True, self.from_pair, self.at + 1, self.pos["me"])

    def total(self, s):
        c, y = self.pos["c"], self.pos["y"]
        return (
            self.full[2 * c + s, y].astype(F32)
            + self.from_core[s, y].astype(F32)
            + self.from_pair[s].astype(F32)
        )


def gelu_both(u):
    inner = GELU_C * (u + 0.044715 * u * u * u)
    tan = jnp.tanh(inner)
    slope = GELU_C * (1.0 + 3.0 * 0.044715 * u * u)
    act = 0.5 * u * (1.0 + tan)
    grad = 0.5 * (1.0 + tan) + 0.5 * u * (1.0 - tan * tan) * slope
    return act, grad


def block_kernel(
    order, n_wide,
    tok_ref, cot_ref, parcel_ref, wada_ref, bada_ref,
    wqkv_ref, wfc1_ref, src_fc2, src_proj,
    out_ref, gtok_ref, got_ref, dmall_ref, vout_ref, dsil_ref,
    p_qkv, p_fc1, j_fc2, j_proj,
    g_qkv, g_proj, g_fc1, g_fc2, w_fc2,
    i_qkv, i_fc1, i_fc2, own_qkv, own_fc1, own_fc2, o_qkv, o_fc1,
    x_qkv, x_proj, x_fc1, x_fc2, z_qkv, z_proj, z_fc1, z_fc2,
    t_qkv, t_fc1, t_fc2, t_proj, j_qkv, j_fc1,
    a_all, m_all, d_all, qkv_all, att_all, act_all, gp_all,
    sum_a, sum_b, core_a, core_b, to_a, to_b, from_a, from_b,
    attn_own, mid_own, dmid_own,
    left, part, parts, tot, modh, mods, bqkv, brow, bias,
    dmod, dm_pair, dm_low, dm_all, v_send, v_all, dm_rows, ds_send,
    send, recv, local,
):
    w, y = lax.axis_index("wide"), lax.axis_index("narrow")
    z, x, c = w // 4, (w // 2) % 2, w % 2
    chip = 2 * z + x
    quarter = 2 * y + c

    def dev(z, x, c, y):
        return ((z * 2 + x) * 2 + c, y)

    sib, pair = dev(z, x, 1 - c, y), dev(z, x, c, 1 - y)
    pos = {"z": z, "x": x, "c": c, "y": y, "dev": dev, "me": sib}
    links = Links(Sems(send, recv))
    sems = links.sems
    half_len = tok_ref.shape[1]
    width = tok_ref.shape[2]
    hd = HEAD_DIM
    hq = g_proj.shape[0]
    hw = hd * hq
    shard = own_qkv.shape[0]
    rows2 = 2 * shard
    rows = 2 * half_len
    all_rows = 4 * rows
    half = modh.shape[2]
    head_scale = 1.0 / math.sqrt(HEAD_DIM)
    da_all = act_all

    greet(
        [(True, (lax.rem(w + k, n_wide), y)) for k in range(1, n_wide)]
        + [(True, pair), (True, dev(z, x, 1 - c, 1 - y))]
    )

    def rows_of(full):
        return lambda s, xx: full.at[pl.ds(pl.multiple_of((2 * s + xx) * rows2, 16), rows2), :]

    def head_of(s, xx):
        return g_proj.at[s]

    on_column = x == y
    not_column = jnp.logical_not(on_column)
    init = sems.take(3)
    ga_qkv = Gather(links, pos, rows_of(g_qkv), True, True)
    ga_proj = GatherAcross(links, pos, head_of, on_column, not_column)
    ga_fc1 = Gather(links, pos, rows_of(g_fc1), True, True)
    ga_fc2 = Gather(links, pos, rows_of(g_fc2), True, True)
    gg_a = GroupGather(links, pos, a_all)
    gg_d = GroupGather(links, pos, d_all)
    gg_m = GroupGather(links, pos, m_all)
    gg_da = GroupGather(links, pos, da_all)
    gs_attn = GroupSum(links, pos, sum_a, core_a, to_a, from_a)
    gs_mlp = GroupSum(links, pos, sum_b, core_b, to_b, from_b)
    gs_dm = GroupSum(links, pos, sum_a, core_a, to_a, from_a)
    gs_da = GroupSum(links, pos, sum_a, core_a, to_a, from_a)
    sc_fc2 = Scatter(links, pos, rows_of(w_fc2), x_fc2, z_fc2, True, True)
    sc_fc1 = Scatter(links, pos, rows_of(g_fc2), x_fc1, z_fc1, True, True)
    sc_qkv = Scatter(links, pos, rows_of(g_qkv), x_qkv, z_qkv, True, True)
    sc_proj = ScatterAcross(links, pos, head_of, x_proj, z_proj, True, True)
    ex_head = PlaneExchange(links, n_wide, w, y)
    ex_mod = PlaneExchange(links, n_wide, w, y)
    ex_dm = PlaneExchange(links, n_wide, w, y)
    ex_v = PlaneExchange(links, n_wide, w, y)
    ex_ds = PlaneExchange(links, n_wide, w, y)
    swap_mod, swap_dm, swap_v, swap_proj = sems.take(1), sems.take(1), sems.take(1), sems.take(1)
    steps = {}

    def step(fn):
        steps[fn.__name__] = fn
        return fn

    def norm(value):
        center = value - jnp.mean(value, axis=-1, keepdims=True)
        inv = lax.rsqrt(jnp.mean(center * center, axis=-1, keepdims=True) + eps_norm)
        return center * inv, inv

    def norm_grad(grad, normed, inv):
        return inv * (
            grad
            - jnp.mean(grad, axis=-1, keepdims=True)
            - normed * jnp.mean(grad * normed, axis=-1, keepdims=True)
        )

    def mod(k, s):
        return mods[k, s : s + 1, :]

    def pick(source, count, which):
        return jnp.concatenate(
            [source[:, (4 * j + which) * hd : (4 * j + which + 1) * hd] for j in range(count)],
            axis=1,
        )

    fc2_copy = pltpu.make_async_copy(src_fc2.at[quarter], own_fc2, local.at[0])
    proj_copy = pltpu.make_async_copy(src_proj, g_proj.at[z], local.at[1])

    @step
    def init0():
        fc2_copy.start()
        do_when(on_column, proj_copy.start)
        ex_head.begin(lambda p: parcel_ref.at[p], got_ref)
        got_ref[w] = parcel_ref[w]
        value = wqkv_ref[...]
        for q in range(4):

            @pl.when(quarter == q)
            def _():
                own_qkv[...] = pick(value, 3 * hq, q)

            @pl.when(2 * y + 1 - c == q)
            def _():
                o_qkv[...] = pick(value, 3 * hq, q)

        links.start(True, o_qkv, i_qkv, init, init, sib)

    @step
    def init1():
        links.start(True, src_fc2.at[2 * y + 1 - c], i_fc2, init + 2, init + 2, sib)
        value = wfc1_ref[...]
        for q in range(4):

            @pl.when(quarter == q)
            def _():
                own_fc1[...] = pick(value, n_wide, q)

            @pl.when(2 * y + 1 - c == q)
            def _():
                o_fc1[...] = pick(value, n_wide, q)

        links.start(True, o_fc1, i_fc1, init + 1, init + 1, sib)

    def place(own, inbox, full, index):
        links.arrived(True, inbox, init + index, sib)
        mine, other = own[...].astype(F32), inbox[...].astype(F32)
        first = jnp.where(c == 0, mine, other)
        second = jnp.where(c == 0, other, mine)
        at = pl.ds(pl.multiple_of(chip * rows2, 16), rows2)
        full[at, :] = jnp.concatenate([first, second], axis=0).astype(BF16)

    @step
    def q0():
        place(own_qkv, i_qkv, g_qkv, 0)
        ga_qkv.own()

    @step
    def f0():
        place(own_fc1, i_fc1, g_fc1, 1)
        ga_fc1.own()

    @step
    def e0():
        fc2_copy.wait()
        place(own_fc2, i_fc2, g_fc2, 2)
        ga_fc2.own()

    @step
    def px():
        do_when(on_column, proj_copy.wait)
        ga_proj.across()

    steps["p0"] = ga_proj.own
    for letter, gather in (("q", ga_qkv), ("p", ga_proj), ("f", ga_fc1), ("e", ga_fc2)):
        for d in range(1, NZ):
            steps[letter + str(d)] = lambda gather=gather, d=d: gather.step(d)

    @step
    def h1():
        ex_head.finish()
        for s in range(n_wide):
            left[2 * s : 2 * s + 2, :] = got_ref[s, 0:2, 0:128]
        lhs = left[...][:, :shard].astype(BF16)
        cols = pl.ds(pl.multiple_of(y * half, 128), half)
        res = dot_nn(lhs, wada_ref[:, cols]) + bada_ref[:, cols]
        for s in range(n_wide):
            part[s] = res[2 * s : 2 * s + 2, :]
        parts[w] = part[w]
        ex_mod.begin(lambda p: part.at[p], parts)

    @step
    def hb():
        def row(lane, owners):
            return jnp.concatenate([got_ref[o, 2:3, lane : lane + hd] for o in owners], axis=1)

        every = range(n_wide)
        brow[0:1, :] = row(0, every)
        brow[1:2, :] = row(128, every)
        brow[2:3, :] = row(256, every)
        bqkv[...] = jnp.concatenate(
            [
                row(384, [2 * j + y for j in range(hq)]),
                jnp.zeros((1, hw), F32),
                row(384, [n_wide // 2 + 2 * j + y for j in range(hq)]),
            ],
            axis=1,
        )

    @step
    def h2():
        ex_mod.finish()
        total = parts[0]
        for s in range(1, n_wide):
            total = total + parts[s]
        tot[...] = total
        modh[y] = total
        links.start(True, tot, modh.at[y], swap_mod, swap_mod, pair)

    @step
    def h3():
        links.arrived(True, modh.at[1 - y], swap_mod, sib)
        for k in range(6):
            at = (k % 3) * width
            mods[k] = modh[k // 3, :, at : at + width]

    @step
    def ln1():
        for s in range(2):
            normed, inv = norm(tok_ref[s].astype(F32))
            a_all[2 * c + s, y] = (normed * (1.0 + mod(1, s)) + mod(0, s)).astype(BF16)
        gg_a.begin()

    steps["ar"], steps["af"] = gg_a.relay, gg_a.finish

    @step
    def d0():
        for s in range(2):
            d_all[2 * c + s, y] = (mod(5, s) * cot_ref[s].astype(F32)).astype(BF16)
        gg_d.begin()

    steps["dr"], steps["df"] = gg_d.relay, gg_d.finish

    @step
    def qkv():
        ga_qkv.finish()

        @pl.loop(0, 4)
        def _(i):
            res = dot_nn(a_all[i].reshape(rows, width), g_qkv[...]) + bqkv[...]
            qkv_all[i] = res.astype(BF16)

    def head_parts(packed, h):
        return [packed[:, t * hw + h * hd : t * hw + (h + 1) * hd] for t in range(3)]

    def softmax(q, k):
        scores = dot_nt(q, k) * head_scale
        top = jnp.max(scores, axis=-1, keepdims=True)
        e = jnp.exp(scores - top)
        return e * (1.0 / jnp.sum(e, axis=-1, keepdims=True))

    @step
    def att():
        @pl.loop(0, 4)
        def _(i):
            packed = qkv_all[i]
            acc = None
            for h in range(hq):
                q, k, v = head_parts(packed, h)
                p = softmax(q, k).astype(BF16)
                o = dot_nn(p, v).astype(BF16)
                att_all[h, i] = o
                term = dot_nn(o, g_proj[h])
                acc = term if acc is None else acc + term
            sum_a[i] = acc.astype(BF16).reshape(2, half_len, width)

        gs_attn.begin()

    steps["sr"] = gs_attn.relay

    @step
    def ln2():
        gs_attn.arrived()
        for s in range(2):
            attn = gs_attn.total(s) + brow[1:2, :]
            attn_own[s] = attn
            mid = tok_ref[s].astype(F32) + mod(2, s) * attn
            mid_own[s] = mid
            normed, inv = norm(mid)
            m_all[2 * c + s, y] = (normed * (1.0 + mod(4, s)) + mod(3, s)).astype(BF16)
        gg_m.begin()

    steps["mr"], steps["mf"] = gg_m.relay, gg_m.finish

    @step
    def fc1():
        ga_fc1.finish()

        @pl.loop(0, 4)
        def _(i):
            u = dot_nn(m_all[i].reshape(rows, width), g_fc1[...]) + brow[0:1, :]
            act, grad = gelu_both(u)
            act_all[i] = act.astype(BF16).reshape(2, half_len, width)
            gp_all[i] = grad.astype(BF16)

    steps["ef"] = ga_fc2.finish

    @step
    def fc2():
        @pl.loop(0, 4)
        def _(i):
            res = dot_nn(act_all[i].reshape(rows, width), g_fc2[...])
            sum_b[i] = res.astype(BF16).reshape(2, half_len, width)

        gs_mlp.begin()

    steps["ur"] = gs_mlp.relay

    def outer(left, right, full):
        lanes = width // 3

        @pl.loop(0, 3)
        def _(j):
            at = pl.ds(pl.multiple_of(j * lanes, 128), lanes)
            full[at, :] = dot_tn(left(at).reshape(all_rows, lanes), right()).astype(BF16)

    @step
    def w2():
        outer(
            lambda at: act_all[:, :, :, at], lambda: d_all[...].reshape(all_rows, width), w_fc2
        )
        sc_fc2.begin()

    @step
    def dh():
        bias[...] = jnp.zeros_like(bias)

        @pl.loop(0, 4)
        def _(i):
            d_act = dot_nt(d_all[i].reshape(rows, width), g_fc2[...])
            d_hidden = (d_act * gp_all[i].astype(F32)).astype(BF16)
            gp_all[i] = d_hidden
            bias[0:1, :] += jnp.sum(d_hidden.astype(F32), axis=0, keepdims=True)

    @step
    def dm():
        links.left(gs_attn.core_copy)

        @pl.loop(0, 4)
        def _(i):
            res = dot_nt(gp_all[i], g_fc1[...])
            sum_a[i] = res.astype(BF16).reshape(2, half_len, width)

        gs_dm.begin()

    @step
    def w1():
        for copy in ga_fc2.mine:
            links.left(copy)
        outer(
            lambda at: m_all[:, :, :, at], lambda: gp_all[...].reshape(all_rows, width), g_fc2
        )
        sc_fc1.begin()

    @step
    def tr():
        links.left(gs_attn.pair_copy)
        gs_dm.relay()

    @step
    def res():
        gs_mlp.arrived()
        for s in range(2):
            mlp = gs_mlp.total(s) + brow[2:3, :]
            out_ref[s] = (mid_own[s] + mod(5, s) * mlp).astype(BF16)
            grad_out = cot_ref[s].astype(F32)
            dmod[5, s : s + 1, :] = jnp.sum(grad_out * mlp, axis=0, keepdims=True)
            bias[2:3, :] += jnp.sum(d_all[2 * c + s, y].astype(F32), axis=0, keepdims=True)

    @step
    def ln2b():
        gs_dm.arrived()
        for s in range(2):
            d_m = gs_dm.total(s)
            normed, inv = norm(mid_own[s])
            dmod[4, s : s + 1, :] = jnp.sum(d_m * normed, axis=0, keepdims=True)
            dmod[3, s : s + 1, :] = jnp.sum(d_m, axis=0, keepdims=True)
            d_mid = cot_ref[s].astype(F32) + norm_grad(d_m * (1.0 + mod(4, s)), normed, inv)
            dmid_own[s] = d_mid
            d_attn = (mod(2, s) * d_mid).astype(BF16)
            da_all[2 * c + s, y] = d_attn
            dmod[2, s : s + 1, :] = jnp.sum(d_mid * attn_own[s], axis=0, keepdims=True)
            bias[1:2, :] += jnp.sum(d_attn.astype(F32), axis=0, keepdims=True)
        gg_da.begin()

    steps["gr"], steps["gf"] = gg_da.relay, gg_da.finish

    @step
    def attb():
        @pl.loop(0, 4)
        def _(i):
            packed = qkv_all[i]
            d_attn = da_all[i].reshape(rows, width)
            grads = [[], [], []]
            for h in range(hq):
                q, k, v = head_parts(packed, h)
                p = softmax(q, k)
                p_low = p.astype(BF16)
                d_att = dot_nt(d_attn, g_proj[h]).astype(BF16)
                d_p = dot_nt(d_att, v)
                d_s = (p * (d_p - jnp.sum(p * d_p, axis=-1, keepdims=True))).astype(BF16)
                grads[0].append(dot_nn(d_s, k) * head_scale)
                grads[1].append(dot_tn(d_s, q) * head_scale)
                grads[2].append(dot_tn(p_low, d_att))
            d_qkv = jnp.concatenate(grads[0] + grads[1] + grads[2], axis=1).astype(BF16)
            qkv_all[i] = d_qkv
            bias[3:4, 0 : 3 * hw] += jnp.sum(d_qkv.astype(F32), axis=0, keepdims=True)

    @step
    def dam():
        links.left(gs_dm.core_copy)

        @pl.loop(0, 4)
        def _(i):
            res = dot_nt(qkv_all[i], g_qkv[...])
            sum_a[i] = res.astype(BF16).reshape(2, half_len, width)

        gs_da.begin()

    @step
    def wq():
        for copy in ga_qkv.mine:
            links.left(copy)
        outer(
            lambda at: a_all[:, :, :, at], lambda: qkv_all[...].reshape(all_rows, 3 * hw), g_qkv
        )
        sc_qkv.begin()

    @step
    def xr():
        links.left(gs_dm.pair_copy)
        gs_da.relay()

    @step
    def wp():
        for copy in ga_proj.mine:
            links.left(copy)

        @pl.loop(0, hq)
        def _(h):
            value = att_all[h].reshape(all_rows, hd)
            g_proj[h] = dot_tn(value, da_all[...].reshape(all_rows, width)).astype(BF16)

    for letter, scatter in (("E", sc_fc2), ("F", sc_fc1), ("Q", sc_qkv), ("P", sc_proj)):
        for name, fn in scatter.hops().items():
            steps[letter + name] = fn

    def join(scatter, pack, target, index):
        at = sems.take(3)
        keep_copy = pltpu.make_async_copy(pack.at[c], target.at[quarter], local.at[index])

        def begin():
            def store(keep):
                total = keep[...].astype(F32)
                pack[0] = total[:shard].astype(BF16)
                pack[1] = total[shard:].astype(BF16)

            scatter.finish(store)
            links.start(True, pack.at[1 - c], target.at[quarter], at, at, sib)
            links.start(True, pack.at[c], target.at[quarter], at + 1, at + 1, pair)
            links.start(
                True, pack.at[1 - c], target.at[quarter], at + 2, at + 2, dev(z, x, 1 - c, 1 - y)
            )
            keep_copy.start()

        def finish():
            keep_copy.wait()
            links.arrived(True, target.at[2 * y + 1 - c], at, sib)
            links.arrived(True, target.at[2 * (1 - y) + c], at + 1, sib)
            links.arrived(True, target.at[2 * (1 - y) + 1 - c], at + 2, sib)

        return begin, finish

    def spread(source, target, count):
        target[...] = jnp.concatenate(
            [source[k % 4, :, (k // 4) * hd : (k // 4 + 1) * hd] for k in range(4 * count)],
            axis=1,
        )

    steps["EJ"], steps["EG"] = join(sc_fc2, t_fc2, j_fc2, 2)
    steps["FJ"], fc1_joined = join(sc_fc1, t_fc1, j_fc1, 3)
    steps["QJ"], qkv_joined = join(sc_qkv, t_qkv, j_qkv, 4)

    @step
    def FG():
        fc1_joined()
        spread(j_fc1, p_fc1, n_wide)

    @step
    def QG():
        qkv_joined()
        spread(j_qkv, p_qkv, 3 * hq)

    steps["PJ"] = lambda: sc_proj.finish(not_column, on_column)

    @step
    def PK():
        sc_proj.land(on_column, t_proj)
        links.start(on_column, t_proj, t_proj, swap_proj, swap_proj, pair)

    @step
    def PG():
        links.arrived(not_column, t_proj, swap_proj, sib)
        j_proj[...] = t_proj[...]

    @step
    def ln1b():
        gs_da.arrived()
        for s in range(2):
            d_a = gs_da.total(s)
            normed, inv = norm(tok_ref[s].astype(F32))
            dmod[1, s : s + 1, :] = jnp.sum(d_a * normed, axis=0, keepdims=True)
            dmod[0, s : s + 1, :] = jnp.sum(d_a, axis=0, keepdims=True)
            gtok_ref[s] = dmid_own[s] + norm_grad(d_a * (1.0 + mod(1, s)), normed, inv)
        links.start(True, dmod, dm_pair, swap_dm, swap_dm, pair)

    @step
    def t1():
        links.arrived(True, dm_pair, swap_dm, sib)
        for k in range(6):
            dm_low[:, k * width : (k + 1) * width] = (dmod[k] + dm_pair[k]).astype(BF16)
        dm_all[w] = dm_low[...]
        ex_dm.begin(lambda p: dm_low, dm_all)

    @step
    def t2():
        ex_dm.finish()
        res = None
        for k in range(6):
            at = slice(k * width, (k + 1) * width)
            for s in range(n_wide):
                dm_rows[2 * s : 2 * s + 2, :] = dm_all[s, :, at].astype(F32)
            low = dm_rows[...].astype(BF16)
            dmall_ref[:, at] = low
            term = dot_nt(low, wada_ref[:, at])
            res = term if res is None else res + term
        ds_send[...] = jnp.zeros_like(ds_send)
        for s in range(n_wide):
            ds_send[s, :, 0:shard] = res[2 * s : 2 * s + 2, :]
        dsil_ref[w] = ds_send[w]
        ex_ds.begin(lambda p: ds_send.at[p], dsil_ref)

    steps["t3"] = ex_ds.finish

    @step
    def v1():
        v_send[...] = jnp.zeros_like(v_send)
        for s in range(n_wide):
            at = slice(s * hd, (s + 1) * hd)
            v_send[s, pl.ds(c, 1), 0:hd] = bias[0:1, at]
            v_send[s, 2:4, 0:hd] = bias[1:3, at]
        for j in range(hq):
            v_send[2 * j + y, pl.ds(4 + c, 1), 0:hd] = bias[3:4, j * hd : (j + 1) * hd]
            v_send[n_wide // 2 + 2 * j + y, pl.ds(4 + c, 1), 0:hd] = bias[
                3:4, 2 * hw + j * hd : 2 * hw + (j + 1) * hd
            ]
        v_all[w] = v_send[w]
        ex_v.begin(lambda p: v_send.at[p], v_all)

    @step
    def v2():
        ex_v.finish()
        total = v_all[0]
        for s in range(1, n_wide):
            total = total + v_all[s]
        vout_ref[y] = total
        links.start(True, vout_ref.at[y], vout_ref.at[y], swap_v, swap_v, pair)

    steps["v3"] = lambda: links.arrived(True, vout_ref.at[1 - y], swap_v, sib)
    steps["end"] = links.drain

    for name in order:
        steps[name]()


ORDER = (
    "init0", "px", "q0", "h1", "q1", "p0", "init1", "h2", "h3", "ln1", "hb", "q2", "q3",
    "p1", "p2", "e0", "ar", "d0", "f0", "af", "qkv", "p3", "att", "f1", "sr", "dr", "f2",
    "e1", "ln2", "f3", "e2", "e3", "mr", "mf", "fc1", "df", "w2", "ef", "dh", "fc2", "dm",
    "E30", "tr", "w1", "E20", "E21", "E10", "ln2b", "ur", "F30", "E31", "gr", "F31", "F20",
    "gf", "attb", "F10", "wp", "E32", "P30", "dam", "P20", "F21", "wq", "xr", "EJ", "P31",
    "res", "P21", "F32", "P32", "v1", "Q30", "Q20", "P10", "Q31", "Q10", "ln1b", "Q21", "FJ",
    "Q32", "t1", "QJ", "FG", "v2", "PJ", "PK", "v3", "EG", "QG", "t2", "t3", "PG", "end",
)


def fast_device(
    tokens,
    cond,
    timesteps,
    counts,
    w_ada,
    b_ada,
    w_qkv,
    b_qv,
    w_proj,
    b_proj,
    w_fc1,
    b_fc1,
    w_fc2,
    b_fc2,
    cotangent,
):
    slots, half_len, width = tokens.shape
    n_wide = lax.axis_size("wide")
    w, y = lax.axis_index("wide"), lax.axis_index("narrow")
    shard = w_ada.shape[0]
    mlp = w_fc1.shape[1]
    hq = HEADS // 4
    nq = 3 * hq * HEAD_DIM
    rows = slots * half_len
    mq = mlp // 4
    half = w_ada.shape[1] // 2

    cond_vec = cond.astype(F32) + time_features(timesteps, width)
    cond_sig = jax.nn.sigmoid(cond_vec)
    silu = (cond_vec * cond_sig).astype(BF16).astype(F32)
    chunks = jnp.pad(
        silu.reshape(slots, n_wide, shard).transpose(1, 0, 2), ((0, 0), (0, 0), (0, 640 - shard))
    )

    def tile(piece):
        return jnp.pad(piece.astype(F32), ((0, 0), (0, 128 - piece.shape[1])))

    fc1_pieces = lax.dynamic_slice_in_dim(b_fc1.reshape(4, shard), 2 * y, 2, 0)
    vector = jnp.concatenate(
        [
            tile(fc1_pieces),
            tile(jnp.broadcast_to(b_proj, (2, shard))),
            tile(jnp.broadcast_to(b_fc2, (2, shard))),
            tile(b_qv.reshape(2, shard)),
            jnp.zeros((2, 128), F32),
        ],
        axis=1,
    )
    vector = jnp.broadcast_to(vector[None], (n_wide // 2, 2, 640)).reshape(n_wide, 1, 640)
    parcel = jnp.concatenate([chunks, vector, jnp.zeros_like(vector)], axis=1)
    ada_cut = b_ada.shape[0]
    ada_bias = lax.dynamic_update_slice_in_dim(
        jnp.zeros((1, w_ada.shape[1]), F32), b_ada.astype(F32)[None], w * ada_cut, 1
    )
    live = (jnp.arange(slots, dtype=jnp.int32) < counts[0])[:, None, None]
    cot_live = jnp.where(live, cotangent, jnp.zeros_like(cotangent))

    def v16(*shape):
        return pltpu.VMEM(shape, BF16)

    def v32(*shape):
        return pltpu.VMEM(shape, F32)

    two = 2 * shard
    full = (4, 2, half_len, width)
    own = (slots, half_len, width)
    scratch = [
        v16(width, nq), v16(hq, shard, width), v16(width, mq), v16(mq, width), v16(mq, width),
        v16(shard, nq), v16(shard, mq), v16(shard, width),
        v16(shard, nq), v16(shard, mq), v16(shard, width), v16(shard, nq), v16(shard, mq),
        v16(4, two, nq), v16(1, shard, width), v16(4, two, mq), v16(4, two, width),
        v16(5, two, nq), v16(5, shard, width), v16(5, two, mq), v16(5, two, width),
        v16(2, shard, nq), v16(2, shard, mq), v16(2, shard, width), v16(shard, width),
        v16(4, shard, nq), v16(4, shard, mq),
        v16(*full), v16(*full), v16(*full),
        v16(4, rows, nq), v16(hq, 4, rows, HEAD_DIM), v16(*full), v16(4, rows, mq),
        v16(*full), v16(*full),
        v16(2, 2, half_len, width), v16(2, 2, half_len, width),
        v16(*own), v16(*own), v16(*own), v16(*own),
        v32(*own), v32(*own), v32(*own),
        v32(n_wide * slots, 128), v32(n_wide, slots, half), v32(n_wide, slots, half),
        v32(slots, half), v32(2, slots, half), v32(6, slots, width), v32(1, nq), v32(4, width),
        v32(4, width),
        v32(6, slots, width), v32(6, slots, width), v16(slots, 6 * width),
        v16(n_wide, slots, 6 * width), v32(n_wide, 8, 128), v32(n_wide, 8, 128),
        v32(n_wide * slots, width), v32(n_wide, slots, 128),
        pltpu.SemaphoreType.DMA((300,)),
        pltpu.SemaphoreType.DMA((300,)),
        pltpu.SemaphoreType.DMA((5,)),
    ]
    out, gtok, got, dm_all, v_out, d_silu, p_qkv, p_fc1, j_fc2, j_proj = pl.pallas_call(
        functools.partial(block_kernel, ORDER, n_wide),
        out_shape=(
            jax.ShapeDtypeStruct(own, BF16),
            jax.ShapeDtypeStruct(own, F32),
            jax.ShapeDtypeStruct((n_wide, 4, 640), F32),
            jax.ShapeDtypeStruct((n_wide * slots, 6 * width), BF16),
            jax.ShapeDtypeStruct((2, 8, 128), F32),
            jax.ShapeDtypeStruct((n_wide, slots, 128), F32),
            jax.ShapeDtypeStruct(w_qkv.shape, BF16),
            jax.ShapeDtypeStruct(w_fc1.shape, BF16),
            jax.ShapeDtypeStruct((4, shard, width), BF16),
            jax.ShapeDtypeStruct((shard, width), BF16),
        ),
        in_specs=[VMEM_SPEC] * 7 + [HBM_SPEC] * 2,
        out_specs=(VMEM_SPEC,) * 8 + (HBM_SPEC, VMEM_SPEC),
        scratch_shapes=scratch,
        compiler_params=pltpu.CompilerParams(
            collective_id=0, has_side_effects=True, vmem_limit_bytes=VMEM_LIMIT
        ),
    )(
        tokens, cot_live, parcel, w_ada, ada_bias, w_qkv, w_fc1,
        w_fc2.reshape(4, shard, width), w_proj,
    )
    out = jnp.where(live, out, jnp.zeros_like(out))
    silu_cols = got[:, 0:2, :shard].reshape(n_wide * slots, shard).astype(BF16)
    grad_ada = outer_sum(silu_cols, dm_all)
    grad_b_ada = jnp.sum(
        lax.dynamic_slice_in_dim(dm_all, w * ada_cut, ada_cut, 1).astype(F32), axis=0
    )
    d_silu = d_silu[:, :, :shard].transpose(1, 0, 2).reshape(slots, width)
    grad_cond = d_silu * (cond_sig + cond_vec * cond_sig * (1.0 - cond_sig))
    v_sum = (v_out[0] + v_out[1])[:, :shard]
    return (
        out,
        gtok,
        grad_cond,
        grad_ada,
        grad_b_ada,
        p_qkv.astype(F32),
        v_sum[4:6].reshape(-1),
        j_proj.astype(F32),
        v_sum[2],
        p_fc1.astype(F32),
        v_out[:, 0:2, :shard].reshape(-1),
        j_fc2.astype(F32).reshape(w_fc2.shape),
        v_sum[3],
    )


def solution(mesh):
    in_specs = (
        P("wide", "narrow", None),
        P("wide", None),
        P("wide"),
        P("wide"),
        P("wide", None),
        P("wide"),
        P("wide", None),
        P("wide"),
        P("wide", None),
        P("wide"),
        P("wide", None),
        P("wide"),
        P("wide", None),
        P("wide"),
        P("wide", "narrow", None),
    )
    out_specs = (
        P("wide", "narrow", None),
        P("wide", "narrow", None),
        P("wide", None),
        P("wide", None),
        P("wide"),
        P("wide", None),
        P("wide"),
        P("wide", None),
        P("wide"),
        P("wide", None),
        P("wide"),
        P("wide", None),
        P("wide"),
    )
    small = mesh.shape["wide"] == 16 and mesh.shape["narrow"] == 2
    per_device = fast_device if small else on_device
    return jax.shard_map(
        per_device, mesh=mesh, in_specs=in_specs, out_specs=out_specs, check_vma=False
    )
```

```python
import functools
import math

import jax
import jax.numpy as jnp
from jax import lax
from jax.experimental import pallas as pl
from jax.experimental.pallas import tpu as pltpu
from jax.sharding import PartitionSpec as P

HEADS = 16
HEAD_DIM = 72

F32 = jnp.float32
BF16 = jnp.bfloat16
eps_norm = 1e-06


def norm_rows(value):
    center = value - jnp.mean(value, axis=-1, keepdims=True)
    inv_std = lax.rsqrt(jnp.mean(center * center, axis=-1, keepdims=True) + eps_norm)
    return (center * inv_std, inv_std)


def norm_back(grad, normed, inv_std):
    return inv_std * (
        grad
        - jnp.mean(grad, axis=-1, keepdims=True)
        - normed * jnp.mean(grad * normed, axis=-1, keepdims=True)
    )


def gelu_tanh(value):
    return (
        0.5
        * value
        * (1.0 + jnp.tanh(0.7978845608028654 * (value + 0.044715 * value * value * value)))
    )


def gelu_tanh_grad(value):
    inner = 0.7978845608028654 * (value + 0.044715 * value * value * value)
    tan = jnp.tanh(inner)
    slope = 0.7978845608028654 * (1.0 + 3.0 * 0.044715 * value * value)
    return 0.5 * (1.0 + tan) + 0.5 * value * (1.0 - tan * tan) * slope


def time_features(steps, width):
    half_width = width // 2
    freqs = jnp.exp(-math.log(10000.0) * jnp.arange(half_width).astype(F32) / half_width)
    angles = steps.astype(F32)[:, None] * freqs[None, :]
    return jnp.concatenate([jnp.cos(angles), jnp.sin(angles)], axis=-1)


def mm(left, right):
    return jnp.einsum("sk,kn->sn", left, right, preferred_element_type=F32)


def mm_back(grad, weight):
    return jnp.einsum("sn,kn->sk", grad, weight, preferred_element_type=F32)


def outer_sum(left, right):
    return jnp.einsum("sk,sn->kn", left, right, preferred_element_type=F32)


def gather_wide(value, axis=0):
    return lax.all_gather(value, "wide", axis=axis, tiled=True)


def on_device(
    tokens,
    cond,
    timesteps,
    counts,
    w_ada,
    b_ada,
    w_qkv,
    b_qv,
    w_proj,
    b_proj,
    w_fc1,
    b_fc1,
    w_fc2,
    b_fc2,
    cotangent,
):
    slots, half_len, width = tokens.shape
    pair = lax.axis_size("narrow")
    n_wide = lax.axis_size("wide")
    me = lax.axis_index("narrow")
    here = lax.axis_index("wide")
    seq = half_len * pair
    rows = slots * half_len
    all_rows = slots * seq
    wh = width // pair
    heads = HEADS // pair
    mlp = w_fc1.shape[1]
    mh = mlp // pair
    shard = w_ada.shape[0]
    head_scale = 1.0 / math.sqrt(HEAD_DIM)

    qkv_half = lax.dynamic_index_in_dim(
        w_qkv.reshape(-1, 3, pair, wh), me, 2, keepdims=False
    ).reshape(-1, 3 * wh)
    fc1_half = lax.dynamic_index_in_dim(
        w_fc1.reshape(-1, n_wide, pair, mh // n_wide), me, 2, keepdims=False
    ).reshape(-1, mh)
    fc2_half = lax.dynamic_index_in_dim(
        w_fc2.reshape(pair, -1, width), me, 0, keepdims=False
    )

    cond_vec = cond.astype(F32) + time_features(timesteps, width)
    cond_sig = jax.nn.sigmoid(cond_vec)
    silu_low = (cond_vec * cond_sig).astype(BF16)
    silu_all = gather_wide(silu_low)
    silu_cols = lax.dynamic_slice_in_dim(silu_all, here * shard, shard, 1)
    mod_part = jnp.dot(silu_cols, w_ada, preferred_element_type=F32)
    biases = gather_wide(jnp.concatenate([b_ada, b_qv, b_proj, b_fc1, b_fc2])[None])
    cuts = []
    at = 0
    for piece in (b_ada, b_qv, b_proj, b_fc1, b_fc2):
        cuts.append(biases[:, at : at + piece.shape[0]].astype(F32))
        at += piece.shape[0]
    ada_bias, qv_bias, proj_bias, fc1_bias, fc2_bias = [c.reshape(-1) for c in cuts]
    fc1_bias_half = lax.dynamic_index_in_dim(
        fc1_bias.reshape(n_wide, pair, -1), me, 1, keepdims=False
    ).reshape(-1)
    qv_bias_half = lax.dynamic_index_in_dim(qv_bias.reshape(2, pair, wh), me, 1, keepdims=False)

    modulate = lax.psum_scatter(mod_part, "wide", scatter_dimension=0, tiled=True) + ada_bias
    shift_one, scale_one, gate_one, shift_two, scale_two, gate_two = [
        modulate[:, None, i * width : (i + 1) * width] for i in range(6)
    ]

    qkv_w = gather_wide(qkv_half)
    proj_w = gather_wide(w_proj)
    fc1_w = gather_wide(fc1_half)
    fc2_w = gather_wide(fc2_half)

    def both_halves(value):
        value = value.reshape(slots, half_len, -1)
        return lax.all_gather(value, "narrow", axis=1, tiled=True).reshape(all_rows, -1)

    def sum_halves(value):
        value = value.astype(BF16).reshape(slots, seq, -1)
        return (
            lax.psum_scatter(value, "narrow", scatter_dimension=1, tiled=True)
            .astype(F32)
            .reshape(slots, half_len, -1)
        )

    live_slot = (jnp.arange(slots, dtype=jnp.int32) < counts[0]).astype(F32)[:, None, None]
    tok_float = tokens.astype(F32)
    normed_one, inv_one = norm_rows(tok_float)
    a_in = (normed_one * (1.0 + scale_one) + shift_one).astype(BF16).reshape(rows, width)
    a_full = both_halves(a_in)
    qkv = mm(a_full, qkv_w)
    query = (qkv[:, :wh] + qv_bias_half[0]).astype(BF16)
    keys = qkv[:, wh : 2 * wh].astype(BF16)
    values = (qkv[:, 2 * wh :] + qv_bias_half[1]).astype(BF16)

    def to_heads(value):
        return value.reshape(slots, seq, heads, HEAD_DIM)

    query_heads, key_heads, value_heads = to_heads(query), to_heads(keys), to_heads(values)
    scores = (
        jnp.einsum("cqhe,ckhe->chqk", query_heads, key_heads, preferred_element_type=F32)
        * head_scale
    )
    log_total = jax.nn.logsumexp(scores, axis=-1, keepdims=True)
    probs = jnp.exp(scores - log_total)
    probs_low = probs.astype(BF16)
    attended = (
        jnp.einsum("chqk,ckhe->cqhe", probs_low, value_heads, preferred_element_type=F32)
        .astype(BF16)
        .reshape(slots, seq, wh)
    )
    att_own = lax.all_to_all(attended, "narrow", split_axis=1, concat_axis=2, tiled=True)
    att_own = att_own.reshape(rows, width)
    attn_out = (mm(att_own, proj_w) + proj_bias).reshape(slots, half_len, width)
    mid = tok_float + gate_one * attn_out
    normed_two, inv_two = norm_rows(mid)
    m_in = (normed_two * (1.0 + scale_two) + shift_two).astype(BF16).reshape(rows, width)
    m_full = both_halves(m_in)
    hidden = mm(m_full, fc1_w) + fc1_bias_half
    act_low = gelu_tanh(hidden).astype(BF16)
    mlp_out = sum_halves(mm(act_low, fc2_w)) + fc2_bias
    out = (live_slot * (mid + gate_two * mlp_out)).astype(BF16)

    grad_out = live_slot * cotangent.astype(F32)
    d_mlp = (gate_two * grad_out).astype(BF16).reshape(rows, width)
    d_mlp_full = both_halves(d_mlp)
    d_gate_two = jnp.sum(grad_out * mlp_out, axis=1)
    fc2_bias_sum = jnp.sum(d_mlp.astype(F32), axis=0)
    grad_fc2_part = outer_sum(act_low, d_mlp_full)
    d_hidden = (mm_back(d_mlp_full, fc2_w) * gelu_tanh_grad(hidden)).astype(BF16)
    fc1_bias_sum = jnp.sum(d_hidden.astype(F32), axis=0)
    grad_fc1_part = outer_sum(m_full, d_hidden)
    d_m_in = sum_halves(mm_back(d_hidden, fc1_w))
    d_scale_two = jnp.sum(d_m_in * normed_two, axis=1)
    d_shift_two = jnp.sum(d_m_in, axis=1)
    d_mid = grad_out + norm_back(d_m_in * (1.0 + scale_two), normed_two, inv_two)
    d_attn = (gate_one * d_mid).astype(BF16).reshape(rows, width)
    d_gate_one = jnp.sum(d_mid * attn_out, axis=1)
    proj_bias_sum = jnp.sum(d_attn.astype(F32), axis=0)
    grad_proj_part = outer_sum(att_own, d_attn)
    d_att_own = mm_back(d_attn, proj_w).astype(BF16).reshape(slots, half_len, width)
    d_att = lax.all_to_all(d_att_own, "narrow", split_axis=2, concat_axis=1, tiled=True)
    d_att = to_heads(d_att)
    d_probs = jnp.einsum("cqhe,ckhe->chqk", d_att, value_heads, preferred_element_type=F32)
    d_scores = (probs * (d_probs - jnp.sum(probs * d_probs, axis=-1, keepdims=True))).astype(BF16)
    d_query = (
        jnp.einsum("chqk,ckhe->cqhe", d_scores, key_heads, preferred_element_type=F32)
        * head_scale
    ).astype(BF16).reshape(all_rows, wh)
    d_keys = (
        jnp.einsum("chqk,cqhe->ckhe", d_scores, query_heads, preferred_element_type=F32)
        * head_scale
    ).astype(BF16).reshape(all_rows, wh)
    d_values = (
        jnp.einsum("chqk,cqhe->ckhe", probs_low, d_att, preferred_element_type=F32)
        .astype(BF16)
        .reshape(all_rows, wh)
    )
    d_qkv = jnp.concatenate([d_query, d_keys, d_values], axis=-1)
    qv_bias_sum = jnp.stack(
        [jnp.sum(d_query.astype(F32), axis=0), jnp.sum(d_values.astype(F32), axis=0)]
    )
    grad_qkv_part = outer_sum(a_full, d_qkv)
    d_a_in = sum_halves(mm_back(d_qkv, qkv_w))
    d_scale_one = jnp.sum(d_a_in * normed_one, axis=1)
    d_shift_one = jnp.sum(d_a_in, axis=1)
    grad_tokens = d_mid + norm_back(d_a_in * (1.0 + scale_one), normed_one, inv_one)

    d_modulate = jnp.concatenate(
        [d_shift_one, d_scale_one, d_gate_one, d_shift_two, d_scale_two, d_gate_two], axis=-1
    )
    def place(half, shape, axis):
        spread = jnp.zeros(shape, F32)
        return lax.dynamic_update_index_in_dim(spread, half, me, axis)

    qv_sum = place(qv_bias_sum, (2, pair, wh), 1).reshape(n_wide, -1)
    fc1_sum = place(fc1_bias_sum.reshape(n_wide, -1), (n_wide, pair, mh // n_wide), 1).reshape(
        n_wide, -1
    )
    bias_sums = jnp.concatenate(
        [
            qv_sum,
            proj_bias_sum.reshape(n_wide, -1),
            fc1_sum,
            fc2_bias_sum.reshape(n_wide, -1),
        ],
        axis=1,
    )
    bias_own = lax.psum(
        lax.psum_scatter(bias_sums, "wide", scatter_dimension=0, tiled=True), "narrow"
    ).reshape(-1)
    bias_grads = []
    at = 0
    for piece in (b_qv, b_proj, b_fc1, b_fc2):
        bias_grads.append(bias_own[at : at + piece.shape[0]])
        at += piece.shape[0]

    d_mod_low = lax.psum(d_modulate, "narrow").astype(BF16)
    d_mod_all = gather_wide(d_mod_low)
    grad_ada = outer_sum(silu_cols, d_mod_all)
    ada_cut = b_ada.shape[0]
    grad_ada_bias = jnp.sum(
        lax.dynamic_slice_in_dim(d_mod_all, here * ada_cut, ada_cut, 1).astype(F32), axis=0
    )
    d_silu_cols = mm_back(d_mod_all, w_ada)
    d_silu = lax.all_to_all(d_silu_cols, "wide", split_axis=0, concat_axis=1, tiled=True)
    grad_cond = d_silu * (cond_sig + cond_vec * cond_sig * (1.0 - cond_sig))

    def scatter_wide(part):
        return lax.psum_scatter(part.astype(BF16), "wide", scatter_dimension=0, tiled=True)

    def join_pair(piece):
        return lax.all_gather(piece, "narrow", axis=0, tiled=False).astype(F32)

    fc2_own = join_pair(scatter_wide(grad_fc2_part)).reshape(-1, width)
    fc1_own = join_pair(scatter_wide(grad_fc1_part)).reshape(pair, shard, n_wide, -1)
    fc1_own = fc1_own.transpose(1, 2, 0, 3).reshape(shard, mlp)
    proj_own = jnp.sum(join_pair(scatter_wide(grad_proj_part)), axis=0)
    qkv_own = join_pair(scatter_wide(grad_qkv_part)).reshape(pair, shard, 3, wh)
    qkv_own = qkv_own.transpose(1, 2, 0, 3).reshape(shard, 3 * width)

    return (
        out,
        grad_tokens,
        grad_cond,
        grad_ada,
        grad_ada_bias,
        qkv_own,
        bias_grads[0],
        proj_own,
        bias_grads[1],
        fc1_own,
        bias_grads[2],
        fc2_own,
        bias_grads[3],
    )


MESH = pl.DeviceIdType.MESH
NZ = 4
GELU_C = 0.7978845608028654
HBM_SPEC = pl.BlockSpec(memory_space=pl.ANY)
VMEM_SPEC = pl.BlockSpec(memory_space=pltpu.VMEM)
VMEM_LIMIT = 63 << 20


def dot_nn(a, b):
    return lax.dot_general(a, b, (((1,), (0,)), ((), ())), preferred_element_type=F32)


def dot_nt(a, b):
    return lax.dot_general(a, b, (((1,), (1,)), ((), ())), preferred_element_type=F32)


def dot_tn(a, b):
    return lax.dot_general(a, b, (((0,), (0,)), ((), ())), preferred_element_type=F32)


def do_when(cond, fn):
    if cond is True:
        fn()
    else:
        pl.when(cond)(fn)


def both(a, b):
    if a is True:
        return b
    if b is True:
        return a
    return jnp.logical_and(a, b)


def greet(peers):
    barrier = pltpu.get_barrier_semaphore()
    total = 0
    for cond, dev in peers:
        do_when(
            cond,
            lambda dev=dev: pl.semaphore_signal(
                barrier, inc=1, device_id=dev, device_id_type=MESH
            ),
        )
        total = total + (1 if cond is True else cond.astype(jnp.int32))
    pl.semaphore_wait(barrier, total)


class Sems:
    def __init__(self, send, recv):
        self.send, self.recv, self.n = send, recv, 0

    def take(self, count):
        at = self.n
        self.n += count
        return at


class Links:
    def __init__(self, sems):
        self.sems = sems
        self.sent = []

    def copy(self, src, dst, index, dev):
        return pltpu.make_async_remote_copy(
            src_ref=src,
            dst_ref=dst,
            send_sem=self.sems.send.at[index],
            recv_sem=self.sems.recv.at[index],
            device_id=dev,
            device_id_type=MESH,
        )

    def start(self, cond, src, dst, send_index, recv_index, dev):
        copy = pltpu.make_async_remote_copy(
            src_ref=src,
            dst_ref=dst,
            send_sem=self.sems.send.at[send_index],
            recv_sem=self.sems.recv.at[recv_index],
            device_id=dev,
            device_id_type=MESH,
        )
        do_when(cond, copy.start)
        self.sent.append((cond, copy))
        return copy

    def arrived(self, cond, ref, index, dev):
        copy = self.copy(ref, ref, index, dev)
        do_when(cond, copy.wait_recv)

    def left(self, copy):
        for cond, one in self.sent:
            if one is copy:
                do_when(cond, one.wait_send)
        self.sent = [entry for entry in self.sent if entry[1] is not copy]

    def drain(self):
        for cond, copy in self.sent:
            do_when(cond, copy.wait_send)
        self.sent = []


class Gather:
    def __init__(self, links, pos, block, source, sink):
        self.links, self.pos, self.block = links, pos, block
        self.source, self.sink = source, sink
        take = links.sems.take
        self.z_at, self.x_at, self.up_at, self.down_at = take(4), take(4), take(4), take(4)
        self.mine = []

    def along_z(self, cond, s, up, down):
        z, x, c, y = self.pos["z"], self.pos["x"], self.pos["c"], self.pos["y"]
        ref = self.block(s, x)
        for wanted, inside, at, to in (
            (up, z < NZ - 1, self.up_at, z + 1),
            (down, z > 0, self.down_at, z - 1),
        ):
            if wanted:
                self.mine.append(
                    self.links.start(
                        both(cond, inside), ref, ref, at + s, self.z_at + s,
                        self.pos["dev"](to, x, c, y),
                    )
                )

    def forward(self, cond, s, up, down):
        z, x, c, y = self.pos["z"], self.pos["x"], self.pos["c"], self.pos["y"]
        self.along_z(cond, s, up, down)
        ref = self.block(s, x)
        self.mine.append(
            self.links.start(
                cond, ref, ref, self.x_at + s, self.x_at + s, self.pos["dev"](z, 1 - x, c, y)
            )
        )

    def own(self):
        self.forward(self.source, self.pos["z"], True, True)

    def step(self, d):
        z, x = self.pos["z"], self.pos["x"]
        cond = both(self.source, z >= d)
        s = jnp.maximum(z - d, 0)
        self.links.arrived(cond, self.block(s, x), self.z_at + s, self.pos["me"])
        self.forward(cond, s, True, False)
        cond = both(self.source, z <= NZ - 1 - d)
        s = jnp.minimum(z + d, NZ - 1)
        self.links.arrived(cond, self.block(s, x), self.z_at + s, self.pos["me"])
        self.forward(cond, s, False, True)

    def finish(self):
        x = self.pos["x"]
        for s in range(NZ):
            self.links.arrived(self.sink, self.block(s, 1 - x), self.x_at + s, self.pos["me"])


class GatherAcross(Gather):
    def __init__(self, links, pos, block, on_column, not_column):
        super().__init__(links, pos, block, True, True)
        self.on_column, self.not_column = on_column, not_column

    def forward(self, cond, s, up, down):
        self.along_z(cond, s, up, down)

    def across(self):
        z, x, c, y = self.pos["z"], self.pos["x"], self.pos["c"], self.pos["y"]
        ref = self.block(z, x)
        self.mine.append(
            self.links.start(
                self.on_column, ref, ref, self.x_at, self.x_at, self.pos["dev"](z, 1 - x, c, y)
            )
        )

    def own(self):
        z, x = self.pos["z"], self.pos["x"]
        self.links.arrived(self.not_column, self.block(z, x), self.x_at, self.pos["me"])
        self.forward(True, z, True, True)

    def finish(self):
        pass


class Scatter:
    def __init__(self, links, pos, block, sums_x, sums_z, source, sink):
        self.links, self.pos, self.block = links, pos, block
        self.sums_x, self.sums_z = sums_x, sums_z
        self.source, self.sink = source, sink
        take = links.sems.take
        self.x_at, self.z_at, self.up_at, self.down_at = take(4), take(5), take(4), take(4)

    def begin(self):
        z, x, c, y = self.pos["z"], self.pos["x"], self.pos["c"], self.pos["y"]
        far = jnp.where(z < 2, 3, 0)
        middle = jnp.where(z == 0, 2, jnp.where(z == 3, 1, 3 - far))
        near = jnp.where(z % 2 == 0, 1, 2)
        for s in (far, middle, near, z):
            self.links.start(
                self.source, self.block(s, 1 - x), self.sums_x.at[s], self.x_at + s,
                self.x_at + s, self.pos["dev"](z, 1 - x, c, y),
            )

    def add_x(self, s):
        self.links.arrived(True, self.sums_x.at[s], self.x_at + s, self.pos["me"])
        return self.block(s, self.pos["x"])[...].astype(F32) + self.sums_x[s].astype(F32)

    def hop(self, here, s, up):
        z, x, c, y = self.pos["z"], self.pos["x"], self.pos["c"], self.pos["y"]
        first = here == (0 if up else NZ - 1)
        ref = self.block(s, x)

        def run():
            total = self.add_x(s)
            if not first:
                self.links.arrived(True, self.sums_z.at[s], self.z_at + s, self.pos["me"])
                total = total + self.sums_z[s].astype(F32)
            ref[...] = total.astype(BF16)

        cond = z == here
        do_when(cond, run)
        to = here + 1 if up else here - 1
        slot = 4 if s == to and not up else s
        at = (self.up_at if up else self.down_at) + s
        self.links.start(
            cond, ref, self.sums_z.at[slot], at, self.z_at + slot, self.pos["dev"](to, x, c, y)
        )

    def finish(self, store):
        z, x = self.pos["z"], self.pos["x"]
        keep = self.block(z, x)

        def run():
            total = keep[...].astype(F32)
            self.links.arrived(True, self.sums_x.at[z], self.x_at + z, self.pos["me"])
            total = total + self.sums_x[z].astype(F32)
            keep[...] = total.astype(BF16)

            @pl.when(z > 0)
            def _():
                self.links.arrived(True, self.sums_z.at[z], self.z_at + z, self.pos["me"])
                keep[...] = (keep[...].astype(F32) + self.sums_z[z].astype(F32)).astype(BF16)

            @pl.when(z < NZ - 1)
            def _():
                self.links.arrived(True, self.sums_z.at[4], self.z_at + 4, self.pos["me"])
                keep[...] = (keep[...].astype(F32) + self.sums_z[4].astype(F32)).astype(BF16)

            store(keep)

        do_when(self.sink, run)

    def hops(self):
        out = {}
        for here in range(NZ - 1):
            for s in range(here + 1, NZ):

                def both_ways(here=here, s=s):
                    self.hop(here, s, True)
                    self.hop(NZ - 1 - here, NZ - 1 - s, False)

                out[str(s) + str(here)] = both_ways
        return out


class ScatterAcross(Scatter):
    def begin(self):
        pass

    def add_x(self, s):
        return self.block(s, self.pos["x"])[...].astype(F32)

    def finish(self, not_column, on_column):
        z, x, c, y = self.pos["z"], self.pos["x"], self.pos["c"], self.pos["y"]
        keep = self.block(z, x)

        @pl.when(z > 0)
        def _():
            self.links.arrived(True, self.sums_z.at[z], self.z_at + z, self.pos["me"])
            keep[...] = (keep[...].astype(F32) + self.sums_z[z].astype(F32)).astype(BF16)

        @pl.when(z < NZ - 1)
        def _():
            self.links.arrived(True, self.sums_z.at[4], self.z_at + 4, self.pos["me"])
            keep[...] = (keep[...].astype(F32) + self.sums_z[4].astype(F32)).astype(BF16)

        self.links.start(
            not_column, keep, self.sums_x.at[0], self.x_at, self.x_at,
            self.pos["dev"](z, 1 - x, c, y),
        )

    def land(self, on_column, target):
        keep = self.block(self.pos["z"], self.pos["x"])

        @pl.when(on_column)
        def _():
            self.links.arrived(True, self.sums_x.at[0], self.x_at, self.pos["me"])
            target[...] = (keep[...].astype(F32) + self.sums_x[0].astype(F32)).astype(BF16)


class PlaneExchange:
    def __init__(self, links, n_wide, w, y):
        self.links, self.n_wide, self.w, self.y = links, n_wide, w, y
        self.at = links.sems.take(n_wide)

    def begin(self, source, target):
        self.copies = []
        for k in range(1, self.n_wide):
            peer = lax.rem(self.w + k, self.n_wide)
            self.copies.append(
                self.links.start(
                    True, source(peer), target.at[self.w], self.at + k, self.at + k,
                    (peer, self.y),
                )
            )

    def finish(self):
        for copy in self.copies:
            copy.wait_recv()


class GroupGather:
    def __init__(self, links, pos, full):
        self.links, self.pos, self.full = links, pos, full
        self.at = links.sems.take(3)

    def begin(self):
        z, x, c, y = self.pos["z"], self.pos["x"], self.pos["c"], self.pos["y"]
        ref = self.full.at[pl.ds(2 * c, 2), y]
        self.links.start(True, ref, ref, self.at, self.at, self.pos["dev"](z, x, c, 1 - y))
        self.links.start(True, ref, ref, self.at + 1, self.at + 1, self.pos["dev"](z, x, 1 - c, y))

    def relay(self):
        z, x, c, y = self.pos["z"], self.pos["x"], self.pos["c"], self.pos["y"]
        ref = self.full.at[pl.ds(2 * c, 2), 1 - y]
        self.links.arrived(True, ref, self.at, self.pos["me"])
        self.links.start(True, ref, ref, self.at + 2, self.at + 2, self.pos["dev"](z, x, 1 - c, y))

    def finish(self):
        c, y = self.pos["c"], self.pos["y"]
        other = pl.ds(2 * (1 - c), 2)
        self.links.arrived(True, self.full.at[other, y], self.at + 1, self.pos["me"])
        self.links.arrived(True, self.full.at[other, 1 - y], self.at + 2, self.pos["me"])


class GroupSum:
    def __init__(self, links, pos, full, from_core, to_pair, from_pair):
        self.links, self.pos, self.full = links, pos, full
        self.from_core, self.to_pair, self.from_pair = from_core, to_pair, from_pair
        self.at = links.sems.take(2)

    def begin(self):
        z, x, c, y = self.pos["z"], self.pos["x"], self.pos["c"], self.pos["y"]
        self.core_copy = self.links.start(
            True, self.full.at[pl.ds(2 * (1 - c), 2)], self.from_core, self.at, self.at,
            self.pos["dev"](z, x, 1 - c, y),
        )

    def relay(self):
        z, x, c, y = self.pos["z"], self.pos["x"], self.pos["c"], self.pos["y"]
        self.links.arrived(True, self.from_core, self.at, self.pos["me"])
        for s in range(2):
            self.to_pair[s] = (
                self.full[2 * c + s, 1 - y].astype(F32) + self.from_core[s, 1 - y].astype(F32)
            ).astype(BF16)
        self.pair_copy = self.links.start(
            True, self.to_pair, self.from_pair, self.at + 1, self.at + 1,
            self.pos["dev"](z, x, c, 1 - y),
        )

    def arrived(self):
        self.links.arrived(True, self.from_pair, self.at + 1, self.pos["me"])

    def total(self, s):
        c, y = self.pos["c"], self.pos["y"]
        return (
            self.full[2 * c + s, y].astype(F32)
            + self.from_core[s, y].astype(F32)
            + self.from_pair[s].astype(F32)
        )


def gelu_both(u):
    inner = GELU_C * (u + 0.044715 * u * u * u)
    tan = jnp.tanh(inner)
    slope = GELU_C * (1.0 + 3.0 * 0.044715 * u * u)
    act = 0.5 * u * (1.0 + tan)
    grad = 0.5 * (1.0 + tan) + 0.5 * u * (1.0 - tan * tan) * slope
    return act, grad


def block_kernel(
    order, n_wide,
    tok_ref, cot_ref, parcel_ref, wada_ref, bada_ref,
    wqkv_ref, wfc1_ref, src_fc2, src_proj,
    out_ref, gtok_ref, got_ref, dmall_ref, vout_ref, dsil_ref,
    p_qkv, p_fc1, j_fc2, j_proj,
    g_qkv, g_proj, g_fc1, g_fc2, w_fc2,
    i_qkv, i_fc1, i_fc2, own_qkv, own_fc1, own_fc2, o_qkv, o_fc1,
    x_qkv, x_proj, x_fc1, x_fc2, z_qkv, z_proj, z_fc1, z_fc2,
    t_qkv, t_fc1, t_fc2, t_proj, j_qkv, j_fc1,
    a_all, m_all, d_all, qkv_all, att_all, act_all, gp_all,
    sum_a, sum_b, core_a, core_b, to_a, to_b, from_a, from_b,
    attn_own, mid_own, dmid_own,
    left, part, parts, tot, modh, mods, bqkv, brow, bias,
    dmod, dm_pair, dm_low, dm_all, v_send, v_all, dm_rows, ds_send,
    send, recv, local,
):
    w, y = lax.axis_index("wide"), lax.axis_index("narrow")
    z, x, c = w // 4, (w // 2) % 2, w % 2
    chip = 2 * z + x
    quarter = 2 * y + c

    def dev(z, x, c, y):
        return ((z * 2 + x) * 2 + c, y)

    sib, pair = dev(z, x, 1 - c, y), dev(z, x, c, 1 - y)
    pos = {"z": z, "x": x, "c": c, "y": y, "dev": dev, "me": sib}
    links = Links(Sems(send, recv))
    sems = links.sems
    half_len = tok_ref.shape[1]
    width = tok_ref.shape[2]
    hd = HEAD_DIM
    hq = g_proj.shape[0]
    hw = hd * hq
    shard = own_qkv.shape[0]
    rows2 = 2 * shard
    rows = 2 * half_len
    all_rows = 4 * rows
    half = modh.shape[2]
    head_scale = 1.0 / math.sqrt(HEAD_DIM)
    da_all = act_all

    greet(
        [(True, (lax.rem(w + k, n_wide), y)) for k in range(1, n_wide)]
        + [(True, pair), (True, dev(z, x, 1 - c, 1 - y))]
    )

    def rows_of(full):
        return lambda s, xx: full.at[pl.ds(pl.multiple_of((2 * s + xx) * rows2, 16), rows2), :]

    def head_of(s, xx):
        return g_proj.at[s]

    on_column = x == y
    not_column = jnp.logical_not(on_column)
    init = sems.take(3)
    ga_qkv = Gather(links, pos, rows_of(g_qkv), True, True)
    ga_proj = GatherAcross(links, pos, head_of, on_column, not_column)
    ga_fc1 = Gather(links, pos, rows_of(g_fc1), True, True)
    ga_fc2 = Gather(links, pos, rows_of(g_fc2), True, True)
    gg_a = GroupGather(links, pos, a_all)
    gg_d = GroupGather(links, pos, d_all)
    gg_m = GroupGather(links, pos, m_all)
    gg_da = GroupGather(links, pos, da_all)
    gs_attn = GroupSum(links, pos, sum_a, core_a, to_a, from_a)
    gs_mlp = GroupSum(links, pos, sum_b, core_b, to_b, from_b)
    gs_dm = GroupSum(links, pos, sum_a, core_a, to_a, from_a)
    gs_da = GroupSum(links, pos, sum_a, core_a, to_a, from_a)
    sc_fc2 = Scatter(links, pos, rows_of(w_fc2), x_fc2, z_fc2, True, True)
    sc_fc1 = Scatter(links, pos, rows_of(g_fc2), x_fc1, z_fc1, True, True)
    sc_qkv = Scatter(links, pos, rows_of(g_qkv), x_qkv, z_qkv, True, True)
    sc_proj = ScatterAcross(links, pos, head_of, x_proj, z_proj, True, True)
    ex_head = PlaneExchange(links, n_wide, w, y)
    ex_mod = PlaneExchange(links, n_wide, w, y)
    ex_dm = PlaneExchange(links, n_wide, w, y)
    ex_v = PlaneExchange(links, n_wide, w, y)
    ex_ds = PlaneExchange(links, n_wide, w, y)
    swap_mod, swap_dm, swap_v, swap_proj = sems.take(1), sems.take(1), sems.take(1), sems.take(1)
    steps = {}

    def step(fn):
        steps[fn.__name__] = fn
        return fn

    def norm(value):
        center = value - jnp.mean(value, axis=-1, keepdims=True)
        inv = lax.rsqrt(jnp.mean(center * center, axis=-1, keepdims=True) + eps_norm)
        return center * inv, inv

    def norm_grad(grad, normed, inv):
        return inv * (
            grad
            - jnp.mean(grad, axis=-1, keepdims=True)
            - normed * jnp.mean(grad * normed, axis=-1, keepdims=True)
        )

    def mod(k, s):
        return mods[k, s : s + 1, :]

    def pick(source, count, which):
        return jnp.concatenate(
            [source[:, (4 * j + which) * hd : (4 * j + which + 1) * hd] for j in range(count)],
            axis=1,
        )

    fc2_copy = pltpu.make_async_copy(src_fc2.at[quarter], own_fc2, local.at[0])
    proj_copy = pltpu.make_async_copy(src_proj, g_proj.at[z], local.at[1])

    @step
    def init0():
        fc2_copy.start()
        do_when(on_column, proj_copy.start)
        ex_head.begin(lambda p: parcel_ref.at[p], got_ref)
        got_ref[w] = parcel_ref[w]
        value = wqkv_ref[...]
        for q in range(4):

            @pl.when(quarter == q)
            def _():
                own_qkv[...] = pick(value, 3 * hq, q)

            @pl.when(2 * y + 1 - c == q)
            def _():
                o_qkv[...] = pick(value, 3 * hq, q)

        links.start(True, o_qkv, i_qkv, init, init, sib)

    @step
    def init1():
        links.start(True, src_fc2.at[2 * y + 1 - c], i_fc2, init + 2, init + 2, sib)
        value = wfc1_ref[...]
        for q in range(4):

            @pl.when(quarter == q)
            def _():
                own_fc1[...] = pick(value, n_wide, q)

            @pl.when(2 * y + 1 - c == q)
            def _():
                o_fc1[...] = pick(value, n_wide, q)

        links.start(True, o_fc1, i_fc1, init + 1, init + 1, sib)

    def place(own, inbox, full, index):
        links.arrived(True, inbox, init + index, sib)
        mine, other = own[...].astype(F32), inbox[...].astype(F32)
        first = jnp.where(c == 0, mine, other)
        second = jnp.where(c == 0, other, mine)
        at = pl.ds(pl.multiple_of(chip * rows2, 16), rows2)
        full[at, :] = jnp.concatenate([first, second], axis=0).astype(BF16)

    @step
    def q0():
        place(own_qkv, i_qkv, g_qkv, 0)
        ga_qkv.own()

    @step
    def f0():
        place(own_fc1, i_fc1, g_fc1, 1)
        ga_fc1.own()

    @step
    def e0():
        fc2_copy.wait()
        place(own_fc2, i_fc2, g_fc2, 2)
        ga_fc2.own()

    @step
    def px():
        do_when(on_column, proj_copy.wait)
        ga_proj.across()

    steps["p0"] = ga_proj.own
    for letter, gather in (("q", ga_qkv), ("p", ga_proj), ("f", ga_fc1), ("e", ga_fc2)):
        for d in range(1, NZ):
            steps[letter + str(d)] = lambda gather=gather, d=d: gather.step(d)

    @step
    def h1():
        ex_head.finish()
        for s in range(n_wide):
            left[2 * s : 2 * s + 2, :] = got_ref[s, 0:2, 0:128]
        lhs = left[...][:, :shard].astype(BF16)
        cols = pl.ds(pl.multiple_of(y * half, 128), half)
        res = dot_nn(lhs, wada_ref[:, cols]) + bada_ref[:, cols]
        for s in range(n_wide):
            part[s] = res[2 * s : 2 * s + 2, :]
        parts[w] = part[w]
        ex_mod.begin(lambda p: part.at[p], parts)

    @step
    def hb():
        def row(lane, owners):
            return jnp.concatenate([got_ref[o, 2:3, lane : lane + hd] for o in owners], axis=1)

        every = range(n_wide)
        brow[0:1, :] = row(0, every)
        brow[1:2, :] = row(128, every)
        brow[2:3, :] = row(256, every)
        bqkv[...] = jnp.concatenate(
            [
                row(384, [2 * j + y for j in range(hq)]),
                jnp.zeros((1, hw), F32),
                row(384, [n_wide // 2 + 2 * j + y for j in range(hq)]),
            ],
            axis=1,
        )

    @step
    def h2():
        ex_mod.finish()
        total = parts[0]
        for s in range(1, n_wide):
            total = total + parts[s]
        tot[...] = total
        modh[y] = total
        links.start(True, tot, modh.at[y], swap_mod, swap_mod, pair)

    @step
    def h3():
        links.arrived(True, modh.at[1 - y], swap_mod, sib)
        for k in range(6):
            at = (k % 3) * width
            mods[k] = modh[k // 3, :, at : at + width]

    @step
    def ln1():
        for s in range(2):
            normed, inv = norm(tok_ref[s].astype(F32))
            a_all[2 * c + s, y] = (normed * (1.0 + mod(1, s)) + mod(0, s)).astype(BF16)
        gg_a.begin()

    steps["ar"], steps["af"] = gg_a.relay, gg_a.finish

    @step
    def d0():
        for s in range(2):
            d_all[2 * c + s, y] = (mod(5, s) * cot_ref[s].astype(F32)).astype(BF16)
        gg_d.begin()

    steps["dr"], steps["df"] = gg_d.relay, gg_d.finish

    @step
    def qkv():
        ga_qkv.finish()

        @pl.loop(0, 4)
        def _(i):
            res = dot_nn(a_all[i].reshape(rows, width), g_qkv[...]) + bqkv[...]
            qkv_all[i] = res.astype(BF16)

    def head_parts(packed, h):
        return [packed[:, t * hw + h * hd : t * hw + (h + 1) * hd] for t in range(3)]

    def softmax(q, k):
        scores = dot_nt(q, k) * head_scale
        top = jnp.max(scores, axis=-1, keepdims=True)
        e = jnp.exp(scores - top)
        return e * (1.0 / jnp.sum(e, axis=-1, keepdims=True))

    @step
    def att():
        @pl.loop(0, 4)
        def _(i):
            packed = qkv_all[i]
            acc = None
            for h in range(hq):
                q, k, v = head_parts(packed, h)
                p = softmax(q, k).astype(BF16)
                o = dot_nn(p, v).astype(BF16)
                att_all[h, i] = o
                term = dot_nn(o, g_proj[h])
                acc = term if acc is None else acc + term
            sum_a[i] = acc.astype(BF16).reshape(2, half_len, width)

        gs_attn.begin()

    steps["sr"] = gs_attn.relay

    @step
    def ln2():
        gs_attn.arrived()
        for s in range(2):
            attn = gs_attn.total(s) + brow[1:2, :]
            attn_own[s] = attn
            mid = tok_ref[s].astype(F32) + mod(2, s) * attn
            mid_own[s] = mid
            normed, inv = norm(mid)
            m_all[2 * c + s, y] = (normed * (1.0 + mod(4, s)) + mod(3, s)).astype(BF16)
        gg_m.begin()

    steps["mr"], steps["mf"] = gg_m.relay, gg_m.finish

    @step
    def fc1():
        ga_fc1.finish()

        @pl.loop(0, 4)
        def _(i):
            u = dot_nn(m_all[i].reshape(rows, width), g_fc1[...]) + brow[0:1, :]
            act, grad = gelu_both(u)
            act_all[i] = act.astype(BF16).reshape(2, half_len, width)
            gp_all[i] = grad.astype(BF16)

    steps["ef"] = ga_fc2.finish

    @step
    def fc2():
        @pl.loop(0, 4)
        def _(i):
            res = dot_nn(act_all[i].reshape(rows, width), g_fc2[...])
            sum_b[i] = res.astype(BF16).reshape(2, half_len, width)

        gs_mlp.begin()

    steps["ur"] = gs_mlp.relay

    def outer(left, right, full):
        lanes = width // 3

        @pl.loop(0, 3)
        def _(j):
            at = pl.ds(pl.multiple_of(j * lanes, 128), lanes)
            full[at, :] = dot_tn(left(at).reshape(all_rows, lanes), right()).astype(BF16)

    @step
    def w2():
        outer(
            lambda at: act_all[:, :, :, at], lambda: d_all[...].reshape(all_rows, width), w_fc2
        )
        sc_fc2.begin()

    @step
    def dh():
        bias[...] = jnp.zeros_like(bias)

        @pl.loop(0, 4)
        def _(i):
            d_act = dot_nt(d_all[i].reshape(rows, width), g_fc2[...])
            d_hidden = (d_act * gp_all[i].astype(F32)).astype(BF16)
            gp_all[i] = d_hidden
            bias[0:1, :] += jnp.sum(d_hidden.astype(F32), axis=0, keepdims=True)

    @step
    def dm():
        links.left(gs_attn.core_copy)

        @pl.loop(0, 4)
        def _(i):
            res = dot_nt(gp_all[i], g_fc1[...])
            sum_a[i] = res.astype(BF16).reshape(2, half_len, width)

        gs_dm.begin()

    @step
    def w1():
        for copy in ga_fc2.mine:
            links.left(copy)
        outer(
            lambda at: m_all[:, :, :, at], lambda: gp_all[...].reshape(all_rows, width), g_fc2
        )
        sc_fc1.begin()

    @step
    def tr():
        links.left(gs_attn.pair_copy)
        gs_dm.relay()

    @step
    def res():
        gs_mlp.arrived()
        for s in range(2):
            mlp = gs_mlp.total(s) + brow[2:3, :]
            out_ref[s] = (mid_own[s] + mod(5, s) * mlp).astype(BF16)
            grad_out = cot_ref[s].astype(F32)
            dmod[5, s : s + 1, :] = jnp.sum(grad_out * mlp, axis=0, keepdims=True)
            bias[2:3, :] += jnp.sum(d_all[2 * c + s, y].astype(F32), axis=0, keepdims=True)

    @step
    def ln2b():
        gs_dm.arrived()
        for s in range(2):
            d_m = gs_dm.total(s)
            normed, inv = norm(mid_own[s])
            dmod[4, s : s + 1, :] = jnp.sum(d_m * normed, axis=0, keepdims=True)
            dmod[3, s : s + 1, :] = jnp.sum(d_m, axis=0, keepdims=True)
            d_mid = cot_ref[s].astype(F32) + norm_grad(d_m * (1.0 + mod(4, s)), normed, inv)
            dmid_own[s] = d_mid
            d_attn = (mod(2, s) * d_mid).astype(BF16)
            da_all[2 * c + s, y] = d_attn
            dmod[2, s : s + 1, :] = jnp.sum(d_mid * attn_own[s], axis=0, keepdims=True)
            bias[1:2, :] += jnp.sum(d_attn.astype(F32), axis=0, keepdims=True)
        gg_da.begin()

    steps["gr"], steps["gf"] = gg_da.relay, gg_da.finish

    @step
    def attb():
        @pl.loop(0, 4)
        def _(i):
            packed = qkv_all[i]
            d_attn = da_all[i].reshape(rows, width)
            grads = [[], [], []]
            for h in range(hq):
                q, k, v = head_parts(packed, h)
                p = softmax(q, k)
                p_low = p.astype(BF16)
                d_att = dot_nt(d_attn, g_proj[h]).astype(BF16)
                d_p = dot_nt(d_att, v)
                d_s = (p * (d_p - jnp.sum(p * d_p, axis=-1, keepdims=True))).astype(BF16)
                grads[0].append(dot_nn(d_s, k) * head_scale)
                grads[1].append(dot_tn(d_s, q) * head_scale)
                grads[2].append(dot_tn(p_low, d_att))
            d_qkv = jnp.concatenate(grads[0] + grads[1] + grads[2], axis=1).astype(BF16)
            qkv_all[i] = d_qkv
            bias[3:4, 0 : 3 * hw] += jnp.sum(d_qkv.astype(F32), axis=0, keepdims=True)

    @step
    def dam():
        links.left(gs_dm.core_copy)

        @pl.loop(0, 4)
        def _(i):
            res = dot_nt(qkv_all[i], g_qkv[...])
            sum_a[i] = res.astype(BF16).reshape(2, half_len, width)

        gs_da.begin()

    @step
    def wq():
        for copy in ga_qkv.mine:
            links.left(copy)
        outer(
            lambda at: a_all[:, :, :, at], lambda: qkv_all[...].reshape(all_rows, 3 * hw), g_qkv
        )
        sc_qkv.begin()

    @step
    def xr():
        links.left(gs_dm.pair_copy)
        gs_da.relay()

    @step
    def wp():
        for copy in ga_proj.mine:
            links.left(copy)

        @pl.loop(0, hq)
        def _(h):
            value = att_all[h].reshape(all_rows, hd)
            g_proj[h] = dot_tn(value, da_all[...].reshape(all_rows, width)).astype(BF16)

    for letter, scatter in (("E", sc_fc2), ("F", sc_fc1), ("Q", sc_qkv), ("P", sc_proj)):
        for name, fn in scatter.hops().items():
            steps[letter + name] = fn

    def join(scatter, pack, target, index):
        at = sems.take(3)
        keep_copy = pltpu.make_async_copy(pack.at[c], target.at[quarter], local.at[index])

        def begin():
            def store(keep):
                total = keep[...].astype(F32)
                pack[0] = total[:shard].astype(BF16)
                pack[1] = total[shard:].astype(BF16)

            scatter.finish(store)
            links.start(True, pack.at[1 - c], target.at[quarter], at, at, sib)
            links.start(True, pack.at[c], target.at[quarter], at + 1, at + 1, pair)
            links.start(
                True, pack.at[1 - c], target.at[quarter], at + 2, at + 2, dev(z, x, 1 - c, 1 - y)
            )
            keep_copy.start()

        def finish():
            keep_copy.wait()
            links.arrived(True, target.at[2 * y + 1 - c], at, sib)
            links.arrived(True, target.at[2 * (1 - y) + c], at + 1, sib)
            links.arrived(True, target.at[2 * (1 - y) + 1 - c], at + 2, sib)

        return begin, finish

    def spread(source, target, count):
        target[...] = jnp.concatenate(
            [source[k % 4, :, (k // 4) * hd : (k // 4 + 1) * hd] for k in range(4 * count)],
            axis=1,
        )

    steps["EJ"], steps["EG"] = join(sc_fc2, t_fc2, j_fc2, 2)
    steps["FJ"], fc1_joined = join(sc_fc1, t_fc1, j_fc1, 3)
    steps["QJ"], qkv_joined = join(sc_qkv, t_qkv, j_qkv, 4)

    @step
    def FG():
        fc1_joined()
        spread(j_fc1, p_fc1, n_wide)

    @step
    def QG():
        qkv_joined()
        spread(j_qkv, p_qkv, 3 * hq)

    steps["PJ"] = lambda: sc_proj.finish(not_column, on_column)

    @step
    def PK():
        sc_proj.land(on_column, t_proj)
        links.start(on_column, t_proj, t_proj, swap_proj, swap_proj, pair)

    @step
    def PG():
        links.arrived(not_column, t_proj, swap_proj, sib)
        j_proj[...] = t_proj[...]

    @step
    def ln1b():
        gs_da.arrived()
        for s in range(2):
            d_a = gs_da.total(s)
            normed, inv = norm(tok_ref[s].astype(F32))
            dmod[1, s : s + 1, :] = jnp.sum(d_a * normed, axis=0, keepdims=True)
            dmod[0, s : s + 1, :] = jnp.sum(d_a, axis=0, keepdims=True)
            gtok_ref[s] = dmid_own[s] + norm_grad(d_a * (1.0 + mod(1, s)), normed, inv)
        links.start(True, dmod, dm_pair, swap_dm, swap_dm, pair)

    @step
    def t1():
        links.arrived(True, dm_pair, swap_dm, sib)
        for k in range(6):
            dm_low[:, k * width : (k + 1) * width] = (dmod[k] + dm_pair[k]).astype(BF16)
        dm_all[w] = dm_low[...]
        ex_dm.begin(lambda p: dm_low, dm_all)

    @step
    def t2():
        ex_dm.finish()
        res = None
        for k in range(6):
            at = slice(k * width, (k + 1) * width)
            for s in range(n_wide):
                dm_rows[2 * s : 2 * s + 2, :] = dm_all[s, :, at].astype(F32)
            low = dm_rows[...].astype(BF16)
            dmall_ref[:, at] = low
            term = dot_nt(low, wada_ref[:, at])
            res = term if res is None else res + term
        ds_send[...] = jnp.zeros_like(ds_send)
        for s in range(n_wide):
            ds_send[s, :, 0:shard] = res[2 * s : 2 * s + 2, :]
        dsil_ref[w] = ds_send[w]
        ex_ds.begin(lambda p: ds_send.at[p], dsil_ref)

    steps["t3"] = ex_ds.finish

    @step
    def v1():
        v_send[...] = jnp.zeros_like(v_send)
        for s in range(n_wide):
            at = slice(s * hd, (s + 1) * hd)
            v_send[s, pl.ds(c, 1), 0:hd] = bias[0:1, at]
            v_send[s, 2:4, 0:hd] = bias[1:3, at]
        for j in range(hq):
            v_send[2 * j + y, pl.ds(4 + c, 1), 0:hd] = bias[3:4, j * hd : (j + 1) * hd]
            v_send[n_wide // 2 + 2 * j + y, pl.ds(4 + c, 1), 0:hd] = bias[
                3:4, 2 * hw + j * hd : 2 * hw + (j + 1) * hd
            ]
        v_all[w] = v_send[w]
        ex_v.begin(lambda p: v_send.at[p], v_all)

    @step
    def v2():
        ex_v.finish()
        total = v_all[0]
        for s in range(1, n_wide):
            total = total + v_all[s]
        vout_ref[y] = total
        links.start(True, vout_ref.at[y], vout_ref.at[y], swap_v, swap_v, pair)

    steps["v3"] = lambda: links.arrived(True, vout_ref.at[1 - y], swap_v, sib)
    steps["end"] = links.drain

    for name in order:
        steps[name]()


def finish_kernel(*refs):
    count = (len(refs) - 3) // 2
    for source, target in zip(refs[:count], refs[count + 2 : 2 * count + 2]):
        target[...] = source[...].astype(target.dtype).reshape(target.shape)
    left, right, product = refs[count], refs[count + 1], refs[-1]
    shard = product.shape[0]
    product[...] = dot_tn(left[...][:, :shard], right[...])


ORDER = (
    "init0", "px", "q0", "h1", "q1", "p0", "init1", "h2", "h3", "ln1", "hb", "q2", "q3",
    "p1", "p2", "e0", "ar", "d0", "f0", "af", "qkv", "p3", "att", "f1", "sr", "dr", "f2",
    "e1", "ln2", "f3", "e2", "e3", "mr", "mf", "fc1", "df", "w2", "ef", "dh", "fc2", "dm",
    "E30", "tr", "w1", "E20", "E21", "E10", "ln2b", "ur", "F30", "E31", "gr", "F31", "F20",
    "gf", "attb", "F10", "wp", "E32", "P30", "dam", "P20", "F21", "wq", "xr", "EJ", "P31",
    "res", "P21", "F32", "P32", "v1", "Q30", "Q20", "P10", "Q31", "Q10", "ln1b", "Q21", "FJ",
    "Q32", "t1", "QJ", "FG", "v2", "PJ", "PK", "v3", "EG", "QG", "t2", "t3", "PG", "end",
)


def fast_device(
    tokens,
    cond,
    timesteps,
    counts,
    w_ada,
    b_ada,
    w_qkv,
    b_qv,
    w_proj,
    b_proj,
    w_fc1,
    b_fc1,
    w_fc2,
    b_fc2,
    cotangent,
):
    slots, half_len, width = tokens.shape
    n_wide = lax.axis_size("wide")
    w, y = lax.axis_index("wide"), lax.axis_index("narrow")
    shard = w_ada.shape[0]
    mlp = w_fc1.shape[1]
    hq = HEADS // 4
    nq = 3 * hq * HEAD_DIM
    rows = slots * half_len
    mq = mlp // 4
    half = w_ada.shape[1] // 2

    cond_vec = cond.astype(F32) + time_features(timesteps, width)
    cond_sig = jax.nn.sigmoid(cond_vec)
    silu = (cond_vec * cond_sig).astype(BF16).astype(F32)
    chunks = jnp.pad(
        silu.reshape(slots, n_wide, shard).transpose(1, 0, 2), ((0, 0), (0, 0), (0, 640 - shard))
    )

    def tile(piece):
        return jnp.pad(piece.astype(F32), ((0, 0), (0, 128 - piece.shape[1])))

    fc1_pieces = lax.dynamic_slice_in_dim(b_fc1.reshape(4, shard), 2 * y, 2, 0)
    vector = jnp.concatenate(
        [
            tile(fc1_pieces),
            tile(jnp.broadcast_to(b_proj, (2, shard))),
            tile(jnp.broadcast_to(b_fc2, (2, shard))),
            tile(b_qv.reshape(2, shard)),
            jnp.zeros((2, 128), F32),
        ],
        axis=1,
    )
    vector = jnp.broadcast_to(vector[None], (n_wide // 2, 2, 640)).reshape(n_wide, 1, 640)
    parcel = jnp.concatenate([chunks, vector, jnp.zeros_like(vector)], axis=1)
    ada_cut = b_ada.shape[0]
    ada_bias = lax.dynamic_update_slice_in_dim(
        jnp.zeros((1, w_ada.shape[1]), F32), b_ada.astype(F32)[None], w * ada_cut, 1
    )
    live = (jnp.arange(slots, dtype=jnp.int32) < counts[0])[:, None, None]
    cot_live = jnp.where(live, cotangent, jnp.zeros_like(cotangent))

    def v16(*shape):
        return pltpu.VMEM(shape, BF16)

    def v32(*shape):
        return pltpu.VMEM(shape, F32)

    two = 2 * shard
    full = (4, 2, half_len, width)
    own = (slots, half_len, width)
    scratch = [
        v16(width, nq), v16(hq, shard, width), v16(width, mq), v16(mq, width), v16(mq, width),
        v16(shard, nq), v16(shard, mq), v16(shard, width),
        v16(shard, nq), v16(shard, mq), v16(shard, width), v16(shard, nq), v16(shard, mq),
        v16(4, two, nq), v16(1, shard, width), v16(4, two, mq), v16(4, two, width),
        v16(5, two, nq), v16(5, shard, width), v16(5, two, mq), v16(5, two, width),
        v16(2, shard, nq), v16(2, shard, mq), v16(2, shard, width), v16(shard, width),
        v16(4, shard, nq), v16(4, shard, mq),
        v16(*full), v16(*full), v16(*full),
        v16(4, rows, nq), v16(hq, 4, rows, HEAD_DIM), v16(*full), v16(4, rows, mq),
        v16(*full), v16(*full),
        v16(2, 2, half_len, width), v16(2, 2, half_len, width),
        v16(*own), v16(*own), v16(*own), v16(*own),
        v32(*own), v32(*own), v32(*own),
        v32(n_wide * slots, 128), v32(n_wide, slots, half), v32(n_wide, slots, half),
        v32(slots, half), v32(2, slots, half), v32(6, slots, width), v32(1, nq), v32(4, width),
        v32(4, width),
        v32(6, slots, width), v32(6, slots, width), v16(slots, 6 * width),
        v16(n_wide, slots, 6 * width), v32(n_wide, 8, 128), v32(n_wide, 8, 128),
        v32(n_wide * slots, width), v32(n_wide, slots, 128),
        pltpu.SemaphoreType.DMA((300,)),
        pltpu.SemaphoreType.DMA((300,)),
        pltpu.SemaphoreType.DMA((5,)),
    ]
    out, gtok, got, dm_all, v_out, d_silu, p_qkv, p_fc1, j_fc2, j_proj = pl.pallas_call(
        functools.partial(block_kernel, ORDER, n_wide),
        out_shape=(
            jax.ShapeDtypeStruct(own, BF16),
            jax.ShapeDtypeStruct(own, F32),
            jax.ShapeDtypeStruct((n_wide, 4, 640), F32),
            jax.ShapeDtypeStruct((n_wide * slots, 6 * width), BF16),
            jax.ShapeDtypeStruct((2, 8, 128), F32),
            jax.ShapeDtypeStruct((n_wide, slots, 128), F32),
            jax.ShapeDtypeStruct(w_qkv.shape, BF16),
            jax.ShapeDtypeStruct(w_fc1.shape, BF16),
            jax.ShapeDtypeStruct((4, shard, width), BF16),
            jax.ShapeDtypeStruct((shard, width), BF16),
        ),
        in_specs=[VMEM_SPEC] * 7 + [HBM_SPEC] * 2,
        out_specs=(VMEM_SPEC,) * 8 + (HBM_SPEC, VMEM_SPEC),
        scratch_shapes=scratch,
        compiler_params=pltpu.CompilerParams(
            collective_id=0, has_side_effects=True, vmem_limit_bytes=VMEM_LIMIT
        ),
    )(
        tokens, cot_live, parcel, w_ada, ada_bias, w_qkv, w_fc1,
        w_fc2.reshape(4, shard, width), w_proj,
    )
    out = jnp.where(live, out, jnp.zeros_like(out))
    silu_cols = got[:, 0:2, :shard].reshape(n_wide * slots, shard).astype(BF16)
    passed = (gtok, p_qkv, j_proj, p_fc1, j_fc2.reshape(w_fc2.shape))
    parts = 3

    def cut(value):
        dims = value.shape[:-1]
        return pl.BlockSpec(
            (*dims, value.shape[-1] // parts), lambda i: (0,) * len(dims) + (i,)
        )

    given = [jax.ShapeDtypeStruct(value.shape, F32) for value in passed]
    product = jax.ShapeDtypeStruct(w_ada.shape, F32)
    gtok, grad_qkv, grad_proj, grad_fc1, grad_fc2, grad_ada = pl.pallas_call(
        finish_kernel,
        grid=(parts,),
        out_shape=given + [product],
        in_specs=[cut(value) for value in passed]
        + [pl.BlockSpec(silu_cols.shape, lambda i: (0, 0)), cut(dm_all)],
        out_specs=[cut(value) for value in given] + [cut(product)],
        compiler_params=pltpu.CompilerParams(vmem_limit_bytes=VMEM_LIMIT),
    )(*passed, silu_cols, dm_all)
    grad_b_ada = jnp.sum(
        lax.dynamic_slice_in_dim(dm_all, w * ada_cut, ada_cut, 1).astype(F32), axis=0
    )
    d_silu = d_silu[:, :, :shard].transpose(1, 0, 2).reshape(slots, width)
    grad_cond = d_silu * (cond_sig + cond_vec * cond_sig * (1.0 - cond_sig))
    v_sum = (v_out[0] + v_out[1])[:, :shard]
    return (
        out,
        gtok,
        grad_cond,
        grad_ada,
        grad_b_ada,
        grad_qkv,
        v_sum[4:6].reshape(-1),
        grad_proj,
        v_sum[2],
        grad_fc1,
        v_out[:, 0:2, :shard].reshape(-1),
        grad_fc2,
        v_sum[3],
    )


def solution(mesh):
    in_specs = (
        P("wide", "narrow", None),
        P("wide", None),
        P("wide"),
        P("wide"),
        P("wide", None),
        P("wide"),
        P("wide", None),
        P("wide"),
        P("wide", None),
        P("wide"),
        P("wide", None),
        P("wide"),
        P("wide", None),
        P("wide"),
        P("wide", "narrow", None),
    )
    out_specs = (
        P("wide", "narrow", None),
        P("wide", "narrow", None),
        P("wide", None),
        P("wide", None),
        P("wide"),
        P("wide", None),
        P("wide"),
        P("wide", None),
        P("wide"),
        P("wide", None),
        P("wide"),
        P("wide", None),
        P("wide"),
    )
    small = mesh.shape["wide"] == 16 and mesh.shape["narrow"] == 2
    per_device = fast_device if small else on_device
    return jax.shard_map(
        per_device, mesh=mesh, in_specs=in_specs, out_specs=out_specs, check_vma=False
    )
```
